256 devices in a mesh: sta: 64 (over z, x_lo, y), freq: 4 (over x_hi, core).
Axes of the slice: x: 4 (x_hi: 2, x_lo: 2; x = x_hi * 2 + x_lo), y: 4, z: 8, core: 2. Of those that a mesh axis runs over, the one named last changes fastest.
Arguments:
- spectra: bfloat16 [4, 2, 4096], P('freq', None, 'sta'), may hold values from -6 to 6
- green: bfloat16 [4, 2, 4096, 1024], P('freq', None, 'sta'), may hold values from -1.0546875 to 1.0546875
- source: float32 [4, 1024], P('freq'), may hold values from 0.25 to 4
- pair_mask: int32 [4096, 4096], P('sta'), may hold values 0 or 1
Outputs:
- new_source: float32 [4, 1024], P('freq')
- misfit: float32 [4], P('freq')
The draws below stay inside these ranges and needn't reach their ends.
All inputs are finite; a program needn't handle non-finite values. No bound on the sum of `pair_mask` on one device may be relied on, other than what follows from the above.
Results may differ from the reference program's by a relative error of at most 0.0003.
Values may be sent and summed in bfloat16 or wider, within the bound.
No kernel may reach another device: no remote copies, remote signals or barrier semaphores. Data moves between devices by JAX's collectives and lax.ppermute only.
A program may use at most 64 MiB of HBM per device.

```python
import math
import jax
import jax.numpy as jnp
from jax import lax

S_DEV = 64
CELLS = 1024
STATIONS = 4096
FREQS = 4


def plant(result, rng, smallest, high):
    place = [jax.random.randint(jax.random.fold_in(rng, axis), (), 0, length) for axis, length in enumerate(result.shape)]
    main_axis = result.shape.index(max(result.shape))
    beside = place[:main_axis] + [(place[main_axis] + 1) % result.shape[main_axis]] + place[main_axis + 1:]
    return result.at[tuple(place)].set(smallest).at[tuple(beside)].set(high)


def block_scale(own_key, dims, split, least, top_value):
    loudness, own = 1.0, jax.random.fold_in(own_key, 6)
    for axis_at, blocks in split:
        draws = jnp.exp(jax.random.uniform(jax.random.fold_in(own, axis_at), (blocks,), jnp.float32, least / len(split), top_value / len(split)))
        loudness = loudness * jnp.repeat(draws, dims[axis_at] // blocks).reshape([-1 if axis == axis_at else 1 for axis in range(len(dims))])
    return loudness


def gaussian(own_key, dims, scale, limit, pieces=(), held_as=jnp.bfloat16):
    entries = jax.random.normal(own_key, dims, jnp.float32) * scale
    if len(pieces) > 0:
        entries = block_scale(own_key, dims, pieces, -0.22, 0.18) * entries
    return jnp.clip(entries, min=-limit, max=limit).astype(held_as)


def setup_inputs(seed: int = 0) -> dict:
    splits = jax.random.split(jax.random.key(seed), 5)
    spectra = gaussian(splits[0], (FREQS, 2, STATIONS), 1.0, 6.0, ((0, 4), (2, 64)))
    green = gaussian(splits[1], (FREQS, 2, STATIONS, CELLS), (CELLS ** -0.25), 1.0546875, ((0, 4), (2, 64)))
    source = jnp.clip(jnp.exp(math.log(4.0) - 2.7725887 * jax.random.uniform(splits[2], (FREQS, CELLS), jnp.float32) ** block_scale(splits[2], (FREQS, CELLS), ((0, 4),), -0.2, 0.2)), 0.25, 4.0)
    pair_mask = plant((jax.random.randint(splits[3], (STATIONS, STATIONS), 0, 2) < 1).astype(jnp.int32), jax.random.fold_in(splits[3], 1), 0, 1)
    return {"spectra": spectra, "green": green, "source": source, "pair_mask": pair_mask}


def contract(a, b):
    return jnp.einsum('fix,fjx->fij', a, b)

def spread(a, b):
    return jnp.einsum('fij,fjx->fix', a, b)

def reference(spectra, green, source, pair_mask):
    weighted = (source[:, None, None, :] * green.astype(jnp.float32)).astype(jnp.bfloat16)
    weight_full = weighted.astype(jnp.float32)
    green_full = green.astype(jnp.float32)
    spec_full = spectra.astype(jnp.float32)

    def row_block(block):
        start = (block * S_DEV).astype(jnp.int32)
        w_rows = lax.dynamic_slice_in_dim(weight_full, start, S_DEV, 2)
        g_rows = lax.dynamic_slice_in_dim(green_full, start, S_DEV, 2)
        u_rows = lax.dynamic_slice_in_dim(spec_full, start, S_DEV, 2)
        m_rows = lax.dynamic_slice_in_dim(pair_mask, start, S_DEV, 0).astype(jnp.float32)
        model_re = contract(w_rows[:, 0], green_full[:, 0]) + contract(w_rows[:, 1], green_full[:, 1])
        model_im = contract(w_rows[:, 1], green_full[:, 0]) - contract(w_rows[:, 0], green_full[:, 1])
        data_re = u_rows[:, 0, :, None] * spec_full[:, 0, None, :] + u_rows[:, 1, :, None] * spec_full[:, 1, None, :]
        data_im = u_rows[:, 1, :, None] * spec_full[:, 0, None, :] - u_rows[:, 0, :, None] * spec_full[:, 1, None, :]
        resid_re = m_rows[None] * (data_re - model_re)
        resid_im = m_rows[None] * (data_im - model_im)
        mis = 0.5 * lax.optimization_barrier(jnp.sum(resid_re * resid_re + resid_im * resid_im, axis=(1, 2)))
        round_re = lax.optimization_barrier(resid_re.astype(jnp.bfloat16)).astype(jnp.float32)
        round_im = lax.optimization_barrier(resid_im.astype(jnp.bfloat16)).astype(jnp.float32)
        acc_re = spread(round_re, green_full[:, 0]) - spread(round_im, green_full[:, 1])
        acc_im = spread(round_re, green_full[:, 1]) + spread(round_im, green_full[:, 0])
        part = -lax.optimization_barrier(jnp.sum(g_rows[:, 0] * acc_re + g_rows[:, 1] * acc_im, axis=1))
        return (part, mis)
    parts, misses = lax.map(row_block, jnp.arange(STATIONS // S_DEV, dtype=jnp.int32))
    grad = lax.optimization_barrier(jnp.sum(parts, axis=0))
    misfit = lax.optimization_barrier(jnp.sum(misses, axis=0)) / (STATIONS * STATIONS)
    rms = jnp.sqrt(jnp.sum(grad * grad) / (FREQS * CELLS) + 1e-06)
    new_source = source * jnp.exp(-0.5 * grad / rms)
    return (new_source, misfit)
```

```python
import jax
import jax.numpy as jnp
from jax import lax
from jax.experimental import pallas as pl
from jax.experimental.pallas import tpu as pltpu
from jax.sharding import PartitionSpec as P

NZ, NX, NY = 8, 2, 4
NQ = NX * NY
ROWS = 64
CELLS = 1024
WIDE = NQ * ROWS
BOTH = (1, 2, -3)
OFFSETS = (1, 2, -3, 4)


def z_shift(u):
    return [
        (z * NQ + q, ((z - u) % NZ) * NQ + q) for z in range(NZ) for q in range(NQ)
    ]


def q_minus(q, a):
    return ((q // NY) ^ (a // NY)) * NY + (q % NY - a % NY) % NY


def q_shift(a):
    return [(z * NQ + q, z * NQ + q_minus(q, a)) for z in range(NZ) for q in range(NQ)]


def nt(a, b):
    return lax.dot_general(
        a, b, (((1,), (1,)), ((), ())), preferred_element_type=jnp.float32
    )


def nn(a, b):
    return lax.dot_general(
        a, b, (((1,), (0,)), ((), ())), preferred_element_type=jnp.float32
    )


def pack(place, green, mask, spec_col, *outs):
    line = outs[: len(OFFSETS)]
    plane = outs[len(OFFSETS) : len(OFFSETS) + NQ - 1]
    own_mask, own_back = outs[-2:]
    z, q = place[0], place[1]
    x, y = q // NY, q % NY

    def window(at):
        start = pl.multiple_of(lax.rem(at + NZ, NZ) * WIDE, WIDE)
        return mask[:, pl.ds(start, WIDE)].astype(jnp.float32).astype(jnp.bfloat16)

    def other(col, sign):
        a = col // ROWS
        ax, ay = a // NY, a % NY
        return (
            ((x + ax) % NX * NY + (y + sign * ay + NY) % NY) * ROWS + col % ROWS
        )

    down = lax.broadcasted_iota(jnp.int32, (WIDE, WIDE), 0)
    across = lax.broadcasted_iota(jnp.int32, (WIDE, WIDE), 1)
    order = (down == other(across, 1)).astype(jnp.float32).astype(jnp.bfloat16)
    ahead = jnp.concatenate([window(z)] + [window(z - u) for u in OFFSETS], axis=0)
    ahead = nn(ahead, order).astype(jnp.bfloat16)
    order = (across == other(down, -1)).astype(jnp.float32).astype(jnp.bfloat16)
    col = lax.broadcasted_iota(jnp.int32, (ROWS, WIDE), 1) % ROWS
    spectra = jnp.where(
        col == 0, spec_col[:, 0:1], jnp.where(col == 1, spec_col[:, 1:2], 0.0)
    )
    back = jnp.concatenate(
        [window(z + u) for u in BOTH] + [spectra.astype(jnp.bfloat16)], axis=0
    )
    back = nt(order, back).astype(jnp.bfloat16)

    own_mask[...] = ahead[:ROWS]
    own_back[...] = back[:ROWS]
    lane = lax.broadcasted_iota(jnp.int32, (ROWS, 128), 1)
    column = jnp.where(
        lane == 0, spec_col[:, 0:1], jnp.where(lane == 1, spec_col[:, 1:2], 0.0)
    ).astype(jnp.bfloat16)
    for k, ref in enumerate(line):
        ref[0:64, :] = green[0]
        ref[64:128, :] = green[1]
        part = ahead[ROWS * (k + 1) : ROWS * (k + 2)]
        ref[128:160, 0:512] = part[0:32]
        ref[128:160, 512:1024] = part[32:64]
        for g in range(8):
            ref[160:168, 128 * g : 128 * (g + 1)] = column[8 * g : 8 * (g + 1)]
    for k, ref in enumerate(plane):
        ref[0:64, :] = green[0]
        ref[64:128, :] = green[1]
        part = back[ROWS * (k + 1) : ROWS * (k + 2)]
        for g in range(4):
            ref[128:144, 256 * g : 256 * (g + 1)] = part[16 * g : 16 * (g + 1)]


def absorb(source, green, spec_col, own_mask, own_back, *rest):
    line = rest[: len(OFFSETS)]
    plane = rest[len(OFFSETS) : len(OFFSETS) + NQ - 1]
    out, far_re, far_im, far_spec, back, near_re, near_im, wt_re, wt_im = rest[
        len(OFFSETS) + NQ - 1 :
    ]
    f32, bf16 = jnp.float32, jnp.bfloat16
    scale = source[...]
    for a in range(NQ):
        rows = slice(ROWS * a, ROWS * (a + 1))
        if a == 0:
            far_re[rows, :] = green[0]
            far_im[rows, :] = green[1]
            piece = own_back[...].astype(f32)
        else:
            ref = plane[a - 1]
            far_re[rows, :] = ref[0:64, :]
            far_im[rows, :] = ref[64:128, :]
            piece = jnp.concatenate(
                [ref[128:144, 256 * g : 256 * (g + 1)].astype(f32) for g in range(4)],
                axis=0,
            )
        for k in range(len(BOTH)):
            back[ROWS * k : ROWS * (k + 1), rows] = piece[:, ROWS * k : ROWS * (k + 1)]
        far_spec[0:2, rows] = piece[0:2, 3 * ROWS : 4 * ROWS]
    us, masks = [], []
    for k in range(1 + len(OFFSETS)):
        rows = slice(ROWS * k, ROWS * (k + 1))
        if k == 0:
            re, im = green[0], green[1]
            us.append(spec_col[...])
            masks.append(own_mask[...].astype(f32))
        else:
            ref = line[k - 1]
            re, im = ref[0:64, :], ref[64:128, :]
            us.append(
                jnp.concatenate(
                    [ref[160:168, 128 * g : 128 * (g + 1)].astype(f32) for g in range(8)],
                    axis=0,
                )
            )
            masks.append(
                jnp.concatenate(
                    [ref[128:160, 0:512], ref[128:160, 512:1024]], axis=0
                ).astype(f32)
            )
        near_re[rows, :] = re
        near_im[rows, :] = im
        wt_re[rows, :] = (scale * re.astype(f32)).astype(bf16)
        wt_im[rows, :] = (scale * im.astype(f32)).astype(bf16)
    for k in range(len(BOTH)):
        masks[k + 1] = masks[k + 1] + back[ROWS * k : ROWS * (k + 1), :]
    weight = jnp.concatenate(masks, axis=0)
    u_re = jnp.concatenate([u[:, 0:1] for u in us], axis=0)
    u_im = jnp.concatenate([u[:, 1:2] for u in us], axis=0)
    v_re, v_im = far_spec[0:1, :], far_spec[1:2, :]
    g_re, g_im = far_re[...], far_im[...]
    model_re = nt(wt_re[...], g_re) + nt(wt_im[...], g_im)
    model_im = nt(wt_im[...], g_re) - nt(wt_re[...], g_im)
    x_re = (u_re * v_re + u_im * v_im) - model_re
    x_im = (u_im * v_re - u_re * v_im) - model_im
    mis = 0.5 * jnp.sum(weight * (x_re * x_re + x_im * x_im), keepdims=True)
    r_re = (weight * x_re.astype(bf16).astype(f32)).astype(bf16)
    r_im = (weight * x_im.astype(bf16).astype(f32)).astype(bf16)
    y_re = nn(r_re, g_re) - nn(r_im, g_im)
    y_im = nn(r_re, g_im) + nn(r_im, g_re)
    total = jnp.sum(
        near_re[...].astype(f32) * y_re + near_im[...].astype(f32) * y_im,
        axis=0,
        keepdims=True,
    )
    out[0:1, 0:CELLS] = -total
    out[0:1, CELLS : CELLS + 128] = jnp.broadcast_to(mis, (1, 128))


def copy_for_each(array, axis):
    peers = lax.axis_size(axis)
    return lax.all_to_all(
        jnp.broadcast_to(array[None], (peers, *array.shape)), axis, 0, 0, tiled=True
    )


def taken_together(array, axis):
    return copy_for_each(array, axis).sum(axis=0)


def local(spectra, green, source, pair_mask):
    g = green[0]
    here = lax.axis_index("sta")
    place = jnp.stack([here // NQ, here % NQ]).astype(jnp.int32)
    spec_col = spectra[0].astype(jnp.float32).T
    vmem = pl.BlockSpec(memory_space=pltpu.VMEM)
    sent = pl.pallas_call(
        pack,
        out_shape=[jax.ShapeDtypeStruct((168, CELLS), jnp.bfloat16)] * len(OFFSETS)
        + [jax.ShapeDtypeStruct((144, CELLS), jnp.bfloat16)] * (NQ - 1)
        + [
            jax.ShapeDtypeStruct((ROWS, WIDE), jnp.bfloat16),
            jax.ShapeDtypeStruct((ROWS, 4 * ROWS), jnp.bfloat16),
        ],
        in_specs=[pl.BlockSpec(memory_space=pltpu.SMEM), vmem, vmem, vmem],
        out_specs=[vmem] * (len(OFFSETS) + NQ + 1),
        name="pack",
    )(place, g, pair_mask, spec_col)
    line = [
        lax.ppermute(s, "sta", z_shift(u)) for s, u in zip(sent[: len(OFFSETS)], OFFSETS)
    ]
    plane = [
        lax.ppermute(s, "sta", q_shift(a + 1))
        for a, s in enumerate(sent[len(OFFSETS) : len(OFFSETS) + NQ - 1])
    ]
    own_mask, own_back = sent[-2:]
    tall = ROWS * (1 + len(OFFSETS))
    part = pl.pallas_call(
        absorb,
        out_shape=jax.ShapeDtypeStruct((1, CELLS + 128), jnp.float32),
        in_specs=[vmem] * (5 + len(OFFSETS) + NQ - 1),
        out_specs=vmem,
        scratch_shapes=[
            pltpu.VMEM((WIDE, CELLS), jnp.bfloat16),
            pltpu.VMEM((WIDE, CELLS), jnp.bfloat16),
            pltpu.VMEM((8, WIDE), jnp.float32),
            pltpu.VMEM((ROWS * len(BOTH), WIDE), jnp.float32),
            pltpu.VMEM((tall, CELLS), jnp.bfloat16),
            pltpu.VMEM((tall, CELLS), jnp.bfloat16),
            pltpu.VMEM((tall, CELLS), jnp.bfloat16),
            pltpu.VMEM((tall, CELLS), jnp.bfloat16),
        ],
        name="absorb",
    )(source, g, spec_col, own_mask, own_back, *line, *plane)
    total = taken_together(part[0], "sta")
    grad, misfit = total[None, :CELLS], total[CELLS : CELLS + 1]
    total_entries = lax.axis_size("freq") * CELLS
    stations = NZ * NQ * ROWS
    squares = taken_together(jnp.sum(grad * grad), "freq")
    rms = jnp.sqrt(squares / total_entries + 1e-06)
    new_source = source * jnp.exp(-0.5 * grad / rms)
    return (new_source, misfit / (stations * stations))


def solution(mesh):
    placed = (P("freq", None, "sta"), P("freq", None, "sta", None), P("freq", None), P("sta", None))
    return jax.shard_map(
        local, mesh=mesh, in_specs=placed, out_specs=(P("freq", None), P("freq")), check_vma=False
    )
```

```python
import jax
import jax.numpy as jnp
from jax import lax
from jax.experimental import pallas as pl
from jax.experimental.pallas import tpu as pltpu
from jax.sharding import Mesh, PartitionSpec as P

NZ, NX, NY = 8, 2, 4
NQ = NX * NY
NF = 4
ROWS = 64
CELLS = 1024
WIDE = NQ * ROWS
PLANE = ("xl", "y")
FREQ = ("xh", "core")
STA = ("z",) + PLANE
BOTH = (1, 2, -3)
OFFSETS = (1, 2, -3, 4)
MASKED, PLAIN, SHARED = 168, 136, 152
LONG = CELLS + 128
f32, bf16 = jnp.float32, jnp.bfloat16


def nt(a, b):
    return lax.dot_general(
        a, b, (((1,), (1,)), ((), ())), preferred_element_type=f32
    )


def nn(a, b):
    return lax.dot_general(
        a, b, (((1,), (0,)), ((), ())), preferred_element_type=f32
    )


def identity(n):
    down = lax.broadcasted_iota(jnp.int32, (n, n), 0)
    across = lax.broadcasted_iota(jnp.int32, (n, n), 1)
    return (down == across).astype(f32).astype(bf16)


def pack(green, mask, spec_row, *outs):
    line = outs[: len(OFFSETS)]
    shared, own_mask, own_spec = outs[len(OFFSETS) :]
    z = lax.axis_index("z")

    def window(at):
        start = pl.multiple_of(lax.rem(at + NZ, NZ) * WIDE, WIDE)
        return mask[:, pl.ds(start, WIDE)].astype(f32)

    row = spec_row[...]
    col = nt(identity(ROWS), row)
    lane = lax.broadcasted_iota(jnp.int32, (ROWS, 128), 1)
    own_spec[...] = jnp.where(
        lane == 0, col[:, 0:1], jnp.where(lane == 1, col[:, 1:2], 0.0)
    )
    own_spec[0:2, 64:128] = row.astype(f32)
    spectra = own_spec[...].astype(bf16)

    def put(ref, at):
        for g in range(8):
            ref[at : at + 8, 128 * g : 128 * (g + 1)] = spectra[8 * g : 8 * (g + 1)]

    own_mask[...] = window(z).astype(bf16)
    for k, (u, ref) in enumerate(zip(OFFSETS, line)):
        ref[0:64, :] = green[0]
        ref[64:128, :] = green[1]
        if u in BOTH:
            part = window(z - u).astype(bf16)
            ref[128:160, 0:512] = part[0:32]
            ref[128:160, 512:1024] = part[32:64]
            put(ref, 160)
        else:
            put(ref, 128)
    wide = [window(z + u) for u in OFFSETS]
    for q in range(NQ):
        ref = shared.at[q]
        ref[0:64, :] = green[0]
        ref[64:128, :] = green[1]
        part = jnp.concatenate(
            [w[:, ROWS * q : ROWS * (q + 1)] for w in wide], axis=1
        ).astype(bf16)
        for g in range(4):
            ref[128:144, 256 * g : 256 * (g + 1)] = part[16 * g : 16 * (g + 1)]
        put(ref, 144)


def absorb(source, green, own_mask, own_spec, shared, *rest):
    line = rest[: len(OFFSETS)]
    out, far_re, far_im, far_spec, back, near_re, near_im, wt_re, wt_im = rest[
        len(OFFSETS) :
    ]
    scale = source[...]
    for q in range(NQ):
        rows = slice(ROWS * q, ROWS * (q + 1))
        ref = shared.at[q]
        far_re[rows, :] = ref[0:64, :]
        far_im[rows, :] = ref[64:128, :]
        for g in range(4):
            back[ROWS * q + 16 * g : ROWS * q + 16 * (g + 1), :] = ref[
                128:144, 256 * g : 256 * (g + 1)
            ]
        far_spec[0:2, rows] = ref[144:152, 0:128].astype(f32)[0:2, 64:128]
    behind = nt(identity(4 * ROWS), back[...])
    us, masks = [], []
    for k in range(1 + len(OFFSETS)):
        rows = slice(ROWS * k, ROWS * (k + 1))
        opposite = behind[ROWS * (k - 1) : ROWS * k] if k else None
        if k == 0:
            re, im = green[0], green[1]
            us.append(own_spec[...])
            masks.append(own_mask[...].astype(f32))
        else:
            ref = line[k - 1]
            re, im = ref[0:64, :], ref[64:128, :]
            at = 128
            if OFFSETS[k - 1] in BOTH:
                at = 160
                opposite = opposite + jnp.concatenate(
                    [ref[128:160, 0:512], ref[128:160, 512:1024]], axis=0
                ).astype(f32)
            us.append(
                jnp.concatenate(
                    [
                        ref[at : at + 8, 128 * g : 128 * (g + 1)].astype(f32)
                        for g in range(8)
                    ],
                    axis=0,
                )
            )
            masks.append(opposite)
        near_re[rows, :] = re
        near_im[rows, :] = im
        wt_re[rows, :] = (scale * re.astype(f32)).astype(bf16)
        wt_im[rows, :] = (scale * im.astype(f32)).astype(bf16)
    weight = jnp.concatenate(masks, axis=0)
    u_re = jnp.concatenate([u[:, 0:1] for u in us], axis=0)
    u_im = jnp.concatenate([u[:, 1:2] for u in us], axis=0)
    v_re, v_im = far_spec[0:1, :], far_spec[1:2, :]
    g_re, g_im = far_re[...], far_im[...]
    model_re = nt(wt_re[...], g_re) + nt(wt_im[...], g_im)
    model_im = nt(wt_im[...], g_re) - nt(wt_re[...], g_im)
    x_re = (u_re * v_re + u_im * v_im) - model_re
    x_im = (u_im * v_re - u_re * v_im) - model_im
    mis = 0.5 * jnp.sum(weight * (x_re * x_re + x_im * x_im), keepdims=True)
    r_re = (weight * x_re.astype(bf16).astype(f32)).astype(bf16)
    r_im = (weight * x_im.astype(bf16).astype(f32)).astype(bf16)
    y_re = nn(r_re, g_re) - nn(r_im, g_im)
    y_im = nn(r_re, g_im) + nn(r_im, g_re)
    total = jnp.sum(
        near_re[...].astype(f32) * y_re + near_im[...].astype(f32) * y_im,
        axis=0,
        keepdims=True,
    )
    out[:, 0:CELLS] = jnp.broadcast_to(-total, (NZ, CELLS))
    out[:, CELLS:LONG] = jnp.broadcast_to(mis, (NZ, 128))


def gather_z(parts, out):
    out[...] = jnp.broadcast_to(
        jnp.sum(parts[...], axis=0, keepdims=True), out.shape
    )


def finish(parts, source, new_source, misfit):
    mine = lax.axis_index("xh") * 2 + lax.axis_index("core")
    by_freq = jnp.sum(parts[...].reshape(NQ, NF, LONG), axis=0)
    grads = by_freq[:, 0:CELLS]
    rms = jnp.sqrt(jnp.sum(grads * grads, keepdims=True) / (NF * CELLS) + 1e-06)
    rows = lax.broadcasted_iota(jnp.int32, (NF, LONG), 0)
    own = jnp.sum(jnp.where(rows == mine, by_freq, 0.0), axis=0, keepdims=True)
    new_source[...] = source[...] * jnp.exp(-0.5 * own[:, 0:CELLS] / rms)
    stations = NZ * NQ * ROWS
    misfit[0] = jnp.max(own[:, CELLS:LONG]) / (stations * stations)


def local(spectra, green, source, pair_mask):
    g = green[0]
    vmem = pl.BlockSpec(memory_space=pltpu.VMEM)
    tall = ROWS * (1 + len(OFFSETS))
    *sent, shared, own_mask, own_spec = pl.pallas_call(
        pack,
        out_shape=[
            jax.ShapeDtypeStruct((MASKED if u in BOTH else PLAIN, CELLS), bf16)
            for u in OFFSETS
        ]
        + [
            jax.ShapeDtypeStruct((NQ, SHARED, CELLS), bf16),
            jax.ShapeDtypeStruct((ROWS, WIDE), bf16),
            jax.ShapeDtypeStruct((ROWS, 128), f32),
        ],
        in_specs=[vmem] * 3,
        out_specs=[vmem] * (len(OFFSETS) + 3),
        name="pack",
    )(g, pair_mask, spectra[0])
    line = [
        lax.ppermute(s, "z", [(z, (z - u) % NZ) for z in range(NZ)])
        for s, u in zip(sent, OFFSETS)
    ]
    shared = lax.all_to_all(shared, PLANE, 0, 0, tiled=True)
    part = pl.pallas_call(
        absorb,
        out_shape=jax.ShapeDtypeStruct((NZ, LONG), f32),
        in_specs=[vmem] * (5 + len(OFFSETS)),
        out_specs=vmem,
        scratch_shapes=[
            pltpu.VMEM((WIDE, CELLS), bf16),
            pltpu.VMEM((WIDE, CELLS), bf16),
            pltpu.VMEM((8, WIDE), f32),
            pltpu.VMEM((WIDE, 4 * ROWS), bf16),
            pltpu.VMEM((tall, CELLS), bf16),
            pltpu.VMEM((tall, CELLS), bf16),
            pltpu.VMEM((tall, CELLS), bf16),
            pltpu.VMEM((tall, CELLS), bf16),
        ],
        name="absorb",
    )(source, g, own_mask, own_spec, shared, *line)
    part = lax.all_to_all(part, "z", 0, 0, tiled=True)
    part = pl.pallas_call(
        gather_z,
        out_shape=jax.ShapeDtypeStruct((NQ * NF, LONG), f32),
        in_specs=[vmem],
        out_specs=vmem,
        name="gather_z",
    )(part)
    part = lax.all_to_all(part, PLANE + FREQ, 0, 0, tiled=True)
    return pl.pallas_call(
        finish,
        out_shape=(
            jax.ShapeDtypeStruct((1, CELLS), f32),
            jax.ShapeDtypeStruct((1,), f32),
        ),
        in_specs=[vmem, vmem],
        out_specs=(vmem, pl.BlockSpec(memory_space=pltpu.SMEM)),
        name="finish",
    )(part, source)


def solution(mesh):
    fine = Mesh(mesh.devices.reshape(NZ, NX, NY, 2, 2), STA + FREQ)
    placed = (P(FREQ, None, STA), P(FREQ, None, STA, None), P(FREQ, None), P(STA, None))
    return jax.shard_map(
        local, mesh=fine, in_specs=placed, out_specs=(P(FREQ, None), P(FREQ)), check_vma=False
    )
```

```python
import jax
import jax.numpy as jnp
from jax import lax
from jax.experimental import pallas as pl
from jax.experimental.pallas import tpu as pltpu
from jax.sharding import Mesh, PartitionSpec as P

NZ, NX, NY = 8, 2, 4
NQ = NX * NY
NF = 4
ROWS = 64
CELLS = 1024
WIDE = NQ * ROWS
PLANE = ("xl", "y")
FREQ = ("xh", "core")
STA = ("z",) + PLANE
OFFSETS = (1, 2, -3, 4)
SHARED = 152
TILES = CELLS // 128
f32, bf16 = jnp.float32, jnp.bfloat16


def nt(a, b):
    return lax.dot_general(
        a, b, (((1,), (1,)), ((), ())), preferred_element_type=f32
    )


def nn(a, b):
    return lax.dot_general(
        a, b, (((1,), (0,)), ((), ())), preferred_element_type=f32
    )


def identity(n):
    down = lax.broadcasted_iota(jnp.int32, (n, n), 0)
    across = lax.broadcasted_iota(jnp.int32, (n, n), 1)
    return (down == across).astype(f32).astype(bf16)


SPEC, IMAG, REAL, MASK, MASKED = 0, 8, 72, 136, 168


def window(mask, at):
    start = pl.multiple_of(lax.rem(at + NZ, NZ) * WIDE, WIDE)
    return mask[:, pl.ds(start, WIDE)].astype(f32)


def put_mask(ref, at, part):
    ref[at : at + 32, 0:512] = part[0:32]
    ref[at : at + 32, 512:1024] = part[32:64]


def take_mask(ref, at):
    return jnp.concatenate(
        [ref[at : at + 32, 0:512], ref[at : at + 32, 512:1024]], axis=0
    ).astype(f32)


def put_spectra(ref, at, spectra):
    for g in range(8):
        ref[at : at + 8, 128 * g : 128 * (g + 1)] = spectra[8 * g : 8 * (g + 1)]


def take_spectra(ref, at):
    return jnp.concatenate(
        [ref[at : at + 8, 128 * g : 128 * (g + 1)].astype(f32) for g in range(8)],
        axis=0,
    )


def pack_line(green, mask, spec_row, near, far, two, own_mask, own_spec):
    z = lax.axis_index("z")
    row = spec_row[...]
    col = nt(identity(ROWS), row)
    lane = lax.broadcasted_iota(jnp.int32, (ROWS, 128), 1)
    own_spec[...] = jnp.where(
        lane == 0, col[:, 0:1], jnp.where(lane == 1, col[:, 1:2], 0.0)
    )
    own_spec[0:2, 64:128] = row.astype(f32)
    spectra = own_spec[...].astype(bf16)
    for ref, u in ((near, 1), (far, -3)):
        put_spectra(ref, SPEC, spectra)
        ref[IMAG : IMAG + ROWS, :] = green[1]
        ref[REAL : REAL + ROWS, :] = green[0]
        put_mask(ref, MASK, window(mask, z - u).astype(bf16))
    put_mask(two, 0, window(mask, z - 2).astype(bf16))
    own_mask[...] = window(mask, z).astype(bf16)


def pack_plane(green, mask, own_spec, shared):
    z = lax.axis_index("z")
    spectra = own_spec[...].astype(bf16)
    wide = [window(mask, z + u) for u in OFFSETS]
    for q in range(NQ):
        ref = shared.at[q]
        ref[0:64, :] = green[0]
        ref[64:128, :] = green[1]
        part = jnp.concatenate(
            [w[:, ROWS * q : ROWS * (q + 1)] for w in wide], axis=1
        ).astype(bf16)
        for g in range(4):
            ref[128:144, 256 * g : 256 * (g + 1)] = part[16 * g : 16 * (g + 1)]
        put_spectra(ref, 144, spectra)


def absorb(
    source, green, own_mask, own_spec, shared, one, two, two_mask, three, four_re, four_im,
    out, far_re, far_im, far_spec, back, near_re, near_im, wt_re, wt_im
):
    scale = source[...]
    for q in range(NQ):
        rows = slice(ROWS * q, ROWS * (q + 1))
        ref = shared.at[q]
        far_re[rows, :] = ref[0:64, :]
        far_im[rows, :] = ref[64:128, :]
        for g in range(4):
            back[ROWS * q + 16 * g : ROWS * q + 16 * (g + 1), :] = ref[
                128:144, 256 * g : 256 * (g + 1)
            ]
        far_spec[0:2, rows] = ref[144:152, 0:128].astype(f32)[0:2, 64:128]
    behind = nt(identity(4 * ROWS), back[...])
    us = [
        own_spec[...],
        take_spectra(one, SPEC),
        take_spectra(two, SPEC),
        take_spectra(three, SPEC),
        take_spectra(four_im, SPEC),
    ]
    weight = jnp.concatenate(
        [
            own_mask[...].astype(f32),
            take_mask(one, MASK) + behind[0:ROWS],
            take_mask(two_mask, 0) + behind[ROWS : 2 * ROWS],
            take_mask(three, MASK) + behind[2 * ROWS : 3 * ROWS],
            behind[3 * ROWS : 4 * ROWS],
        ],
        axis=0,
    )
    real, imag = slice(REAL, REAL + ROWS), slice(IMAG, IMAG + ROWS)
    held = [
        (green[0], green[1]),
        (one[real, :], one[imag, :]),
        (two[real, :], two[imag, :]),
        (three[real, :], three[imag, :]),
        (four_re[...], four_im[imag, :]),
    ]
    for k, (re, im) in enumerate(held):
        rows = slice(ROWS * k, ROWS * (k + 1))
        near_re[rows, :] = re
        near_im[rows, :] = im
        wt_re[rows, :] = (scale * re.astype(f32)).astype(bf16)
        wt_im[rows, :] = (scale * im.astype(f32)).astype(bf16)
    u_re = jnp.concatenate([u[:, 0:1] for u in us], axis=0)
    u_im = jnp.concatenate([u[:, 1:2] for u in us], axis=0)
    v_re, v_im = far_spec[0:1, :], far_spec[1:2, :]
    g_re, g_im = far_re[...], far_im[...]
    model_re = nt(wt_re[...], g_re) + nt(wt_im[...], g_im)
    model_im = nt(wt_im[...], g_re) - nt(wt_re[...], g_im)
    x_re = (u_re * v_re + u_im * v_im) - model_re
    x_im = (u_im * v_re - u_re * v_im) - model_im
    mis = 0.5 * jnp.sum(weight * (x_re * x_re + x_im * x_im), keepdims=True)
    r_re = (weight * x_re.astype(bf16).astype(f32)).astype(bf16)
    r_im = (weight * x_im.astype(bf16).astype(f32)).astype(bf16)
    y_re = nn(r_re, g_re) - nn(r_im, g_im)
    y_im = nn(r_re, g_im) + nn(r_im, g_re)
    total = -jnp.sum(
        near_re[...].astype(f32) * y_re + near_im[...].astype(f32) * y_im,
        axis=0,
        keepdims=True,
    )
    tiles = jnp.concatenate(
        [total[:, 128 * i : 128 * (i + 1)] for i in range(TILES)], axis=0
    )
    out[:, 0:TILES] = jnp.broadcast_to(tiles[None], (NZ, TILES, 128))
    out[:, TILES : 2 * TILES] = jnp.broadcast_to(mis[None], (NZ, TILES, 128))


def gather_z(parts, out):
    out[...] = jnp.broadcast_to(
        jnp.sum(parts[...], axis=0, keepdims=True), out.shape
    )


def finish(parts, source, new_source, misfit):
    mine = lax.axis_index("xh") * 2 + lax.axis_index("core")
    squares = jnp.zeros((TILES, 128), f32)
    own = jnp.zeros((2 * TILES, 128), f32)
    for f in range(NF):
        here = jnp.sum(
            jnp.concatenate([parts[q * NF + f][None] for q in range(NQ)], axis=0), axis=0
        )
        squares = squares + here[0:TILES] * here[0:TILES]
        own = jnp.where(mine == f, here, own)
    rms = jnp.sqrt(jnp.sum(squares, keepdims=True) / (NF * CELLS) + 1e-06)
    step = jnp.exp(-0.5 * own[0:TILES] / rms)
    step = jnp.concatenate([step[i : i + 1] for i in range(TILES)], axis=1)
    new_source[...] = source[...] * step
    stations = NZ * NQ * ROWS
    misfit[0] = jnp.max(own[TILES : TILES + 1]) / (stations * stations)


def shape(dtype, *dims):
    return jax.ShapeDtypeStruct(dims, dtype)


def from_z(array, u):
    return lax.ppermute(array, "z", [(z, (z - u) % NZ) for z in range(NZ)])


def local(spectra, green, source, pair_mask):
    g = green[0]
    vmem = pl.BlockSpec(memory_space=pltpu.VMEM)
    tall = ROWS * (1 + len(OFFSETS))
    near, far, two_mask, own_mask, own_spec = pl.pallas_call(
        pack_line,
        out_shape=[
            shape(bf16, MASKED, CELLS),
            shape(bf16, MASKED, CELLS),
            shape(bf16, 32, CELLS),
            shape(bf16, ROWS, WIDE),
            shape(f32, ROWS, 128),
        ],
        in_specs=[vmem] * 3,
        out_specs=[vmem] * 5,
        name="pack_line",
    )(g, pair_mask, spectra[0])
    two_mask = from_z(two_mask, 2)
    one = from_z(near, 1)
    three = from_z(far, -3)
    shared = pl.pallas_call(
        pack_plane,
        out_shape=shape(bf16, NQ, SHARED, CELLS),
        in_specs=[vmem] * 3,
        out_specs=vmem,
        name="pack_plane",
    )(g, pair_mask, own_spec)
    shared = lax.all_to_all(shared, PLANE, 0, 0, tiled=True)
    two = from_z(one[:MASK], 1)
    four_re = from_z(two[REAL:MASK], 2)
    four_im = from_z(three[:REAL], -1)
    part = pl.pallas_call(
        absorb,
        out_shape=shape(f32, NZ, 2 * TILES, 128),
        in_specs=[vmem] * 11,
        out_specs=vmem,
        scratch_shapes=[
            pltpu.VMEM((WIDE, CELLS), bf16),
            pltpu.VMEM((WIDE, CELLS), bf16),
            pltpu.VMEM((8, WIDE), f32),
            pltpu.VMEM((WIDE, 4 * ROWS), bf16),
            pltpu.VMEM((tall, CELLS), bf16),
            pltpu.VMEM((tall, CELLS), bf16),
            pltpu.VMEM((tall, CELLS), bf16),
            pltpu.VMEM((tall, CELLS), bf16),
        ],
        name="absorb",
    )(source, g, own_mask, own_spec, shared, one, two, two_mask, three, four_re, four_im)
    part = lax.all_to_all(part, "z", 0, 0, tiled=True)
    part = pl.pallas_call(
        gather_z,
        out_shape=shape(f32, NQ * NF, 2 * TILES, 128),
        in_specs=[vmem],
        out_specs=vmem,
        name="gather_z",
    )(part)
    part = lax.all_to_all(part, PLANE + FREQ, 0, 0, tiled=True)
    return pl.pallas_call(
        finish,
        out_shape=(shape(f32, 1, CELLS), shape(f32, 1)),
        in_specs=[vmem, vmem],
        out_specs=(vmem, pl.BlockSpec(memory_space=pltpu.SMEM)),
        name="finish",
    )(part, source)


def solution(mesh):
    fine = Mesh(mesh.devices.reshape(NZ, NX, NY, 2, 2), STA + FREQ)
    placed = (P(FREQ, None, STA), P(FREQ, None, STA, None), P(FREQ, None), P(STA, None))
    return jax.shard_map(
        local, mesh=fine, in_specs=placed, out_specs=(P(FREQ, None), P(FREQ)), check_vma=False
    )
```

```python
import jax
import jax.numpy as jnp
from jax import lax
from jax.experimental import pallas as pl
from jax.experimental.pallas import tpu as pltpu
from jax.sharding import Mesh, PartitionSpec as P

NZ, NX, NY = 8, 2, 4
NQ = NX * NY
NF = 4
ROWS = 64
CELLS = 1024
WIDE = NQ * ROWS
PLANE = ("xl", "y")
FREQ = ("xh", "core")
STA = ("z",) + PLANE
OFFSETS = (1, 2, -3, 4)
SHARED = 152
LONG = CELLS + 128
f32, bf16 = jnp.float32, jnp.bfloat16


def nt(a, b):
    return lax.dot_general(
        a, b, (((1,), (1,)), ((), ())), preferred_element_type=f32
    )


def nn(a, b):
    return lax.dot_general(
        a, b, (((1,), (0,)), ((), ())), preferred_element_type=f32
    )


def identity(n):
    down = lax.broadcasted_iota(jnp.int32, (n, n), 0)
    across = lax.broadcasted_iota(jnp.int32, (n, n), 1)
    return (down == across).astype(f32).astype(bf16)


SPEC, IMAG, REAL, MASK, MASKED = 0, 8, 72, 136, 168
PREPARE = 14_500_000_000


def window(mask, at):
    start = pl.multiple_of(lax.rem(at + NZ, NZ) * WIDE, WIDE)
    return mask[:, pl.ds(start, WIDE)].astype(f32)


def put_mask(ref, at, part):
    ref[at : at + 32, 0:512] = part[0:32]
    ref[at : at + 32, 512:1024] = part[32:64]


def take_mask(ref, at):
    return jnp.concatenate(
        [ref[at : at + 32, 0:512], ref[at : at + 32, 512:1024]], axis=0
    ).astype(f32)


def put_spectra(ref, at, spectra):
    for g in range(8):
        ref[at : at + 8, 128 * g : 128 * (g + 1)] = spectra[8 * g : 8 * (g + 1)]


def take_spectra(ref, at):
    return jnp.concatenate(
        [ref[at : at + 8, 128 * g : 128 * (g + 1)].astype(f32) for g in range(8)],
        axis=0,
    )


def pack_line(green, mask, spec_row, near, far, two, own_mask, own_spec):
    z = lax.axis_index("z")
    row = spec_row[...]
    col = nt(identity(ROWS), row)
    lane = lax.broadcasted_iota(jnp.int32, (ROWS, 128), 1)
    own_spec[...] = jnp.where(
        lane == 0, col[:, 0:1], jnp.where(lane == 1, col[:, 1:2], 0.0)
    )
    own_spec[0:2, 64:128] = row.astype(f32)
    spectra = own_spec[...].astype(bf16)
    for ref, u in ((near, 1), (far, -3)):
        put_spectra(ref, SPEC, spectra)
        ref[IMAG : IMAG + ROWS, :] = green[1]
        ref[REAL : REAL + ROWS, :] = green[0]
        put_mask(ref, MASK, window(mask, z - u).astype(bf16))
    put_mask(two, 0, window(mask, z - 2).astype(bf16))
    own_mask[...] = window(mask, z).astype(bf16)


def pack_plane(green, mask, own_spec, shared):
    z = lax.axis_index("z")
    spectra = own_spec[...].astype(bf16)
    wide = [window(mask, z + u) for u in OFFSETS]
    for q in range(NQ):
        ref = shared.at[q]
        ref[0:64, :] = green[0]
        ref[64:128, :] = green[1]
        part = jnp.concatenate(
            [w[:, ROWS * q : ROWS * (q + 1)] for w in wide], axis=1
        ).astype(bf16)
        for g in range(4):
            ref[128:144, 256 * g : 256 * (g + 1)] = part[16 * g : 16 * (g + 1)]
        put_spectra(ref, 144, spectra)


def prepare(
    source, green, own_mask, own_spec, one, two, two_mask, three, four,
    near_re, near_im, wt_re, wt_im, weight, spec_re, spec_im
):
    scale = source[...]
    real, imag = slice(REAL, REAL + ROWS), slice(IMAG, IMAG + ROWS)
    us = [own_spec[...]]
    held = [(green[0], green[1])]
    for ref in (one, two, three, four):
        us.append(take_spectra(ref, SPEC))
        held.append((ref[real, :], ref[imag, :]))
    masks = [
        own_mask[...].astype(f32),
        take_mask(one, MASK),
        take_mask(two_mask, 0),
        take_mask(three, MASK),
        jnp.zeros((ROWS, WIDE), f32),
    ]
    for k, (re, im) in enumerate(held):
        rows = slice(ROWS * k, ROWS * (k + 1))
        near_re[rows, :] = re
        near_im[rows, :] = im
        wt_re[rows, :] = (scale * re.astype(f32)).astype(bf16)
        wt_im[rows, :] = (scale * im.astype(f32)).astype(bf16)
        weight[rows, :] = masks[k]
        spec_re[rows, :] = jnp.broadcast_to(us[k][:, 0:1], (ROWS, 128))
        spec_im[rows, :] = jnp.broadcast_to(us[k][:, 1:2], (ROWS, 128))


def absorb(
    shared, near_re, near_im, wt_re, wt_im, weight, spec_re, spec_im,
    out, far_re, far_im, far_spec, back
):
    for q in range(NQ):
        rows = slice(ROWS * q, ROWS * (q + 1))
        ref = shared.at[q]
        far_re[rows, :] = ref[0:64, :]
        far_im[rows, :] = ref[64:128, :]
        for g in range(4):
            back[ROWS * q + 16 * g : ROWS * q + 16 * (g + 1), :] = ref[
                128:144, 256 * g : 256 * (g + 1)
            ]
        far_spec[0:2, rows] = ref[144:152, 0:128].astype(f32)[0:2, 64:128]
    behind = nt(identity(4 * ROWS), back[...])
    counts = weight[...] + jnp.concatenate(
        [jnp.zeros((ROWS, WIDE), f32), behind], axis=0
    )
    u_re, u_im = spec_re[:, 0:1], spec_im[:, 0:1]
    v_re, v_im = far_spec[0:1, :], far_spec[1:2, :]
    g_re, g_im = far_re[...], far_im[...]
    model_re = nt(wt_re[...], g_re) + nt(wt_im[...], g_im)
    model_im = nt(wt_im[...], g_re) - nt(wt_re[...], g_im)
    x_re = (u_re * v_re + u_im * v_im) - model_re
    x_im = (u_im * v_re - u_re * v_im) - model_im
    mis = 0.5 * jnp.sum(counts * (x_re * x_re + x_im * x_im), keepdims=True)
    r_re = (counts * x_re.astype(bf16).astype(f32)).astype(bf16)
    r_im = (counts * x_im.astype(bf16).astype(f32)).astype(bf16)
    y_re = nn(r_re, g_re) - nn(r_im, g_im)
    y_im = nn(r_re, g_im) + nn(r_im, g_re)
    total = -jnp.sum(
        near_re[...].astype(f32) * y_re + near_im[...].astype(f32) * y_im,
        axis=0,
        keepdims=True,
    )
    out[:, :, 0:CELLS] = jnp.broadcast_to(total[None], (NZ, 1, CELLS))
    out[:, :, CELLS:LONG] = jnp.broadcast_to(mis[None], (NZ, 1, 128))


def gather_z(parts, out):
    out[...] = jnp.broadcast_to(
        jnp.sum(parts[...], axis=0, keepdims=True), out.shape
    )


def finish(parts, source, new_source, misfit):
    mine = lax.axis_index("xh") * 2 + lax.axis_index("core")
    squares = jnp.zeros((1, CELLS), f32)
    own = jnp.zeros((1, LONG), f32)
    for f in range(NF):
        here = parts[f]
        for q in range(1, NQ):
            here = here + parts[q * NF + f]
        squares = squares + here[:, 0:CELLS] * here[:, 0:CELLS]
        own = jnp.where(mine == f, here, own)
    rms = jnp.sqrt(jnp.sum(squares, keepdims=True) / (NF * CELLS) + 1e-06)
    new_source[...] = source[...] * jnp.exp(-0.5 * own[:, 0:CELLS] / rms)
    stations = NZ * NQ * ROWS
    misfit[0] = jnp.max(own[:, CELLS:LONG]) / (stations * stations)


def shape(dtype, *dims):
    return jax.ShapeDtypeStruct(dims, dtype)


def from_z(array, u):
    return lax.ppermute(array, "z", [(z, (z - u) % NZ) for z in range(NZ)])


def local(spectra, green, source, pair_mask):
    g = green[0]
    vmem = pl.BlockSpec(memory_space=pltpu.VMEM)
    tall = ROWS * (1 + len(OFFSETS))
    near, far, two_mask, own_mask, own_spec = pl.pallas_call(
        pack_line,
        out_shape=[
            shape(bf16, MASKED, CELLS),
            shape(bf16, MASKED, CELLS),
            shape(bf16, 32, CELLS),
            shape(bf16, ROWS, WIDE),
            shape(f32, ROWS, 128),
        ],
        in_specs=[vmem] * 3,
        out_specs=[vmem] * 5,
        name="pack_line",
    )(g, pair_mask, spectra[0])
    three = from_z(from_z(from_z(far, -1), -1), -1)
    one = from_z(near, 1)
    two_mask = from_z(two_mask, 2)
    shared = pl.pallas_call(
        pack_plane,
        out_shape=shape(bf16, NQ, SHARED, CELLS),
        in_specs=[vmem] * 3,
        out_specs=vmem,
        name="pack_plane",
    )(g, pair_mask, own_spec)
    shared = lax.all_to_all(shared, PLANE, 0, 0, tiled=True)
    two = from_z(one[:MASK], 1)
    four = from_z(two, 2)
    ready = pl.pallas_call(
        prepare,
        out_shape=[shape(bf16, tall, CELLS)] * 4
        + [shape(f32, tall, WIDE)]
        + [shape(f32, tall, 128)] * 2,
        in_specs=[vmem] * 9,
        out_specs=[vmem] * 7,
        cost_estimate=pl.CostEstimate(
            flops=PREPARE, transcendentals=0, bytes_accessed=0
        ),
        name="prepare",
    )(source, g, own_mask, own_spec, one, two, two_mask, three, four)
    part = pl.pallas_call(
        absorb,
        out_shape=shape(f32, NZ, 1, LONG),
        in_specs=[vmem] * 8,
        out_specs=vmem,
        scratch_shapes=[
            pltpu.VMEM((WIDE, CELLS), bf16),
            pltpu.VMEM((WIDE, CELLS), bf16),
            pltpu.VMEM((8, WIDE), f32),
            pltpu.VMEM((WIDE, 4 * ROWS), bf16),
        ],
        name="absorb",
    )(shared, *ready)
    part = lax.all_to_all(part, "z", 0, 0, tiled=True)
    part = pl.pallas_call(
        gather_z,
        out_shape=shape(f32, NQ * NF, 1, LONG),
        in_specs=[vmem],
        out_specs=vmem,
        name="gather_z",
    )(part)
    part = lax.all_to_all(part, PLANE + FREQ, 0, 0, tiled=True)
    return pl.pallas_call(
        finish,
        out_shape=(shape(f32, 1, CELLS), shape(f32, 1)),
        in_specs=[vmem, vmem],
        out_specs=(vmem, pl.BlockSpec(memory_space=pltpu.SMEM)),
        name="finish",
    )(part, source)


def solution(mesh):
    fine = Mesh(mesh.devices.reshape(NZ, NX, NY, 2, 2), STA + FREQ)
    placed = (P(FREQ, None, STA), P(FREQ, None, STA, None), P(FREQ, None), P(STA, None))
    return jax.shard_map(
        local, mesh=fine, in_specs=placed, out_specs=(P(FREQ, None), P(FREQ)), check_vma=False
    )
```

```python
import jax
import jax.numpy as jnp
from jax import lax
from jax.experimental import pallas as pl
from jax.experimental.pallas import tpu as pltpu
from jax.sharding import Mesh, PartitionSpec as P

NZ, NX, NY = 8, 2, 4
NQ = NX * NY
NF = 4
ROWS = 64
CELLS = 1024
WIDE = NQ * ROWS
PLANE = ("xl", "y")
FREQ = ("xh", "core")
STA = ("z",) + PLANE
OFFSETS = (1, 2, -3, 4)
SHARED = 152
LONG = CELLS + 128
f32, bf16 = jnp.float32, jnp.bfloat16


def nt(a, b):
    return lax.dot_general(
        a, b, (((1,), (1,)), ((), ())), preferred_element_type=f32
    )


def nn(a, b):
    return lax.dot_general(
        a, b, (((1,), (0,)), ((), ())), preferred_element_type=f32
    )


def identity(n):
    down = lax.broadcasted_iota(jnp.int32, (n, n), 0)
    across = lax.broadcasted_iota(jnp.int32, (n, n), 1)
    return (down == across).astype(f32).astype(bf16)


SPEC, IMAG, REAL, MASK, MASKED = 0, 8, 72, 136, 168
PREPARE = 16_500_000_000


def window(mask, at):
    start = pl.multiple_of(lax.rem(at + NZ, NZ) * WIDE, WIDE)
    return mask[:, pl.ds(start, WIDE)].astype(f32)


def put_mask(ref, part):
    ref[:, 0:512] = part[0:32]
    ref[:, 512:1024] = part[32:64]


def take_mask(ref, at):
    return jnp.concatenate(
        [ref[at : at + 32, 0:512], ref[at : at + 32, 512:1024]], axis=0
    ).astype(f32)


def take_spectra(ref, at):
    return jnp.concatenate(
        [ref[at : at + 8, 128 * g : 128 * (g + 1)].astype(f32) for g in range(8)],
        axis=0,
    )


def pack(
    green, mask_hbm, spec_row, near, far, two, shared, own_mask, own_spec,
    mask, masks, spec8, extra, sems
):
    z = lax.axis_index("z")
    used = []

    def copy(src, dst):
        done = pltpu.make_async_copy(src, dst, sems.at[len(used)])
        done.start()
        used.append(done)
        return done

    loaded = copy(mask_hbm, mask)
    for ref in (near, far):
        copy(green.at[1], ref.at[IMAG : IMAG + ROWS])
        copy(green.at[0], ref.at[REAL : REAL + ROWS])
    for q in range(NQ):
        copy(green.at[0], shared.at[q, 0:64])
        copy(green.at[1], shared.at[q, 64:128])
    row = spec_row[...]
    col = nt(identity(ROWS), row)
    lane = lax.broadcasted_iota(jnp.int32, (ROWS, 128), 1)
    own_spec[...] = jnp.where(
        lane == 0, col[:, 0:1], jnp.where(lane == 1, col[:, 1:2], 0.0)
    )
    own_spec[0:2, 64:128] = row.astype(f32)
    spectra = own_spec[...].astype(bf16)
    for g in range(8):
        spec8[:, 128 * g : 128 * (g + 1)] = spectra[8 * g : 8 * (g + 1)]
    copy(spec8, near.at[SPEC : SPEC + 8])
    copy(spec8, far.at[SPEC : SPEC + 8])
    loaded.wait()
    for k, (u, ref) in enumerate(((1, near), (-3, far), (2, two))):
        put_mask(masks.at[k], window(mask, z - u).astype(bf16))
        copy(masks.at[k], two if ref is two else ref.at[MASK : MASK + 32])
    wide = [window(mask, z + u) for u in OFFSETS]
    for q in range(NQ):
        part = jnp.concatenate(
            [w[:, ROWS * q : ROWS * (q + 1)] for w in wide], axis=1
        ).astype(bf16)
        for g in range(4):
            extra[q, 0:16, 256 * g : 256 * (g + 1)] = part[16 * g : 16 * (g + 1)]
        for g in range(8):
            extra[q, 16:24, 128 * g : 128 * (g + 1)] = spectra[8 * g : 8 * (g + 1)]
        copy(extra.at[q], shared.at[q, 128:152])
    own_mask[...] = window(mask, z).astype(bf16)
    for done in used[1:]:
        done.wait()


def prepare(
    source, green, own_mask, own_spec, one, two, two_mask, three, four,
    wt_re, wt_im, weight, spec_re, spec_im
):
    scale = source[...]
    real, imag = slice(REAL, REAL + ROWS), slice(IMAG, IMAG + ROWS)
    us = [own_spec[...]]
    held = [(green[0], green[1])]
    for ref in (one, two, three, four):
        us.append(take_spectra(ref, SPEC))
        held.append((ref[real, :], ref[imag, :]))
    masks = [
        own_mask[...].astype(f32),
        take_mask(one, MASK),
        take_mask(two_mask, 0),
        take_mask(three, MASK),
        jnp.zeros((ROWS, WIDE), f32),
    ]
    for k, (re, im) in enumerate(held):
        rows = slice(ROWS * k, ROWS * (k + 1))
        wt_re[rows, :] = (scale * re.astype(f32)).astype(bf16)
        wt_im[rows, :] = (scale * im.astype(f32)).astype(bf16)
        weight[rows, :] = masks[k]
        spec_re[rows, :] = jnp.broadcast_to(us[k][:, 0:1], (ROWS, 128))
        spec_im[rows, :] = jnp.broadcast_to(us[k][:, 1:2], (ROWS, 128))


def absorb(
    shared, green, one, two, three, four, wt_re, wt_im, weight, spec_re, spec_im,
    out, far_re, far_im, extra, far_spec, back, sems
):
    copies = []
    for q in range(NQ):
        rows = slice(ROWS * q, ROWS * (q + 1))
        for i, (src, dst) in enumerate(
            (
                (shared.at[q, 0:64], far_re.at[rows]),
                (shared.at[q, 64:128], far_im.at[rows]),
                (shared.at[q, 128:152], extra.at[q]),
            )
        ):
            copies.append(pltpu.make_async_copy(src, dst, sems.at[3 * q + i]))
            copies[-1].start()
    for done in copies:
        done.wait()
    for q in range(NQ):
        rows = slice(ROWS * q, ROWS * (q + 1))
        for g in range(4):
            back[ROWS * q + 16 * g : ROWS * q + 16 * (g + 1), :] = extra[
                q, 0:16, 256 * g : 256 * (g + 1)
            ]
        far_spec[0:2, rows] = extra[q, 16:24, 0:128].astype(f32)[0:2, 64:128]
    behind = nt(identity(4 * ROWS), back[...])
    counts = weight[...] + jnp.concatenate(
        [jnp.zeros((ROWS, WIDE), f32), behind], axis=0
    )
    u_re, u_im = spec_re[:, 0:1], spec_im[:, 0:1]
    v_re, v_im = far_spec[0:1, :], far_spec[1:2, :]
    g_re, g_im = far_re[...], far_im[...]
    model_re = nt(wt_re[...], g_re) + nt(wt_im[...], g_im)
    model_im = nt(wt_im[...], g_re) - nt(wt_re[...], g_im)
    x_re = (u_re * v_re + u_im * v_im) - model_re
    x_im = (u_im * v_re - u_re * v_im) - model_im
    mis = 0.5 * jnp.sum(counts * (x_re * x_re + x_im * x_im), keepdims=True)
    r_re = (counts * x_re.astype(bf16).astype(f32)).astype(bf16)
    r_im = (counts * x_im.astype(bf16).astype(f32)).astype(bf16)
    y_re = nn(r_re, g_re) - nn(r_im, g_im)
    y_im = nn(r_re, g_im) + nn(r_im, g_re)
    real, imag = slice(REAL, REAL + ROWS), slice(IMAG, IMAG + ROWS)
    held = [(green[0], green[1])]
    for ref in (one, two, three, four):
        held.append((ref[real, :], ref[imag, :]))
    total = jnp.zeros((ROWS, CELLS), f32)
    for k, (re, im) in enumerate(held):
        rows = slice(ROWS * k, ROWS * (k + 1))
        total = total + (re.astype(f32) * y_re[rows] + im.astype(f32) * y_im[rows])
    total = -jnp.sum(total, axis=0, keepdims=True)
    out[:, :, 0:CELLS] = jnp.broadcast_to(total[None], (NZ, 1, CELLS))
    out[:, :, CELLS:LONG] = jnp.broadcast_to(mis[None], (NZ, 1, 128))


def gather_z(parts, out):
    out[...] = jnp.broadcast_to(
        jnp.sum(parts[...], axis=0, keepdims=True), out.shape
    )


def finish(parts, source, new_source, misfit):
    mine = lax.axis_index("xh") * 2 + lax.axis_index("core")
    squares = jnp.zeros((1, CELLS), f32)
    own = jnp.zeros((1, LONG), f32)
    for f in range(NF):
        here = parts[f]
        for q in range(1, NQ):
            here = here + parts[q * NF + f]
        squares = squares + here[:, 0:CELLS] * here[:, 0:CELLS]
        own = jnp.where(mine == f, here, own)
    rms = jnp.sqrt(jnp.sum(squares, keepdims=True) / (NF * CELLS) + 1e-06)
    new_source[...] = source[...] * jnp.exp(-0.5 * own[:, 0:CELLS] / rms)
    stations = NZ * NQ * ROWS
    misfit[0] = jnp.max(own[:, CELLS:LONG]) / (stations * stations)


def shape(dtype, *dims):
    return jax.ShapeDtypeStruct(dims, dtype)


def from_z(array, u):
    return lax.ppermute(array, "z", [(z, (z - u) % NZ) for z in range(NZ)])


def local(spectra, green, source, pair_mask):
    g = green[0]
    vmem = pl.BlockSpec(memory_space=pltpu.VMEM)
    tall = ROWS * (1 + len(OFFSETS))
    hbm = pl.BlockSpec(memory_space=pl.ANY)
    near, far, two_mask, shared, own_mask, own_spec = pl.pallas_call(
        pack,
        out_shape=[
            shape(bf16, MASKED, CELLS),
            shape(bf16, MASKED, CELLS),
            shape(bf16, 32, CELLS),
            shape(bf16, NQ, SHARED, CELLS),
            shape(bf16, ROWS, WIDE),
            shape(f32, ROWS, 128),
        ],
        in_specs=[hbm, hbm, vmem],
        out_specs=[hbm] * 4 + [vmem] * 2,
        scratch_shapes=[
            pltpu.VMEM((ROWS, NZ * WIDE), jnp.int32),
            pltpu.VMEM((3, 32, CELLS), bf16),
            pltpu.VMEM((8, CELLS), bf16),
            pltpu.VMEM((NQ, 24, CELLS), bf16),
            pltpu.SemaphoreType.DMA((34,)),
        ],
        name="pack",
    )(g, pair_mask, spectra[0])
    three = from_z(from_z(far, -2), -1)
    one = from_z(near, 1)
    two_mask = from_z(two_mask, 2)
    shared = lax.all_to_all(shared, PLANE, 0, 0, tiled=True)
    two = from_z(one[:MASK], 1)
    four = from_z(two, 2)
    ready = pl.pallas_call(
        prepare,
        out_shape=[shape(bf16, tall, CELLS)] * 2
        + [shape(f32, tall, WIDE)]
        + [shape(f32, tall, 128)] * 2,
        in_specs=[vmem] * 9,
        out_specs=[vmem] * 5,
        cost_estimate=pl.CostEstimate(
            flops=PREPARE, transcendentals=0, bytes_accessed=0
        ),
        name="prepare",
    )(source, g, own_mask, own_spec, one, two, two_mask, three, four)
    part = pl.pallas_call(
        absorb,
        out_shape=shape(f32, NZ, 1, LONG),
        in_specs=[hbm] + [vmem] * 10,
        out_specs=vmem,
        scratch_shapes=[
            pltpu.VMEM((WIDE, CELLS), bf16),
            pltpu.VMEM((WIDE, CELLS), bf16),
            pltpu.VMEM((NQ, 24, CELLS), bf16),
            pltpu.VMEM((8, WIDE), f32),
            pltpu.VMEM((WIDE, 4 * ROWS), bf16),
            pltpu.SemaphoreType.DMA((3 * NQ,)),
        ],
        name="absorb",
    )(shared, g, one, two, three, four, *ready)
    part = lax.all_to_all(part, "z", 0, 0, tiled=True)
    part = pl.pallas_call(
        gather_z,
        out_shape=shape(f32, NQ * NF, 1, LONG),
        in_specs=[vmem],
        out_specs=vmem,
        name="gather_z",
    )(part)
    part = lax.all_to_all(part, PLANE + FREQ, 0, 0, tiled=True)
    return pl.pallas_call(
        finish,
        out_shape=(shape(f32, 1, CELLS), shape(f32, 1)),
        in_specs=[vmem, vmem],
        out_specs=(vmem, pl.BlockSpec(memory_space=pltpu.SMEM)),
        name="finish",
    )(part, source)


def solution(mesh):
    fine = Mesh(mesh.devices.reshape(NZ, NX, NY, 2, 2), STA + FREQ)
    placed = (P(FREQ, None, STA), P(FREQ, None, STA, None), P(FREQ, None), P(STA, None))
    return jax.shard_map(
        local, mesh=fine, in_specs=placed, out_specs=(P(FREQ, None), P(FREQ)), check_vma=False
    )
```

```python
import jax
import jax.numpy as jnp
from jax import lax
from jax.experimental import pallas as pl
from jax.experimental.pallas import tpu as pltpu
from jax.sharding import Mesh, PartitionSpec as P

NZ, NX, NY = 8, 2, 4
NQ = NX * NY
NF = 4
ROWS = 64
CELLS = 1024
WIDE = NQ * ROWS
PLANE = ("xl", "y")
FREQ = ("xh", "core")
STA = ("z",) + PLANE
OFFSETS = (1, 2, -3, 4)
SHARED = 152
LONG = CELLS + 128
f32, bf16 = jnp.float32, jnp.bfloat16


def nt(a, b):
    return lax.dot_general(
        a, b, (((1,), (1,)), ((), ())), preferred_element_type=f32
    )


def nn(a, b):
    return lax.dot_general(
        a, b, (((1,), (0,)), ((), ())), preferred_element_type=f32
    )


def identity(n):
    down = lax.broadcasted_iota(jnp.int32, (n, n), 0)
    across = lax.broadcasted_iota(jnp.int32, (n, n), 1)
    return (down == across).astype(f32).astype(bf16)


SPEC, IMAG, REAL, MASK, NEXT, FULL = 0, 8, 72, 136, 168, 200
PREPARE = 16_500_000_000


def window(mask, at):
    start = pl.multiple_of(lax.rem(at + NZ, NZ) * WIDE, WIDE)
    return mask[:, pl.ds(start, WIDE)].astype(f32)


def put_mask(ref, part):
    ref[:, 0:512] = part[0:32]
    ref[:, 512:1024] = part[32:64]


def take_mask(ref, at):
    return jnp.concatenate(
        [ref[at : at + 32, 0:512], ref[at : at + 32, 512:1024]], axis=0
    ).astype(f32)


def take_spectra(ref, at):
    return jnp.concatenate(
        [ref[at : at + 8, 128 * g : 128 * (g + 1)].astype(f32) for g in range(8)],
        axis=0,
    )


def pack(
    green_hbm, mask_hbm, spec_row, near, far, shared, own_mask, own_spec,
    green, mask, masks, spec8, extra, sems
):
    z = lax.axis_index("z")
    used = []

    def copy(src, dst):
        done = pltpu.make_async_copy(src, dst, sems.at[len(used)])
        done.start()
        used.append(done)
        return done

    held = copy(green_hbm, green)
    loaded = copy(mask_hbm, mask)
    held.wait()
    for ref in (near, far):
        copy(green.at[1], ref.at[IMAG : IMAG + ROWS])
        copy(green.at[0], ref.at[REAL : REAL + ROWS])
    for q in range(NQ):
        copy(green.at[0], shared.at[q, 0:64])
        copy(green.at[1], shared.at[q, 64:128])
    row = spec_row[...]
    col = nt(identity(ROWS), row)
    lane = lax.broadcasted_iota(jnp.int32, (ROWS, 128), 1)
    own_spec[...] = jnp.where(
        lane == 0, col[:, 0:1], jnp.where(lane == 1, col[:, 1:2], 0.0)
    )
    own_spec[0:2, 64:128] = row.astype(f32)
    spectra = own_spec[...].astype(bf16)
    for g in range(8):
        spec8[:, 128 * g : 128 * (g + 1)] = spectra[8 * g : 8 * (g + 1)]
    copy(spec8, near.at[SPEC : SPEC + 8])
    copy(spec8, far.at[SPEC : SPEC + 8])
    loaded.wait()
    for k, (u, ref, at) in enumerate(((1, near, NEXT), (2, near, MASK), (-3, far, MASK))):
        put_mask(masks.at[k], window(mask, z - u).astype(bf16))
        copy(masks.at[k], ref.at[at : at + 32])
    wide = [window(mask, z + u) for u in OFFSETS]
    for q in range(NQ):
        part = jnp.concatenate(
            [w[:, ROWS * q : ROWS * (q + 1)] for w in wide], axis=1
        ).astype(bf16)
        for g in range(4):
            extra[q, 0:16, 256 * g : 256 * (g + 1)] = part[16 * g : 16 * (g + 1)]
        for g in range(8):
            extra[q, 16:24, 128 * g : 128 * (g + 1)] = spectra[8 * g : 8 * (g + 1)]
        copy(extra.at[q], shared.at[q, 128:152])
    own_mask[...] = window(mask, z).astype(bf16)
    for done in used[2:]:
        done.wait()


def prepare(
    source, green, own_mask, own_spec, one, two, three,
    wt_re, wt_im, weight, spec_re, spec_im
):
    scale = source[...]
    real, imag = slice(REAL, REAL + ROWS), slice(IMAG, IMAG + ROWS)
    us = [own_spec[...]]
    held = [(green[0], green[1])]
    for ref in (one, two, three):
        us.append(take_spectra(ref, SPEC))
        held.append((ref[real, :], ref[imag, :]))
    masks = [
        own_mask[...].astype(f32),
        take_mask(one, NEXT),
        take_mask(two, MASK),
        take_mask(three, MASK),
    ]
    for k, (re, im) in enumerate(held):
        rows = slice(ROWS * k, ROWS * (k + 1))
        wt_re[rows, :] = (scale * re.astype(f32)).astype(bf16)
        wt_im[rows, :] = (scale * im.astype(f32)).astype(bf16)
        weight[rows, :] = masks[k]
        spec_re[rows, :] = jnp.broadcast_to(us[k][:, 0:1], (ROWS, 128))
        spec_im[rows, :] = jnp.broadcast_to(us[k][:, 1:2], (ROWS, 128))


def absorb(
    shared, source, green, one, two, three, four,
    near_re, near_im, weight, spec_re, spec_im,
    out, far_re, far_im, extra, far_spec, back, wt_re, wt_im, sems
):
    copies = []
    for q in range(NQ):
        rows = slice(ROWS * q, ROWS * (q + 1))
        for i, (src, dst) in enumerate(
            (
                (shared.at[q, 0:64], far_re.at[rows]),
                (shared.at[q, 64:128], far_im.at[rows]),
                (shared.at[q, 128:152], extra.at[q]),
            )
        ):
            copies.append(pltpu.make_async_copy(src, dst, sems.at[3 * q + i]))
            copies[-1].start()
    real, imag = slice(REAL, REAL + ROWS), slice(IMAG, IMAG + ROWS)
    first, last = slice(0, 4 * ROWS), slice(4 * ROWS, 5 * ROWS)
    scale = source[...]
    wt_re[first, :] = near_re[...]
    wt_im[first, :] = near_im[...]
    wt_re[last, :] = (scale * four[real, :].astype(f32)).astype(bf16)
    wt_im[last, :] = (scale * four[imag, :].astype(f32)).astype(bf16)
    spec = take_spectra(four, SPEC)
    u_re = jnp.concatenate([spec_re[:, 0:1], spec[:, 0:1]], axis=0)
    u_im = jnp.concatenate([spec_im[:, 0:1], spec[:, 1:2]], axis=0)
    for done in copies:
        done.wait()
    for q in range(NQ):
        rows = slice(ROWS * q, ROWS * (q + 1))
        for g in range(4):
            back[ROWS * q + 16 * g : ROWS * q + 16 * (g + 1), :] = extra[
                q, 0:16, 256 * g : 256 * (g + 1)
            ]
        far_spec[0:2, rows] = extra[q, 16:24, 0:128].astype(f32)[0:2, 64:128]
    behind = nt(identity(4 * ROWS), back[...])
    counts = jnp.concatenate(
        [
            weight[0:ROWS, :],
            weight[ROWS : 4 * ROWS, :] + behind[0 : 3 * ROWS],
            behind[3 * ROWS : 4 * ROWS],
        ],
        axis=0,
    )
    v_re, v_im = far_spec[0:1, :], far_spec[1:2, :]
    g_re, g_im = far_re[...], far_im[...]
    model_re = nt(wt_re[...], g_re) + nt(wt_im[...], g_im)
    model_im = nt(wt_im[...], g_re) - nt(wt_re[...], g_im)
    x_re = (u_re * v_re + u_im * v_im) - model_re
    x_im = (u_im * v_re - u_re * v_im) - model_im
    mis = 0.5 * jnp.sum(counts * (x_re * x_re + x_im * x_im), keepdims=True)
    r_re = (counts * x_re.astype(bf16).astype(f32)).astype(bf16)
    r_im = (counts * x_im.astype(bf16).astype(f32)).astype(bf16)
    y_re = nn(r_re, g_re) - nn(r_im, g_im)
    y_im = nn(r_re, g_im) + nn(r_im, g_re)
    held = [(green[0], green[1])]
    for ref in (one, two, three, four):
        held.append((ref[real, :], ref[imag, :]))
    total = jnp.zeros((ROWS, CELLS), f32)
    for k, (re, im) in enumerate(held):
        rows = slice(ROWS * k, ROWS * (k + 1))
        total = total + (re.astype(f32) * y_re[rows] + im.astype(f32) * y_im[rows])
    total = -jnp.sum(total, axis=0, keepdims=True)
    out[:, :, 0:CELLS] = jnp.broadcast_to(total[None], (NZ, 1, CELLS))
    out[:, :, CELLS:LONG] = jnp.broadcast_to(mis[None], (NZ, 1, 128))


def gather_z(parts, out):
    out[...] = jnp.broadcast_to(
        jnp.sum(parts[...], axis=0, keepdims=True), out.shape
    )


def finish(parts, source, new_source, misfit):
    mine = lax.axis_index("xh") * 2 + lax.axis_index("core")
    squares = jnp.zeros((1, CELLS), f32)
    own = jnp.zeros((1, LONG), f32)
    for f in range(NF):
        here = parts[f]
        for q in range(1, NQ):
            here = here + parts[q * NF + f]
        squares = squares + here[:, 0:CELLS] * here[:, 0:CELLS]
        own = jnp.where(mine == f, here, own)
    rms = jnp.sqrt(jnp.sum(squares, keepdims=True) / (NF * CELLS) + 1e-06)
    new_source[...] = source[...] * jnp.exp(-0.5 * own[:, 0:CELLS] / rms)
    stations = NZ * NQ * ROWS
    misfit[0] = jnp.max(own[:, CELLS:LONG]) / (stations * stations)


def shape(dtype, *dims):
    return jax.ShapeDtypeStruct(dims, dtype)


def from_z(array, u):
    return lax.ppermute(array, "z", [(z, (z - u) % NZ) for z in range(NZ)])


def local(spectra, green, source, pair_mask):
    g = green[0]
    vmem = pl.BlockSpec(memory_space=pltpu.VMEM)
    hbm = pl.BlockSpec(memory_space=pltpu.HBM)
    near, far, shared, own_mask, own_spec = pl.pallas_call(
        pack,
        out_shape=[
            shape(bf16, FULL, CELLS),
            shape(bf16, NEXT, CELLS),
            shape(bf16, NQ, SHARED, CELLS),
            shape(bf16, ROWS, WIDE),
            shape(f32, ROWS, 128),
        ],
        in_specs=[hbm, hbm, vmem],
        out_specs=[hbm] * 3 + [vmem] * 2,
        scratch_shapes=[
            pltpu.VMEM((2, ROWS, CELLS), bf16),
            pltpu.VMEM((ROWS, NZ * WIDE), jnp.int32),
            pltpu.VMEM((3, 32, CELLS), bf16),
            pltpu.VMEM((8, CELLS), bf16),
            pltpu.VMEM((NQ, 24, CELLS), bf16),
            pltpu.SemaphoreType.DMA((35,)),
        ],
        name="pack",
    )(g, pair_mask, spectra[0])
    three = from_z(from_z(far, -2), -1)
    one = from_z(near, 1)
    shared = lax.all_to_all(shared, PLANE, 0, 0, tiled=True)
    two = from_z(one[:NEXT], 1)
    four = from_z(two[:MASK], 2)
    most = 4 * ROWS
    ready = pl.pallas_call(
        prepare,
        out_shape=[shape(bf16, most, CELLS)] * 2
        + [shape(f32, most, WIDE)]
        + [shape(f32, most, 128)] * 2,
        in_specs=[vmem] * 7,
        out_specs=[vmem] * 5,
        cost_estimate=pl.CostEstimate(
            flops=PREPARE, transcendentals=0, bytes_accessed=0
        ),
        name="prepare",
    )(source, g, own_mask, own_spec, one, two, three)
    part = pl.pallas_call(
        absorb,
        out_shape=shape(f32, NZ, 1, LONG),
        in_specs=[hbm] + [vmem] * 11,
        out_specs=vmem,
        scratch_shapes=[
            pltpu.VMEM((WIDE, CELLS), bf16),
            pltpu.VMEM((WIDE, CELLS), bf16),
            pltpu.VMEM((NQ, 24, CELLS), bf16),
            pltpu.VMEM((8, WIDE), f32),
            pltpu.VMEM((WIDE, 4 * ROWS), bf16),
            pltpu.VMEM((5 * ROWS, CELLS), bf16),
            pltpu.VMEM((5 * ROWS, CELLS), bf16),
            pltpu.SemaphoreType.DMA((3 * NQ,)),
        ],
        name="absorb",
    )(shared, source, g, one, two, three, four, *ready)
    part = lax.all_to_all(part, "z", 0, 0, tiled=True)
    part = pl.pallas_call(
        gather_z,
        out_shape=shape(f32, NQ * NF, 1, LONG),
        in_specs=[vmem],
        out_specs=vmem,
        name="gather_z",
    )(part)
    part = lax.all_to_all(part, PLANE + FREQ, 0, 0, tiled=True)
    return pl.pallas_call(
        finish,
        out_shape=(shape(f32, 1, CELLS), shape(f32, 1)),
        in_specs=[vmem, vmem],
        out_specs=(vmem, pl.BlockSpec(memory_space=pltpu.SMEM)),
        name="finish",
    )(part, source)


def solution(mesh):
    fine = Mesh(mesh.devices.reshape(NZ, NX, NY, 2, 2), STA + FREQ)
    placed = (P(FREQ, None, STA), P(FREQ, None, STA, None), P(FREQ, None), P(STA, None))
    return jax.shard_map(
        local, mesh=fine, in_specs=placed, out_specs=(P(FREQ, None), P(FREQ)), check_vma=False
    )
```

```python
import jax
import jax.numpy as jnp
from jax import lax
from jax.experimental import pallas as pl
from jax.experimental.pallas import tpu as pltpu
from jax.sharding import Mesh, PartitionSpec as P

NZ, NX, NY = 8, 2, 4
NQ = NX * NY
NF = 4
ROWS = 64
CELLS = 1024
WIDE = NQ * ROWS
PLANE = ("xl", "y")
FREQ = ("xh", "core")
STA = ("z",) + PLANE
OFFSETS = (1, 2, -3, 4)
SHARED = 152
LONG = CELLS + 128
f32, bf16 = jnp.float32, jnp.bfloat16


def nt(a, b):
    return lax.dot_general(
        a, b, (((1,), (1,)), ((), ())), preferred_element_type=f32
    )


def nn(a, b):
    return lax.dot_general(
        a, b, (((1,), (0,)), ((), ())), preferred_element_type=f32
    )


def identity(n):
    down = lax.broadcasted_iota(jnp.int32, (n, n), 0)
    across = lax.broadcasted_iota(jnp.int32, (n, n), 1)
    return (down == across).astype(f32).astype(bf16)


SPEC, IMAG, REAL, MASK, NEXT, FULL = 0, 8, 72, 136, 168, 200
PREPARE = 16_500_000_000


def window(mask, at):
    start = pl.multiple_of(lax.rem(at + NZ, NZ) * WIDE, WIDE)
    return mask[:, pl.ds(start, WIDE)].astype(f32)


def put_mask(ref, part):
    ref[:, 0:512] = part[0:32]
    ref[:, 512:1024] = part[32:64]


def take_mask(ref, at):
    return jnp.concatenate(
        [ref[at : at + 32, 0:512], ref[at : at + 32, 512:1024]], axis=0
    ).astype(f32)


def take_spectra(ref, at):
    return jnp.concatenate(
        [ref[at : at + 8, 128 * g : 128 * (g + 1)].astype(f32) for g in range(8)],
        axis=0,
    )


def pack(
    green, mask_hbm, spec_row, near, far, shared, own_mask, own_spec, mask, sem
):
    loading = pltpu.make_async_copy(mask_hbm, mask, sem)
    loading.start()
    z = lax.axis_index("z")
    row = spec_row[...]
    col = nt(identity(ROWS), row)
    lane = lax.broadcasted_iota(jnp.int32, (ROWS, 128), 1)
    own_spec[...] = jnp.where(
        lane == 0, col[:, 0:1], jnp.where(lane == 1, col[:, 1:2], 0.0)
    )
    own_spec[0:2, 64:128] = row.astype(f32)
    spectra = own_spec[...].astype(bf16)
    places = [(near, IMAG, REAL, SPEC), (far, IMAG, REAL, SPEC)]
    places += [(shared.at[q], 64, 0, 144) for q in range(NQ)]
    for ref, imag, real, spec in places:
        ref[imag : imag + ROWS, :] = green[1]
        ref[real : real + ROWS, :] = green[0]
        for g in range(8):
            ref[spec : spec + 8, 128 * g : 128 * (g + 1)] = spectra[8 * g : 8 * (g + 1)]
    loading.wait()
    for u, ref, at in ((1, near, NEXT), (2, near, MASK), (-3, far, MASK)):
        put_mask(ref.at[at : at + 32], window(mask, z - u).astype(bf16))
    own_mask[...] = window(mask, z).astype(bf16)
    wide = [window(mask, z + u) for u in OFFSETS]
    for q in range(NQ):
        part = jnp.concatenate(
            [w[:, ROWS * q : ROWS * (q + 1)] for w in wide], axis=1
        ).astype(bf16)
        for g in range(4):
            shared[q, 128:144, 256 * g : 256 * (g + 1)] = part[16 * g : 16 * (g + 1)]


def prepare(
    source, green, own_mask, own_spec, one, two, three,
    wt_re, wt_im, weight, spec_re, spec_im
):
    scale = source[...]
    real, imag = slice(REAL, REAL + ROWS), slice(IMAG, IMAG + ROWS)
    us = [own_spec[...]]
    held = [(green[0], green[1])]
    for ref in (one, two, three):
        us.append(take_spectra(ref, SPEC))
        held.append((ref[real, :], ref[imag, :]))
    masks = [
        own_mask[...].astype(f32),
        take_mask(one, NEXT),
        take_mask(two, MASK),
        take_mask(three, MASK),
    ]
    for k, (re, im) in enumerate(held):
        rows = slice(ROWS * k, ROWS * (k + 1))
        wt_re[rows, :] = (scale * re.astype(f32)).astype(bf16)
        wt_im[rows, :] = (scale * im.astype(f32)).astype(bf16)
        weight[rows, :] = masks[k]
        spec_re[rows, :] = jnp.broadcast_to(us[k][:, 0:1], (ROWS, 128))
        spec_im[rows, :] = jnp.broadcast_to(us[k][:, 1:2], (ROWS, 128))


def absorb(
    shared, source, green, one, two, three, four,
    near_re, near_im, weight, spec_re, spec_im,
    out, far_re, far_im, far_spec, back, wt
):
    real, imag = slice(REAL, REAL + ROWS), slice(IMAG, IMAG + ROWS)
    tall = 5 * ROWS
    scale = source[...]
    for at, near, part in ((0, near_re, real), (tall, near_im, imag)):
        wt[at : at + 4 * ROWS, :] = near[...]
        wt[at + 4 * ROWS : at + tall, :] = (scale * four[part, :].astype(f32)).astype(
            bf16
        )
    spec = take_spectra(four, SPEC)
    u_re = jnp.concatenate([spec_re[:, 0:1], spec[:, 0:1]], axis=0)
    u_im = jnp.concatenate([spec_im[:, 0:1], spec[:, 1:2]], axis=0)
    for q in range(NQ):
        rows = slice(ROWS * q, ROWS * (q + 1))
        ref = shared.at[q]
        far_re[rows, :] = ref[0:64, :]
        far_im[rows, :] = ref[64:128, :]
        for g in range(4):
            back[ROWS * q + 16 * g : ROWS * q + 16 * (g + 1), :] = ref[
                128:144, 256 * g : 256 * (g + 1)
            ]
        far_spec[0:2, rows] = ref[144:152, 0:128].astype(f32)[0:2, 64:128]
    behind = nt(identity(4 * ROWS), back[...])
    counts = jnp.concatenate(
        [
            weight[0:ROWS, :],
            weight[ROWS : 4 * ROWS, :] + behind[0 : 3 * ROWS],
            behind[3 * ROWS : 4 * ROWS],
        ],
        axis=0,
    )
    v_re, v_im = far_spec[0:1, :], far_spec[1:2, :]
    g_re, g_im = far_re[...], far_im[...]
    by_re = nt(wt[...], g_re)
    by_im = nt(wt[...], g_im)
    x_re = (u_re * v_re + u_im * v_im) - (by_re[:tall] + by_im[tall:])
    x_im = (u_im * v_re - u_re * v_im) - (by_re[tall:] - by_im[:tall])
    mis = 0.5 * jnp.sum(counts * (x_re * x_re + x_im * x_im), keepdims=True)
    resid = jnp.concatenate(
        [
            (counts * x_re.astype(bf16).astype(f32)).astype(bf16),
            (counts * x_im.astype(bf16).astype(f32)).astype(bf16),
        ],
        axis=0,
    )
    by_re = nn(resid, g_re)
    by_im = nn(resid, g_im)
    held = [(green[0], green[1])]
    for ref in (one, two, three, four):
        held.append((ref[real, :], ref[imag, :]))
    total = jnp.zeros((ROWS, CELLS), f32)
    for k, (re, im) in enumerate(held):
        rows = slice(ROWS * k, ROWS * (k + 1))
        more = slice(tall + ROWS * k, tall + ROWS * (k + 1))
        total = total + (
            re.astype(f32) * (by_re[rows] - by_im[more])
            + im.astype(f32) * (by_im[rows] + by_re[more])
        )
    total = -jnp.sum(total, axis=0, keepdims=True)
    out[:, :, 0:CELLS] = jnp.broadcast_to(total[None], (NZ, 1, CELLS))
    out[:, :, CELLS:LONG] = jnp.broadcast_to(mis[None], (NZ, 1, 128))


def gather_z(parts, out):
    out[...] = jnp.broadcast_to(
        jnp.sum(parts[...], axis=0, keepdims=True), out.shape
    )


def finish(parts, source, new_source, misfit):
    mine = lax.axis_index("xh") * 2 + lax.axis_index("core")
    squares = jnp.zeros((1, CELLS), f32)
    own = jnp.zeros((1, LONG), f32)
    for f in range(NF):
        here = parts[f]
        for q in range(1, NQ):
            here = here + parts[q * NF + f]
        squares = squares + here[:, 0:CELLS] * here[:, 0:CELLS]
        own = jnp.where(mine == f, here, own)
    rms = jnp.sqrt(jnp.sum(squares, keepdims=True) / (NF * CELLS) + 1e-06)
    new_source[...] = source[...] * jnp.exp(-0.5 * own[:, 0:CELLS] / rms)
    stations = NZ * NQ * ROWS
    misfit[0] = jnp.max(own[:, CELLS:LONG]) / (stations * stations)


def shape(dtype, *dims):
    return jax.ShapeDtypeStruct(dims, dtype)


def from_z(array, u):
    return lax.ppermute(array, "z", [(z, (z - u) % NZ) for z in range(NZ)])


def local(spectra, green, source, pair_mask):
    g = green[0]
    vmem = pl.BlockSpec(memory_space=pltpu.VMEM)
    near, far, shared, own_mask, own_spec = pl.pallas_call(
        pack,
        out_shape=[
            shape(bf16, FULL, CELLS),
            shape(bf16, NEXT, CELLS),
            shape(bf16, NQ, SHARED, CELLS),
            shape(bf16, ROWS, WIDE),
            shape(f32, ROWS, 128),
        ],
        in_specs=[vmem, pl.BlockSpec(memory_space=pl.ANY), vmem],
        out_specs=[vmem] * 5,
        scratch_shapes=[
            pltpu.VMEM((ROWS, NZ * WIDE), jnp.int32),
            pltpu.SemaphoreType.DMA,
        ],
        name="pack",
    )(g, pair_mask, spectra[0])
    three = from_z(from_z(far, -2), -1)
    one = from_z(near, 1)
    shared = lax.all_to_all(shared, PLANE, 0, 0, tiled=True)
    two = from_z(one[:NEXT], 1)
    four = from_z(two[:MASK], 2)
    most = 4 * ROWS
    ready = pl.pallas_call(
        prepare,
        out_shape=[shape(bf16, most, CELLS)] * 2
        + [shape(f32, most, WIDE)]
        + [shape(f32, most, 128)] * 2,
        in_specs=[vmem] * 7,
        out_specs=[vmem] * 5,
        cost_estimate=pl.CostEstimate(
            flops=PREPARE, transcendentals=0, bytes_accessed=0
        ),
        name="prepare",
    )(source, g, own_mask, own_spec, one, two, three)
    part = pl.pallas_call(
        absorb,
        out_shape=shape(f32, NZ, 1, LONG),
        in_specs=[vmem] * 12,
        out_specs=vmem,
        scratch_shapes=[
            pltpu.VMEM((WIDE, CELLS), bf16),
            pltpu.VMEM((WIDE, CELLS), bf16),
            pltpu.VMEM((8, WIDE), f32),
            pltpu.VMEM((WIDE, 4 * ROWS), bf16),
            pltpu.VMEM((10 * ROWS, CELLS), bf16),
        ],
        name="absorb",
    )(shared, source, g, one, two, three, four, *ready)
    part = lax.all_to_all(part, "z", 0, 0, tiled=True)
    part = pl.pallas_call(
        gather_z,
        out_shape=shape(f32, NQ * NF, 1, LONG),
        in_specs=[vmem],
        out_specs=vmem,
        name="gather_z",
    )(part)
    part = lax.all_to_all(part, PLANE + FREQ, 0, 0, tiled=True)
    return pl.pallas_call(
        finish,
        out_shape=(shape(f32, 1, CELLS), shape(f32, 1)),
        in_specs=[vmem, vmem],
        out_specs=(vmem, pl.BlockSpec(memory_space=pltpu.SMEM)),
        name="finish",
    )(part, source)


def solution(mesh):
    fine = Mesh(mesh.devices.reshape(NZ, NX, NY, 2, 2), STA + FREQ)
    placed = (P(FREQ, None, STA), P(FREQ, None, STA, None), P(FREQ, None), P(STA, None))
    return jax.shard_map(
        local, mesh=fine, in_specs=placed, out_specs=(P(FREQ, None), P(FREQ)), check_vma=False
    )
```

```python
import jax
import jax.numpy as jnp
from jax import lax
from jax.experimental import pallas as pl
from jax.experimental.pallas import tpu as pltpu
from jax.sharding import Mesh, PartitionSpec as P

NZ, NX, NY = 8, 2, 4
NQ = NX * NY
NF = 4
ROWS = 64
CELLS = 1024
WIDE = NQ * ROWS
PLANE = ("xl", "y")
FREQ = ("xh", "core")
STA = ("z",) + PLANE
OFFSETS = (1, 2, -3, 4)
SHARED = 152
LONG = CELLS + 128
f32, bf16 = jnp.float32, jnp.bfloat16


def nt(a, b):
    return lax.dot_general(
        a, b, (((1,), (1,)), ((), ())), preferred_element_type=f32
    )


def nn(a, b):
    return lax.dot_general(
        a, b, (((1,), (0,)), ((), ())), preferred_element_type=f32
    )


def identity(n):
    down = lax.broadcasted_iota(jnp.int32, (n, n), 0)
    across = lax.broadcasted_iota(jnp.int32, (n, n), 1)
    return (down == across).astype(f32).astype(bf16)


SPEC, IMAG, REAL, MASK, NEXT, FULL = 0, 8, 72, 136, 168, 200
PREPARE = 16_500_000_000


def start_windows(mask_hbm, windows, sems, offsets):
    z = lax.axis_index("z")
    copies = []
    for k, u in enumerate(offsets):
        start = pl.multiple_of(lax.rem(z + (u + NZ), NZ) * WIDE, WIDE)
        copies.append(
            pltpu.make_async_copy(
                mask_hbm.at[:, pl.ds(start, WIDE)], windows.at[k], sems.at[k]
            )
        )
        copies[-1].start()
    return copies


def put_mask(ref, part):
    ref[:, 0:512] = part[0:32]
    ref[:, 512:1024] = part[32:64]


def put_spectra(ref, spectra):
    for g in range(8):
        ref[:, 128 * g : 128 * (g + 1)] = spectra[8 * g : 8 * (g + 1)]


def take_mask(ref, at):
    return jnp.concatenate(
        [ref[at : at + 32, 0:512], ref[at : at + 32, 512:1024]], axis=0
    ).astype(f32)


def take_spectra(ref, at):
    return jnp.concatenate(
        [ref[at : at + 8, 128 * g : 128 * (g + 1)].astype(f32) for g in range(8)],
        axis=0,
    )


def pack_line(
    green, mask_hbm, spec_row, near, far, own_mask, own_spec, windows, sems
):
    loading = start_windows(mask_hbm, windows, sems, (-1, -2, 3, 0))
    row = spec_row[...]
    col = nt(identity(ROWS), row)
    lane = lax.broadcasted_iota(jnp.int32, (ROWS, 128), 1)
    own_spec[...] = jnp.where(
        lane == 0, col[:, 0:1], jnp.where(lane == 1, col[:, 1:2], 0.0)
    )
    own_spec[0:2, 64:128] = row.astype(f32)
    spectra = own_spec[...].astype(bf16)
    for ref in (near, far):
        ref[IMAG : IMAG + ROWS, :] = green[1]
        ref[REAL : REAL + ROWS, :] = green[0]
        put_spectra(ref.at[SPEC : SPEC + 8], spectra)
    for k, (ref, at) in enumerate(((near, NEXT), (near, MASK), (far, MASK))):
        loading[k].wait()
        put_mask(ref.at[at : at + 32], windows[k].astype(f32).astype(bf16))
    loading[3].wait()
    own_mask[...] = windows[3].astype(f32).astype(bf16)


def pack_plane(green, mask_hbm, own_spec, shared, windows, sems):
    loading = start_windows(mask_hbm, windows, sems, OFFSETS)
    spectra = own_spec[...].astype(bf16)
    for q in range(NQ):
        shared[q, 0:64, :] = green[0]
        shared[q, 64:128, :] = green[1]
        put_spectra(shared.at[q, 144:152], spectra)
    for copy in loading:
        copy.wait()
    wide = [windows[k].astype(f32) for k in range(len(OFFSETS))]
    for q in range(NQ):
        part = jnp.concatenate(
            [w[:, ROWS * q : ROWS * (q + 1)] for w in wide], axis=1
        ).astype(bf16)
        for g in range(4):
            shared[q, 128:144, 256 * g : 256 * (g + 1)] = part[16 * g : 16 * (g + 1)]


def prepare(
    source, green, own_mask, own_spec, one, two, three,
    wt_re, wt_im, weight, spec_re, spec_im
):
    scale = source[...]
    real, imag = slice(REAL, REAL + ROWS), slice(IMAG, IMAG + ROWS)
    us = [own_spec[...]]
    held = [(green[0], green[1])]
    for ref in (one, two, three):
        us.append(take_spectra(ref, SPEC))
        held.append((ref[real, :], ref[imag, :]))
    masks = [
        own_mask[...].astype(f32),
        take_mask(one, NEXT),
        take_mask(two, MASK),
        take_mask(three, MASK),
    ]
    for k, (re, im) in enumerate(held):
        rows = slice(ROWS * k, ROWS * (k + 1))
        wt_re[rows, :] = (scale * re.astype(f32)).astype(bf16)
        wt_im[rows, :] = (scale * im.astype(f32)).astype(bf16)
        weight[rows, :] = masks[k]
        spec_re[rows, :] = jnp.broadcast_to(us[k][:, 0:1], (ROWS, 128))
        spec_im[rows, :] = jnp.broadcast_to(us[k][:, 1:2], (ROWS, 128))


def absorb(
    shared, source, green_hbm, one_hbm, two_hbm, three_hbm, four_hbm,
    near_re, near_im, weight_hbm, spec_re_hbm, spec_im_hbm,
    out, far_re, far_im, far_spec, back, wt, green, blocks, weight, spec_re, spec_im, sems
):
    real, imag = slice(REAL, REAL + ROWS), slice(IMAG, IMAG + ROWS)
    tall, most = 5 * ROWS, 4 * ROWS
    copies = []
    for src, dst in (
        (four_hbm, blocks.at[3]),
        (weight_hbm, weight),
        (spec_re_hbm, spec_re),
        (spec_im_hbm, spec_im),
        (near_re, wt.at[0:most]),
        (near_im, wt.at[tall : tall + most]),
        (green_hbm, green),
        (one_hbm.at[0:MASK], blocks.at[0]),
        (two_hbm.at[0:MASK], blocks.at[1]),
        (three_hbm.at[0:MASK], blocks.at[2]),
    ):
        copies.append(pltpu.make_async_copy(src, dst, sems.at[len(copies)]))
        copies[-1].start()
    for q in range(NQ):
        rows = slice(ROWS * q, ROWS * (q + 1))
        ref = shared.at[q]
        far_re[rows, :] = ref[0:64, :]
        far_im[rows, :] = ref[64:128, :]
        for g in range(4):
            back[ROWS * q + 16 * g : ROWS * q + 16 * (g + 1), :] = ref[
                128:144, 256 * g : 256 * (g + 1)
            ]
        far_spec[0:2, rows] = ref[144:152, 0:128].astype(f32)[0:2, 64:128]
    behind = nt(identity(4 * ROWS), back[...])
    for copy in copies:
        copy.wait()
    four = blocks.at[3]
    scale = source[...]
    wt[most:tall, :] = (scale * four[real, :].astype(f32)).astype(bf16)
    wt[tall + most : 2 * tall, :] = (scale * four[imag, :].astype(f32)).astype(bf16)
    spec = take_spectra(four, SPEC)
    u_re = jnp.concatenate([spec_re[:, 0:1], spec[:, 0:1]], axis=0)
    u_im = jnp.concatenate([spec_im[:, 0:1], spec[:, 1:2]], axis=0)
    counts = jnp.concatenate(
        [
            weight[0:ROWS, :],
            weight[ROWS : 4 * ROWS, :] + behind[0 : 3 * ROWS],
            behind[3 * ROWS : 4 * ROWS],
        ],
        axis=0,
    )
    v_re, v_im = far_spec[0:1, :], far_spec[1:2, :]
    g_re, g_im = far_re[...], far_im[...]
    by_re = nt(wt[...], g_re)
    by_im = nt(wt[...], g_im)
    x_re = (u_re * v_re + u_im * v_im) - (by_re[:tall] + by_im[tall:])
    x_im = (u_im * v_re - u_re * v_im) - (by_re[tall:] - by_im[:tall])
    mis = 0.5 * jnp.sum(counts * (x_re * x_re + x_im * x_im), keepdims=True)
    resid = jnp.concatenate(
        [
            (counts * x_re.astype(bf16).astype(f32)).astype(bf16),
            (counts * x_im.astype(bf16).astype(f32)).astype(bf16),
        ],
        axis=0,
    )
    by_re = nn(resid, g_re)
    by_im = nn(resid, g_im)
    held = [(green[0], green[1])]
    for k in range(4):
        held.append((blocks[k, real, :], blocks[k, imag, :]))
    total = jnp.zeros((ROWS, CELLS), f32)
    for k, (re, im) in enumerate(held):
        rows = slice(ROWS * k, ROWS * (k + 1))
        more = slice(tall + ROWS * k, tall + ROWS * (k + 1))
        total = total + (
            re.astype(f32) * (by_re[rows] - by_im[more])
            + im.astype(f32) * (by_im[rows] + by_re[more])
        )
    total = -jnp.sum(total, axis=0, keepdims=True)
    out[:, :, 0:CELLS] = jnp.broadcast_to(total[None], (NZ, 1, CELLS))
    out[:, :, CELLS:LONG] = jnp.broadcast_to(mis[None], (NZ, 1, 128))


def gather_z(parts, out):
    out[...] = jnp.broadcast_to(
        jnp.sum(parts[...], axis=0, keepdims=True), out.shape
    )


def finish(parts, source, new_source, misfit):
    mine = lax.axis_index("xh") * 2 + lax.axis_index("core")
    squares = jnp.zeros((1, CELLS), f32)
    own = jnp.zeros((1, LONG), f32)
    for f in range(NF):
        here = parts[f]
        for q in range(1, NQ):
            here = here + parts[q * NF + f]
        squares = squares + here[:, 0:CELLS] * here[:, 0:CELLS]
        own = jnp.where(mine == f, here, own)
    rms = jnp.sqrt(jnp.sum(squares, keepdims=True) / (NF * CELLS) + 1e-06)
    new_source[...] = source[...] * jnp.exp(-0.5 * own[:, 0:CELLS] / rms)
    stations = NZ * NQ * ROWS
    misfit[0] = jnp.max(own[:, CELLS:LONG]) / (stations * stations)


def shape(dtype, *dims):
    return jax.ShapeDtypeStruct(dims, dtype)


def from_z(array, u):
    return lax.ppermute(array, "z", [(z, (z - u) % NZ) for z in range(NZ)])


def local(spectra, green, source, pair_mask):
    g = green[0]
    vmem = pl.BlockSpec(memory_space=pltpu.VMEM)
    hbm = pl.BlockSpec(memory_space=pltpu.HBM)
    windows = [
        pltpu.VMEM((4, ROWS, WIDE), jnp.int32),
        pltpu.SemaphoreType.DMA((4,)),
    ]
    near, far, own_mask, own_spec = pl.pallas_call(
        pack_line,
        out_shape=[
            shape(bf16, FULL, CELLS),
            shape(bf16, NEXT, CELLS),
            shape(bf16, ROWS, WIDE),
            shape(f32, ROWS, 128),
        ],
        in_specs=[vmem, hbm, vmem],
        out_specs=[vmem] * 4,
        scratch_shapes=windows,
        name="pack_line",
    )(g, pair_mask, spectra[0])
    shared = pl.pallas_call(
        pack_plane,
        out_shape=shape(bf16, NQ, SHARED, CELLS),
        in_specs=[vmem, hbm, vmem],
        out_specs=vmem,
        scratch_shapes=windows,
        name="pack_plane",
    )(g, pair_mask, own_spec)
    three = from_z(from_z(far, -2), -1)
    one = from_z(near, 1)
    shared = lax.all_to_all(shared, PLANE, 0, 0, tiled=True)
    two = from_z(one[:NEXT], 1)
    four = from_z(two[:MASK], 2)
    most = 4 * ROWS
    ready = pl.pallas_call(
        prepare,
        out_shape=[shape(bf16, most, CELLS)] * 2
        + [shape(f32, most, WIDE)]
        + [shape(f32, most, 128)] * 2,
        in_specs=[vmem] * 7,
        out_specs=[vmem] * 5,
        cost_estimate=pl.CostEstimate(
            flops=PREPARE, transcendentals=0, bytes_accessed=0
        ),
        name="prepare",
    )(source, g, own_mask, own_spec, one, two, three)
    part = pl.pallas_call(
        absorb,
        out_shape=shape(f32, NZ, 1, LONG),
        in_specs=[vmem] * 2 + [hbm] * 10,
        out_specs=vmem,
        scratch_shapes=[
            pltpu.VMEM((WIDE, CELLS), bf16),
            pltpu.VMEM((WIDE, CELLS), bf16),
            pltpu.VMEM((8, WIDE), f32),
            pltpu.VMEM((WIDE, 4 * ROWS), bf16),
            pltpu.VMEM((10 * ROWS, CELLS), bf16),
            pltpu.VMEM((2, ROWS, CELLS), bf16),
            pltpu.VMEM((4, MASK, CELLS), bf16),
            pltpu.VMEM((most, WIDE), f32),
            pltpu.VMEM((most, 128), f32),
            pltpu.VMEM((most, 128), f32),
            pltpu.SemaphoreType.DMA((10,)),
        ],
        name="absorb",
    )(shared, source, g, one, two, three, four, *ready)
    part = lax.all_to_all(part, "z", 0, 0, tiled=True)
    part = pl.pallas_call(
        gather_z,
        out_shape=shape(f32, NQ * NF, 1, LONG),
        in_specs=[vmem],
        out_specs=vmem,
        name="gather_z",
    )(part)
    part = lax.all_to_all(part, PLANE + FREQ, 0, 0, tiled=True)
    return pl.pallas_call(
        finish,
        out_shape=(shape(f32, 1, CELLS), shape(f32, 1)),
        in_specs=[vmem, vmem],
        out_specs=(vmem, pl.BlockSpec(memory_space=pltpu.SMEM)),
        name="finish",
    )(part, source)


def solution(mesh):
    fine = Mesh(mesh.devices.reshape(NZ, NX, NY, 2, 2), STA + FREQ)
    placed = (P(FREQ, None, STA), P(FREQ, None, STA, None), P(FREQ, None), P(STA, None))
    return jax.shard_map(
        local, mesh=fine, in_specs=placed, out_specs=(P(FREQ, None), P(FREQ)), check_vma=False
    )
```

```python
import jax
import jax.numpy as jnp
from jax import lax
from jax.experimental import pallas as pl
from jax.experimental.pallas import tpu as pltpu
from jax.sharding import Mesh, PartitionSpec as P

NZ, NX, NY = 8, 2, 4
NQ = NX * NY
NF = 4
ROWS = 64
CELLS = 1024
WIDE = NQ * ROWS
PLANE = ("xl", "y")
FREQ = ("xh", "core")
STA = ("z",) + PLANE
OFFSETS = (1, 2, -3, 4)
SHARED = 152
LONG = CELLS + 128
f32, bf16 = jnp.float32, jnp.bfloat16


def nt(a, b):
    return lax.dot_general(
        a, b, (((1,), (1,)), ((), ())), preferred_element_type=f32
    )


def nn(a, b):
    return lax.dot_general(
        a, b, (((1,), (0,)), ((), ())), preferred_element_type=f32
    )


def identity(n):
    down = lax.broadcasted_iota(jnp.int32, (n, n), 0)
    across = lax.broadcasted_iota(jnp.int32, (n, n), 1)
    return (down == across).astype(f32).astype(bf16)


SPEC, IMAG, REAL, MASK, NEXT, FULL = 0, 8, 72, 136, 168, 200
PREPARE = 16_500_000_000


def window(mask, at):
    start = pl.multiple_of(lax.rem(at + NZ, NZ) * WIDE, WIDE)
    return mask[:, pl.ds(start, WIDE)].astype(f32)


def put_mask(ref, part):
    ref[:, 0:512] = part[0:32]
    ref[:, 512:1024] = part[32:64]


def take_mask(ref, at):
    return jnp.concatenate(
        [ref[at : at + 32, 0:512], ref[at : at + 32, 512:1024]], axis=0
    ).astype(f32)


def take_spectra(ref, at):
    return jnp.concatenate(
        [ref[at : at + 8, 128 * g : 128 * (g + 1)].astype(f32) for g in range(8)],
        axis=0,
    )


def put_spectra(ref, spectra):
    for g in range(8):
        ref[:, 128 * g : 128 * (g + 1)] = spectra[8 * g : 8 * (g + 1)]


def pack_line(green, mask, spec_row, near, far, own_mask, own_spec):
    z = lax.axis_index("z")
    row = spec_row[...]
    col = nt(identity(ROWS), row)
    lane = lax.broadcasted_iota(jnp.int32, (ROWS, 128), 1)
    own_spec[...] = jnp.where(
        lane == 0, col[:, 0:1], jnp.where(lane == 1, col[:, 1:2], 0.0)
    )
    own_spec[0:2, 64:128] = row.astype(f32)
    spectra = own_spec[...].astype(bf16)
    for ref in (near, far):
        ref[IMAG : IMAG + ROWS, :] = green[1]
        ref[REAL : REAL + ROWS, :] = green[0]
        put_spectra(ref.at[SPEC : SPEC + 8], spectra)
    for u, ref, at in ((1, near, NEXT), (2, near, MASK), (-3, far, MASK)):
        put_mask(ref.at[at : at + 32], window(mask, z - u).astype(bf16))
    own_mask[...] = window(mask, z).astype(bf16)


def pack_plane(green, mask, own_spec, shared):
    z = lax.axis_index("z")
    spectra = own_spec[...].astype(bf16)
    wide = [window(mask, z + u) for u in OFFSETS]
    for q in range(NQ):
        shared[q, 0:64, :] = green[0]
        shared[q, 64:128, :] = green[1]
        put_spectra(shared.at[q, 144:152], spectra)
        part = jnp.concatenate(
            [w[:, ROWS * q : ROWS * (q + 1)] for w in wide], axis=1
        ).astype(bf16)
        for g in range(4):
            shared[q, 128:144, 256 * g : 256 * (g + 1)] = part[16 * g : 16 * (g + 1)]


MOST = 4 * ROWS
WT_RE, WT_IM, NEAR_RE, NEAR_IM, COUNT = (MOST * i for i in range(5))
SPECTRA = COUNT + MOST // 2
BUNDLE = SPECTRA + MOST // 8


def prepare(source, green, own_mask, own_spec, one, two, three, bundle):
    scale = source[...]
    real, imag = slice(REAL, REAL + ROWS), slice(IMAG, IMAG + ROWS)
    us = [own_spec[...]]
    held = [(green[0], green[1])]
    for ref in (one, two, three):
        us.append(take_spectra(ref, SPEC))
        held.append((ref[real, :], ref[imag, :]))
    masks = [
        own_mask[...].astype(f32),
        take_mask(one, NEXT),
        take_mask(two, MASK),
        take_mask(three, MASK),
    ]
    for k, (re, im) in enumerate(held):
        at = ROWS * k
        bundle[NEAR_RE + at : NEAR_RE + at + ROWS, :] = re
        bundle[NEAR_IM + at : NEAR_IM + at + ROWS, :] = im
        bundle[WT_RE + at : WT_RE + at + ROWS, :] = (scale * re.astype(f32)).astype(bf16)
        bundle[WT_IM + at : WT_IM + at + ROWS, :] = (scale * im.astype(f32)).astype(bf16)
    counts = jnp.concatenate(masks, axis=0).astype(bf16)
    for h in range(2):
        bundle[COUNT : COUNT + MOST // 2, WIDE * h : WIDE * (h + 1)] = counts[
            MOST // 2 * h : MOST // 2 * (h + 1)
        ]
    spectra = jnp.concatenate(us, axis=0).astype(bf16)
    for h in range(8):
        bundle[SPECTRA : SPECTRA + MOST // 8, 128 * h : 128 * (h + 1)] = spectra[
            MOST // 8 * h : MOST // 8 * (h + 1)
        ]


def absorb(shared, source, four, bundle, out, far_re, far_im, far_spec, back, wt):
    real, imag = slice(REAL, REAL + ROWS), slice(IMAG, IMAG + ROWS)
    tall = 5 * ROWS
    scale = source[...]
    for at, near, part in ((0, WT_RE, real), (tall, WT_IM, imag)):
        wt[at : at + MOST, :] = bundle[near : near + MOST, :]
        wt[at + MOST : at + tall, :] = (scale * four[part, :].astype(f32)).astype(bf16)
    spec = jnp.concatenate(
        [
            bundle[SPECTRA : SPECTRA + MOST // 8, 128 * h : 128 * (h + 1)].astype(f32)
            for h in range(8)
        ]
        + [take_spectra(four, SPEC)],
        axis=0,
    )
    u_re, u_im = spec[:, 0:1], spec[:, 1:2]
    weight = jnp.concatenate(
        [
            bundle[COUNT : COUNT + MOST // 2, WIDE * h : WIDE * (h + 1)].astype(f32)
            for h in range(2)
        ],
        axis=0,
    )
    for q in range(NQ):
        rows = slice(ROWS * q, ROWS * (q + 1))
        ref = shared.at[q]
        far_re[rows, :] = ref[0:64, :]
        far_im[rows, :] = ref[64:128, :]
        for g in range(4):
            back[ROWS * q + 16 * g : ROWS * q + 16 * (g + 1), :] = ref[
                128:144, 256 * g : 256 * (g + 1)
            ]
        far_spec[0:2, rows] = ref[144:152, 0:128].astype(f32)[0:2, 64:128]
    behind = nt(identity(4 * ROWS), back[...])
    counts = jnp.concatenate(
        [
            weight[0:ROWS],
            weight[ROWS : 4 * ROWS] + behind[0 : 3 * ROWS],
            behind[3 * ROWS : 4 * ROWS],
        ],
        axis=0,
    )
    v_re, v_im = far_spec[0:1, :], far_spec[1:2, :]
    g_re, g_im = far_re[...], far_im[...]
    by_re = nt(wt[...], g_re)
    by_im = nt(wt[...], g_im)
    x_re = (u_re * v_re + u_im * v_im) - (by_re[:tall] + by_im[tall:])
    x_im = (u_im * v_re - u_re * v_im) - (by_re[tall:] - by_im[:tall])
    mis = 0.5 * jnp.sum(counts * (x_re * x_re + x_im * x_im), keepdims=True)
    resid = jnp.concatenate(
        [
            (counts * x_re.astype(bf16).astype(f32)).astype(bf16),
            (counts * x_im.astype(bf16).astype(f32)).astype(bf16),
        ],
        axis=0,
    )
    by_re = nn(resid, g_re)
    by_im = nn(resid, g_im)
    held = []
    for k in range(4):
        at = ROWS * k
        held.append(
            (
                bundle[NEAR_RE + at : NEAR_RE + at + ROWS, :],
                bundle[NEAR_IM + at : NEAR_IM + at + ROWS, :],
            )
        )
    held.append((four[real, :], four[imag, :]))
    total = jnp.zeros((ROWS, CELLS), f32)
    for k, (re, im) in enumerate(held):
        rows = slice(ROWS * k, ROWS * (k + 1))
        more = slice(tall + ROWS * k, tall + ROWS * (k + 1))
        total = total + (
            re.astype(f32) * (by_re[rows] - by_im[more])
            + im.astype(f32) * (by_im[rows] + by_re[more])
        )
    total = -jnp.sum(total, axis=0, keepdims=True)
    out[:, :, 0:CELLS] = jnp.broadcast_to(total[None], (NZ, 1, CELLS))
    out[:, :, CELLS:LONG] = jnp.broadcast_to(mis[None], (NZ, 1, 128))


def gather_z(parts, out):
    out[...] = jnp.broadcast_to(
        jnp.sum(parts[...], axis=0, keepdims=True), out.shape
    )


def finish(parts, source, new_source, misfit):
    mine = lax.axis_index("xh") * 2 + lax.axis_index("core")
    squares = jnp.zeros((1, CELLS), f32)
    own = jnp.zeros((1, LONG), f32)
    for f in range(NF):
        here = parts[f]
        for q in range(1, NQ):
            here = here + parts[q * NF + f]
        squares = squares + here[:, 0:CELLS] * here[:, 0:CELLS]
        own = jnp.where(mine == f, here, own)
    rms = jnp.sqrt(jnp.sum(squares, keepdims=True) / (NF * CELLS) + 1e-06)
    new_source[...] = source[...] * jnp.exp(-0.5 * own[:, 0:CELLS] / rms)
    stations = NZ * NQ * ROWS
    misfit[0] = jnp.max(own[:, CELLS:LONG]) / (stations * stations)


def shape(dtype, *dims):
    return jax.ShapeDtypeStruct(dims, dtype)


def from_z(array, u):
    return lax.ppermute(array, "z", [(z, (z - u) % NZ) for z in range(NZ)])


def local(spectra, green, source, pair_mask):
    g = green[0]
    vmem = pl.BlockSpec(memory_space=pltpu.VMEM)
    near, far, own_mask, own_spec = pl.pallas_call(
        pack_line,
        out_shape=[
            shape(bf16, FULL, CELLS),
            shape(bf16, NEXT, CELLS),
            shape(bf16, ROWS, WIDE),
            shape(f32, ROWS, 128),
        ],
        in_specs=[vmem] * 3,
        out_specs=[vmem] * 4,
        name="pack_line",
    )(g, pair_mask, spectra[0])
    shared = pl.pallas_call(
        pack_plane,
        out_shape=shape(bf16, NQ, SHARED, CELLS),
        in_specs=[vmem] * 3,
        out_specs=vmem,
        name="pack_plane",
    )(g, pair_mask, own_spec)
    three = from_z(from_z(far, -2), -1)
    one = from_z(near, 1)
    shared = lax.all_to_all(shared, PLANE, 0, 0, tiled=True)
    two = from_z(one[:NEXT], 1)
    four = from_z(two[:MASK], 2)
    ready = pl.pallas_call(
        prepare,
        out_shape=shape(bf16, BUNDLE, CELLS),
        in_specs=[vmem] * 7,
        out_specs=vmem,
        cost_estimate=pl.CostEstimate(
            flops=PREPARE, transcendentals=0, bytes_accessed=0
        ),
        name="prepare",
    )(source, g, own_mask, own_spec, one, two, three)
    part = pl.pallas_call(
        absorb,
        out_shape=shape(f32, NZ, 1, LONG),
        in_specs=[vmem] * 4,
        out_specs=vmem,
        scratch_shapes=[
            pltpu.VMEM((WIDE, CELLS), bf16),
            pltpu.VMEM((WIDE, CELLS), bf16),
            pltpu.VMEM((8, WIDE), f32),
            pltpu.VMEM((WIDE, 4 * ROWS), bf16),
            pltpu.VMEM((10 * ROWS, CELLS), bf16),
        ],
        name="absorb",
        compiler_params=pltpu.CompilerParams(vmem_limit_bytes=40 << 20),
    )(shared, source, four, ready)
    part = lax.all_to_all(part, "z", 0, 0, tiled=True)
    part = pl.pallas_call(
        gather_z,
        out_shape=shape(f32, NQ * NF, 1, LONG),
        in_specs=[vmem],
        out_specs=vmem,
        name="gather_z",
        compiler_params=pltpu.CompilerParams(vmem_limit_bytes=8 << 20),
    )(part)
    part = lax.all_to_all(part, PLANE + FREQ, 0, 0, tiled=True)
    return pl.pallas_call(
        finish,
        out_shape=(shape(f32, 1, CELLS), shape(f32, 1)),
        in_specs=[vmem, vmem],
        out_specs=(vmem, pl.BlockSpec(memory_space=pltpu.SMEM)),
        name="finish",
        compiler_params=pltpu.CompilerParams(vmem_limit_bytes=8 << 20),
    )(part, source)


def solution(mesh):
    fine = Mesh(mesh.devices.reshape(NZ, NX, NY, 2, 2), STA + FREQ)
    placed = (P(FREQ, None, STA), P(FREQ, None, STA, None), P(FREQ, None), P(STA, None))
    return jax.shard_map(
        local, mesh=fine, in_specs=placed, out_specs=(P(FREQ, None), P(FREQ)), check_vma=False
    )
```

```python
import jax
import jax.numpy as jnp
from jax import lax
from jax.experimental import pallas as pl
from jax.experimental.pallas import tpu as pltpu
from jax.sharding import Mesh, PartitionSpec as P

NZ, NX, NY = 8, 2, 4
NQ = NX * NY
NF = 4
ROWS = 64
CELLS = 1024
WIDE = NQ * ROWS
PLANE = ("xl", "y")
FREQ = ("xh", "core")
STA = ("z",) + PLANE
OFFSETS = (1, 2, -3, 4)
SHARED = 152
LONG = CELLS + 128
f32, bf16 = jnp.float32, jnp.bfloat16


def nt(a, b):
    return lax.dot_general(
        a, b, (((1,), (1,)), ((), ())), preferred_element_type=f32
    )


def nn(a, b):
    return lax.dot_general(
        a, b, (((1,), (0,)), ((), ())), preferred_element_type=f32
    )


def identity(n):
    down = lax.broadcasted_iota(jnp.int32, (n, n), 0)
    across = lax.broadcasted_iota(jnp.int32, (n, n), 1)
    return (down == across).astype(f32).astype(bf16)


SPEC, IMAG, REAL, MASK, NEXT, FULL = 0, 8, 72, 136, 168, 200
PREPARE = 16_500_000_000


def window(mask, at):
    start = pl.multiple_of(lax.rem(at + NZ, NZ) * WIDE, WIDE)
    return mask[:, pl.ds(start, WIDE)].astype(f32)


def put_mask(ref, part):
    ref[:, 0:512] = part[0:32]
    ref[:, 512:1024] = part[32:64]


def take_mask(ref, at):
    return jnp.concatenate(
        [ref[at : at + 32, 0:512], ref[at : at + 32, 512:1024]], axis=0
    ).astype(f32)


def take_spectra(ref, at):
    return jnp.concatenate(
        [ref[at : at + 8, 128 * g : 128 * (g + 1)].astype(f32) for g in range(8)],
        axis=0,
    )


def put_spectra(ref, spectra):
    for g in range(8):
        ref[:, 128 * g : 128 * (g + 1)] = spectra[8 * g : 8 * (g + 1)]


def pack(green, mask, spec_row, near, far, shared, own_mask, own_spec):
    z = lax.axis_index("z")
    row = spec_row[...]
    col = nt(identity(ROWS), row)
    lane = lax.broadcasted_iota(jnp.int32, (ROWS, 128), 1)
    own_spec[...] = jnp.where(
        lane == 0, col[:, 0:1], jnp.where(lane == 1, col[:, 1:2], 0.0)
    )
    own_spec[0:2, 64:128] = row.astype(f32)
    spectra = own_spec[...].astype(bf16)
    for ref in (near, far):
        ref[IMAG : IMAG + ROWS, :] = green[1]
        ref[REAL : REAL + ROWS, :] = green[0]
        put_spectra(ref.at[SPEC : SPEC + 8], spectra)
    for u, ref, at in ((1, near, NEXT), (2, near, MASK), (-3, far, MASK)):
        put_mask(ref.at[at : at + 32], window(mask, z - u).astype(bf16))
    own_mask[...] = window(mask, z).astype(bf16)
    wide = [window(mask, z + u) for u in OFFSETS]
    for q in range(NQ):
        shared[q, 0:64, :] = green[0]
        shared[q, 64:128, :] = green[1]
        put_spectra(shared.at[q, 144:152], spectra)
        part = jnp.concatenate(
            [w[:, ROWS * q : ROWS * (q + 1)] for w in wide], axis=1
        ).astype(bf16)
        for g in range(4):
            shared[q, 128:144, 256 * g : 256 * (g + 1)] = part[16 * g : 16 * (g + 1)]


MOST = 3 * ROWS
WT_RE, WT_IM, NEAR_RE, NEAR_IM, COUNT = (MOST * i for i in range(5))
SPECTRA = COUNT + MOST // 2
BUNDLE = SPECTRA + MOST // 8


def prepare(source, green, own_mask, own_spec, one, two, bundle):
    scale = source[...]
    real, imag = slice(REAL, REAL + ROWS), slice(IMAG, IMAG + ROWS)
    us = [own_spec[...]]
    held = [(green[0], green[1])]
    for ref in (one, two):
        us.append(take_spectra(ref, SPEC))
        held.append((ref[real, :], ref[imag, :]))
    masks = [
        own_mask[...].astype(f32),
        take_mask(one, NEXT),
        take_mask(two, MASK),
    ]
    for k, (re, im) in enumerate(held):
        at = ROWS * k
        bundle[NEAR_RE + at : NEAR_RE + at + ROWS, :] = re
        bundle[NEAR_IM + at : NEAR_IM + at + ROWS, :] = im
        bundle[WT_RE + at : WT_RE + at + ROWS, :] = (scale * re.astype(f32)).astype(bf16)
        bundle[WT_IM + at : WT_IM + at + ROWS, :] = (scale * im.astype(f32)).astype(bf16)
    counts = jnp.concatenate(masks, axis=0).astype(bf16)
    for h in range(2):
        bundle[COUNT : COUNT + MOST // 2, WIDE * h : WIDE * (h + 1)] = counts[
            MOST // 2 * h : MOST // 2 * (h + 1)
        ]
    spectra = jnp.concatenate(us, axis=0)
    for h in range(8):
        bundle[SPECTRA : SPECTRA + MOST // 8, 128 * h : 128 * (h + 1)] = spectra[
            MOST // 8 * h : MOST // 8 * (h + 1)
        ].astype(bf16)


def absorb(shared, source, three, four, bundle, out, far_re, far_im, far_spec, back, wt):
    real, imag = slice(REAL, REAL + ROWS), slice(IMAG, IMAG + ROWS)
    tall = 5 * ROWS
    scale = source[...]
    for at, near, part in ((0, WT_RE, real), (tall, WT_IM, imag)):
        wt[at : at + MOST, :] = bundle[near : near + MOST, :]
        for k, ref in ((3, three), (4, four)):
            wt[at + ROWS * k : at + ROWS * (k + 1), :] = (
                scale * ref[part, :].astype(f32)
            ).astype(bf16)
    spec = jnp.concatenate(
        [
            bundle[SPECTRA : SPECTRA + MOST // 8, 128 * h : 128 * (h + 1)].astype(f32)
            for h in range(8)
        ]
        + [take_spectra(three, SPEC), take_spectra(four, SPEC)],
        axis=0,
    )
    u_re, u_im = spec[:, 0:1], spec[:, 1:2]
    weight = jnp.concatenate(
        [
            bundle[COUNT : COUNT + MOST // 2, WIDE * h : WIDE * (h + 1)].astype(f32)
            for h in range(2)
        ]
        + [take_mask(three, MASK)],
        axis=0,
    )
    for q in range(NQ):
        rows = slice(ROWS * q, ROWS * (q + 1))
        ref = shared.at[q]
        far_re[rows, :] = ref[0:64, :]
        far_im[rows, :] = ref[64:128, :]
        for g in range(4):
            back[ROWS * q + 16 * g : ROWS * q + 16 * (g + 1), :] = ref[
                128:144, 256 * g : 256 * (g + 1)
            ]
        far_spec[0:2, rows] = ref[144:152, 0:128].astype(f32)[0:2, 64:128]
    behind = nt(identity(4 * ROWS), back[...])
    counts = jnp.concatenate(
        [
            weight[0:ROWS],
            weight[ROWS : 4 * ROWS] + behind[0 : 3 * ROWS],
            behind[3 * ROWS : 4 * ROWS],
        ],
        axis=0,
    )
    v_re, v_im = far_spec[0:1, :], far_spec[1:2, :]
    g_re, g_im = far_re[...], far_im[...]
    by_re = nt(wt[...], g_re)
    by_im = nt(wt[...], g_im)
    x_re = (u_re * v_re + u_im * v_im) - (by_re[:tall] + by_im[tall:])
    x_im = (u_im * v_re - u_re * v_im) - (by_re[tall:] - by_im[:tall])
    mis = 0.5 * jnp.sum(counts * (x_re * x_re + x_im * x_im), keepdims=True)
    resid = jnp.concatenate(
        [
            (counts * x_re.astype(bf16).astype(f32)).astype(bf16),
            (counts * x_im.astype(bf16).astype(f32)).astype(bf16),
        ],
        axis=0,
    )
    by_re = nn(resid, g_re)
    by_im = nn(resid, g_im)
    held = []
    for k in range(3):
        at = ROWS * k
        held.append(
            (
                bundle[NEAR_RE + at : NEAR_RE + at + ROWS, :],
                bundle[NEAR_IM + at : NEAR_IM + at + ROWS, :],
            )
        )
    for ref in (three, four):
        held.append((ref[real, :], ref[imag, :]))
    total = jnp.zeros((ROWS, CELLS), f32)
    for k, (re, im) in enumerate(held):
        rows = slice(ROWS * k, ROWS * (k + 1))
        more = slice(tall + ROWS * k, tall + ROWS * (k + 1))
        total = total + (
            re.astype(f32) * (by_re[rows] - by_im[more])
            + im.astype(f32) * (by_im[rows] + by_re[more])
        )
    total = -jnp.sum(total, axis=0, keepdims=True)
    out[:, :, 0:CELLS] = jnp.broadcast_to(total[None], (NZ, 1, CELLS))
    out[:, :, CELLS:LONG] = jnp.broadcast_to(mis[None], (NZ, 1, 128))


def gather_z(parts, out):
    out[...] = jnp.broadcast_to(
        jnp.sum(parts[...], axis=0, keepdims=True), out.shape
    )


def finish(parts, source, new_source, misfit):
    mine = lax.axis_index("xh") * 2 + lax.axis_index("core")
    squares = jnp.zeros((1, CELLS), f32)
    own = jnp.zeros((1, LONG), f32)
    for f in range(NF):
        here = parts[f]
        for q in range(1, NQ):
            here = here + parts[q * NF + f]
        squares = squares + here[:, 0:CELLS] * here[:, 0:CELLS]
        own = jnp.where(mine == f, here, own)
    rms = jnp.sqrt(jnp.sum(squares, keepdims=True) / (NF * CELLS) + 1e-06)
    new_source[...] = source[...] * jnp.exp(-0.5 * own[:, 0:CELLS] / rms)
    stations = NZ * NQ * ROWS
    misfit[0] = jnp.max(own[:, CELLS:LONG]) / (stations * stations)


def shape(dtype, *dims):
    return jax.ShapeDtypeStruct(dims, dtype)


def from_z(array, u):
    return lax.ppermute(array, "z", [(z, (z - u) % NZ) for z in range(NZ)])


def local(spectra, green, source, pair_mask):
    g = green[0]
    vmem = pl.BlockSpec(memory_space=pltpu.VMEM)
    near, far, shared, own_mask, own_spec = pl.pallas_call(
        pack,
        out_shape=[
            shape(bf16, FULL, CELLS),
            shape(bf16, NEXT, CELLS),
            shape(bf16, NQ, SHARED, CELLS),
            shape(bf16, ROWS, WIDE),
            shape(f32, ROWS, 128),
        ],
        in_specs=[vmem] * 3,
        out_specs=[vmem] * 5,
        name="pack",
    )(g, pair_mask, spectra[0])
    three = from_z(from_z(far, -2), -1)
    one = from_z(near, 1)
    shared = lax.all_to_all(shared, PLANE, 0, 0, tiled=True)
    two = from_z(one[:NEXT], 1)
    four = from_z(two[:MASK], 2)
    ready = pl.pallas_call(
        prepare,
        out_shape=shape(bf16, BUNDLE, CELLS),
        in_specs=[vmem] * 6,
        out_specs=vmem,
        cost_estimate=pl.CostEstimate(
            flops=PREPARE, transcendentals=0, bytes_accessed=0
        ),
        name="prepare",
    )(source, g, own_mask, own_spec, one, two)
    part = pl.pallas_call(
        absorb,
        out_shape=shape(f32, NZ, 1, LONG),
        in_specs=[vmem] * 5,
        out_specs=vmem,
        scratch_shapes=[
            pltpu.VMEM((WIDE, CELLS), bf16),
            pltpu.VMEM((WIDE, CELLS), bf16),
            pltpu.VMEM((8, WIDE), f32),
            pltpu.VMEM((WIDE, 4 * ROWS), bf16),
            pltpu.VMEM((10 * ROWS, CELLS), bf16),
        ],
        name="absorb",
        compiler_params=pltpu.CompilerParams(vmem_limit_bytes=40 << 20),
    )(shared, source, three, four, ready)
    part = lax.all_to_all(part, "z", 0, 0, tiled=True)
    part = pl.pallas_call(
        gather_z,
        out_shape=shape(f32, NQ * NF, 1, LONG),
        in_specs=[vmem],
        out_specs=vmem,
        name="gather_z",
        compiler_params=pltpu.CompilerParams(vmem_limit_bytes=8 << 20),
    )(part)
    part = lax.all_to_all(part, PLANE + FREQ, 0, 0, tiled=True)
    return pl.pallas_call(
        finish,
        out_shape=(shape(f32, 1, CELLS), shape(f32, 1)),
        in_specs=[vmem, vmem],
        out_specs=(vmem, pl.BlockSpec(memory_space=pltpu.SMEM)),
        name="finish",
        compiler_params=pltpu.CompilerParams(vmem_limit_bytes=8 << 20),
    )(part, source)


def solution(mesh):
    fine = Mesh(mesh.devices.reshape(NZ, NX, NY, 2, 2), STA + FREQ)
    placed = (P(FREQ, None, STA), P(FREQ, None, STA, None), P(FREQ, None), P(STA, None))
    return jax.shard_map(
        local, mesh=fine, in_specs=placed, out_specs=(P(FREQ, None), P(FREQ)), check_vma=False
    )
```

```python
import jax
import jax.numpy as jnp
from jax import lax
from jax.experimental import pallas as pl
from jax.experimental.pallas import tpu as pltpu
from jax.sharding import Mesh, PartitionSpec as P

NZ, NX, NY = 8, 2, 4
NQ = NX * NY
NF = 4
ROWS = 64
CELLS = 1024
WIDE = NQ * ROWS
PLANE = ("xl", "y")
FREQ = ("xh", "core")
STA = ("z",) + PLANE
OFFSETS = (1, 2, -3, 4)
SHARED = 152
LONG = CELLS + 128
f32, bf16 = jnp.float32, jnp.bfloat16


def nt(a, b):
    return lax.dot_general(
        a, b, (((1,), (1,)), ((), ())), preferred_element_type=f32
    )


def nn(a, b):
    return lax.dot_general(
        a, b, (((1,), (0,)), ((), ())), preferred_element_type=f32
    )


def identity(n):
    down = lax.broadcasted_iota(jnp.int32, (n, n), 0)
    across = lax.broadcasted_iota(jnp.int32, (n, n), 1)
    return (down == across).astype(f32).astype(bf16)


SPEC, IMAG, REAL, MASK, NEXT, FULL = 0, 8, 72, 136, 168, 200
PREPARE = 17_500_000_000


def window(mask, at):
    start = pl.multiple_of(lax.rem(at + NZ, NZ) * WIDE, WIDE)
    return mask[:, pl.ds(start, WIDE)].astype(f32)


def put_mask(ref, part):
    ref[:, 0:512] = part[0:32]
    ref[:, 512:1024] = part[32:64]


def take_mask(ref, at):
    return jnp.concatenate(
        [ref[at : at + 32, 0:512], ref[at : at + 32, 512:1024]], axis=0
    ).astype(f32)


def take_spectra(ref, at):
    return jnp.concatenate(
        [ref[at : at + 8, 128 * g : 128 * (g + 1)].astype(f32) for g in range(8)],
        axis=0,
    )


def put_spectra(ref, spectra):
    for g in range(8):
        ref[:, 128 * g : 128 * (g + 1)] = spectra[8 * g : 8 * (g + 1)]


def pack(green, mask, spec_row, near, far, shared, own_mask, own_spec):
    z = lax.axis_index("z")
    row = spec_row[...]
    col = nt(identity(ROWS), row)
    lane = lax.broadcasted_iota(jnp.int32, (ROWS, 128), 1)
    own_spec[...] = jnp.where(
        lane == 0, col[:, 0:1], jnp.where(lane == 1, col[:, 1:2], 0.0)
    )
    own_spec[0:2, 64:128] = row.astype(f32)
    spectra = own_spec[...].astype(bf16)
    for ref in (near, far):
        ref[IMAG : IMAG + ROWS, :] = green[1]
        ref[REAL : REAL + ROWS, :] = green[0]
        put_spectra(ref.at[SPEC : SPEC + 8], spectra)
    for u, ref, at in ((1, near, NEXT), (2, near, MASK), (-3, far, MASK)):
        put_mask(ref.at[at : at + 32], window(mask, z - u).astype(bf16))
    own_mask[...] = window(mask, z).astype(bf16)
    wide = [window(mask, z + u) for u in OFFSETS]
    for q in range(NQ):
        shared[q, 0:64, :] = green[0]
        shared[q, 64:128, :] = green[1]
        put_spectra(shared.at[q, 144:152], spectra)
        part = jnp.concatenate(
            [w[:, ROWS * q : ROWS * (q + 1)] for w in wide], axis=1
        ).astype(bf16)
        for g in range(4):
            shared[q, 128:144, 256 * g : 256 * (g + 1)] = part[16 * g : 16 * (g + 1)]


MOST = 3 * ROWS
WT_RE, WT_IM, NEAR_RE, NEAR_IM, COUNT = (MOST * i for i in range(5))
SPECTRA = COUNT + MOST // 2
BUNDLE = SPECTRA + MOST // 8


def prepare(source, green, own_mask, own_spec, one, two, bundle):
    scale = source[...]
    real, imag = slice(REAL, REAL + ROWS), slice(IMAG, IMAG + ROWS)
    us = [own_spec[...]]
    held = [(green[0], green[1])]
    for ref in (one, two):
        us.append(take_spectra(ref, SPEC))
        held.append((ref[real, :], ref[imag, :]))
    masks = [
        own_mask[...].astype(f32),
        take_mask(one, NEXT),
        take_mask(two, MASK),
    ]
    for k, (re, im) in enumerate(held):
        at = ROWS * k
        bundle[NEAR_RE + at : NEAR_RE + at + ROWS, :] = re
        bundle[NEAR_IM + at : NEAR_IM + at + ROWS, :] = im
        bundle[WT_RE + at : WT_RE + at + ROWS, :] = (scale * re.astype(f32)).astype(bf16)
        bundle[WT_IM + at : WT_IM + at + ROWS, :] = (scale * im.astype(f32)).astype(bf16)
    counts = jnp.concatenate(masks, axis=0).astype(bf16)
    for h in range(2):
        bundle[COUNT : COUNT + MOST // 2, WIDE * h : WIDE * (h + 1)] = counts[
            MOST // 2 * h : MOST // 2 * (h + 1)
        ]
    spectra = jnp.concatenate(us, axis=0)
    for h in range(8):
        bundle[SPECTRA : SPECTRA + MOST // 8, 128 * h : 128 * (h + 1)] = spectra[
            MOST // 8 * h : MOST // 8 * (h + 1)
        ].astype(bf16)


def absorb(shared, source, three, four, bundle, out, far_re, far_im, far_spec, back, wt):
    real, imag = slice(REAL, REAL + ROWS), slice(IMAG, IMAG + ROWS)
    tall = 5 * ROWS
    scale = source[...]
    for at, near, part in ((0, WT_RE, real), (tall, WT_IM, imag)):
        wt[at : at + MOST, :] = bundle[near : near + MOST, :]
        for k, ref in ((3, three), (4, four)):
            wt[at + ROWS * k : at + ROWS * (k + 1), :] = (
                scale * ref[part, :].astype(f32)
            ).astype(bf16)
    spec = jnp.concatenate(
        [
            bundle[SPECTRA : SPECTRA + MOST // 8, 128 * h : 128 * (h + 1)].astype(f32)
            for h in range(8)
        ]
        + [take_spectra(three, SPEC), take_spectra(four, SPEC)],
        axis=0,
    )
    u_re, u_im = spec[:, 0:1], spec[:, 1:2]
    weight = jnp.concatenate(
        [
            bundle[COUNT : COUNT + MOST // 2, WIDE * h : WIDE * (h + 1)].astype(f32)
            for h in range(2)
        ]
        + [take_mask(three, MASK)],
        axis=0,
    )
    for q in range(NQ):
        rows = slice(ROWS * q, ROWS * (q + 1))
        ref = shared.at[q]
        far_re[rows, :] = ref[0:64, :]
        far_im[rows, :] = ref[64:128, :]
        for g in range(4):
            back[ROWS * q + 16 * g : ROWS * q + 16 * (g + 1), :] = ref[
                128:144, 256 * g : 256 * (g + 1)
            ]
        far_spec[0:2, rows] = ref[144:152, 0:128].astype(f32)[0:2, 64:128]
    behind = nt(identity(4 * ROWS), back[...])
    counts = jnp.concatenate(
        [
            weight[0:ROWS],
            weight[ROWS : 4 * ROWS] + behind[0 : 3 * ROWS],
            behind[3 * ROWS : 4 * ROWS],
        ],
        axis=0,
    )
    v_re, v_im = far_spec[0:1, :], far_spec[1:2, :]
    g_re, g_im = far_re[...], far_im[...]
    by_re = nt(wt[...], g_re)
    by_im = nt(wt[...], g_im)
    x_re = (u_re * v_re + u_im * v_im) - (by_re[:tall] + by_im[tall:])
    x_im = (u_im * v_re - u_re * v_im) - (by_re[tall:] - by_im[:tall])
    mis = 0.5 * jnp.sum(counts * (x_re * x_re + x_im * x_im), keepdims=True)
    resid = jnp.concatenate(
        [
            (counts * x_re.astype(bf16).astype(f32)).astype(bf16),
            (counts * x_im.astype(bf16).astype(f32)).astype(bf16),
        ],
        axis=0,
    )
    by_re = nn(resid, g_re)
    by_im = nn(resid, g_im)
    held = []
    for k in range(3):
        at = ROWS * k
        held.append(
            (
                bundle[NEAR_RE + at : NEAR_RE + at + ROWS, :],
                bundle[NEAR_IM + at : NEAR_IM + at + ROWS, :],
            )
        )
    for ref in (three, four):
        held.append((ref[real, :], ref[imag, :]))
    total = jnp.zeros((ROWS, CELLS), f32)
    for k, (re, im) in enumerate(held):
        rows = slice(ROWS * k, ROWS * (k + 1))
        more = slice(tall + ROWS * k, tall + ROWS * (k + 1))
        total = total + (
            re.astype(f32) * (by_re[rows] - by_im[more])
            + im.astype(f32) * (by_im[rows] + by_re[more])
        )
    total = -jnp.sum(total, axis=0, keepdims=True)
    out[:, :, 0:CELLS] = jnp.broadcast_to(total[None], (NZ, 1, CELLS))
    out[:, :, CELLS:LONG] = jnp.broadcast_to(mis[None], (NZ, 1, 128))


def gather_z(parts, out):
    out[...] = jnp.broadcast_to(
        jnp.sum(parts[...], axis=0, keepdims=True), out.shape
    )


def finish(parts, source, new_source, misfit):
    mine = lax.axis_index("xh") * 2 + lax.axis_index("core")
    squares = jnp.zeros((1, CELLS), f32)
    own = jnp.zeros((1, LONG), f32)
    for f in range(NF):
        here = parts[f]
        for q in range(1, NQ):
            here = here + parts[q * NF + f]
        squares = squares + here[:, 0:CELLS] * here[:, 0:CELLS]
        own = jnp.where(mine == f, here, own)
    rms = jnp.sqrt(jnp.sum(squares, keepdims=True) / (NF * CELLS) + 1e-06)
    new_source[...] = source[...] * jnp.exp(-0.5 * own[:, 0:CELLS] / rms)
    stations = NZ * NQ * ROWS
    misfit[0] = jnp.max(own[:, CELLS:LONG]) / (stations * stations)


def shape(dtype, *dims):
    return jax.ShapeDtypeStruct(dims, dtype)


def from_z(array, u):
    return lax.ppermute(array, "z", [(z, (z - u) % NZ) for z in range(NZ)])


def local(spectra, green, source, pair_mask):
    g = green[0]
    vmem = pl.BlockSpec(memory_space=pltpu.VMEM)
    near, far, shared, own_mask, own_spec = pl.pallas_call(
        pack,
        out_shape=[
            shape(bf16, FULL, CELLS),
            shape(bf16, NEXT, CELLS),
            shape(bf16, NQ, SHARED, CELLS),
            shape(bf16, ROWS, WIDE),
            shape(f32, ROWS, 128),
        ],
        in_specs=[vmem] * 3,
        out_specs=[vmem] * 5,
        name="pack",
    )(g, pair_mask, spectra[0])
    three = from_z(from_z(far, -1), -2)
    one = from_z(near, 1)
    shared = lax.all_to_all(shared, PLANE, 0, 0, tiled=True)
    two = from_z(one[:NEXT], 1)
    four = from_z(two[:MASK], 2)
    ready = pl.pallas_call(
        prepare,
        out_shape=shape(bf16, BUNDLE, CELLS),
        in_specs=[vmem] * 6,
        out_specs=vmem,
        cost_estimate=pl.CostEstimate(
            flops=PREPARE, transcendentals=0, bytes_accessed=0
        ),
        name="prepare",
    )(source, g, own_mask, own_spec, one, two)
    part = pl.pallas_call(
        absorb,
        out_shape=shape(f32, NZ, 1, LONG),
        in_specs=[vmem] * 5,
        out_specs=vmem,
        scratch_shapes=[
            pltpu.VMEM((WIDE, CELLS), bf16),
            pltpu.VMEM((WIDE, CELLS), bf16),
            pltpu.VMEM((8, WIDE), f32),
            pltpu.VMEM((WIDE, 4 * ROWS), bf16),
            pltpu.VMEM((10 * ROWS, CELLS), bf16),
        ],
        name="absorb",
        compiler_params=pltpu.CompilerParams(vmem_limit_bytes=40 << 20),
    )(shared, source, three, four, ready)
    part = lax.all_to_all(part, "z", 0, 0, tiled=True)
    part = pl.pallas_call(
        gather_z,
        out_shape=shape(f32, NQ * NF, 1, LONG),
        in_specs=[vmem],
        out_specs=vmem,
        name="gather_z",
        compiler_params=pltpu.CompilerParams(vmem_limit_bytes=8 << 20),
    )(part)
    part = lax.all_to_all(part, PLANE + FREQ, 0, 0, tiled=True)
    return pl.pallas_call(
        finish,
        out_shape=(shape(f32, 1, CELLS), shape(f32, 1)),
        in_specs=[vmem, vmem],
        out_specs=(vmem, pl.BlockSpec(memory_space=pltpu.SMEM)),
        name="finish",
        compiler_params=pltpu.CompilerParams(vmem_limit_bytes=8 << 20),
    )(part, source)


def solution(mesh):
    fine = Mesh(mesh.devices.reshape(NZ, NX, NY, 2, 2), STA + FREQ)
    placed = (P(FREQ, None, STA), P(FREQ, None, STA, None), P(FREQ, None), P(STA, None))
    return jax.shard_map(
        local, mesh=fine, in_specs=placed, out_specs=(P(FREQ, None), P(FREQ)), check_vma=False
    )
```

```python
import jax
import jax.numpy as jnp
from jax import lax
from jax.experimental import pallas as pl
from jax.experimental.pallas import tpu as pltpu
from jax.sharding import Mesh, PartitionSpec as P

NZ, NX, NY = 8, 2, 4
NQ = NX * NY
NF = 4
ROWS = 64
CELLS = 1024
WIDE = NQ * ROWS
PLANE = ("xl", "y")
FREQ = ("xh", "core")
STA = ("z",) + PLANE
OFFSETS = (1, 2, -3, 4)
SHARED = 152
LONG = CELLS + 128
f32, bf16 = jnp.float32, jnp.bfloat16


def nt(a, b):
    return lax.dot_general(
        a, b, (((1,), (1,)), ((), ())), preferred_element_type=f32
    )


def nn(a, b):
    return lax.dot_general(
        a, b, (((1,), (0,)), ((), ())), preferred_element_type=f32
    )


def identity(n):
    down = lax.broadcasted_iota(jnp.int32, (n, n), 0)
    across = lax.broadcasted_iota(jnp.int32, (n, n), 1)
    return (down == across).astype(f32).astype(bf16)


SPEC, IMAG, REAL, MASK, NEXT, FULL = 0, 8, 72, 136, 168, 200
PREPARE = 17_500_000_000


def window(mask, at):
    start = pl.multiple_of(lax.rem(at + NZ, NZ) * WIDE, WIDE)
    return mask[:, pl.ds(start, WIDE)].astype(f32)


def put_mask(ref, part):
    ref[:, 0:512] = part[0:32]
    ref[:, 512:1024] = part[32:64]


def take_mask(ref, at):
    return jnp.concatenate(
        [ref[at : at + 32, 0:512], ref[at : at + 32, 512:1024]], axis=0
    ).astype(f32)


def take_spectra(ref, at):
    return jnp.concatenate(
        [ref[at : at + 8, 128 * g : 128 * (g + 1)].astype(f32) for g in range(8)],
        axis=0,
    )


def put_spectra(ref, spectra):
    for g in range(8):
        ref[:, 128 * g : 128 * (g + 1)] = spectra[8 * g : 8 * (g + 1)]


def pack(green, mask, spec_row, near, far, shared, own_mask, own_spec):
    z = lax.axis_index("z")
    row = spec_row[...]
    col = nt(identity(ROWS), row)
    lane = lax.broadcasted_iota(jnp.int32, (ROWS, 128), 1)
    own_spec[...] = jnp.where(
        lane == 0, col[:, 0:1], jnp.where(lane == 1, col[:, 1:2], 0.0)
    )
    own_spec[0:2, 64:128] = row.astype(f32)
    spectra = own_spec[...].astype(bf16)
    for ref in (near, far):
        ref[IMAG : IMAG + ROWS, :] = green[1]
        ref[REAL : REAL + ROWS, :] = green[0]
        put_spectra(ref.at[SPEC : SPEC + 8], spectra)
    for u, ref, at in ((1, near, NEXT), (2, near, MASK), (-3, far, MASK)):
        put_mask(ref.at[at : at + 32], window(mask, z - u).astype(bf16))
    own_mask[...] = window(mask, z).astype(bf16)
    wide = [window(mask, z + u) for u in OFFSETS]
    for q in range(NQ):
        shared[q, 0:64, :] = green[0]
        shared[q, 64:128, :] = green[1]
        put_spectra(shared.at[q, 144:152], spectra)
        part = jnp.concatenate(
            [w[:, ROWS * q : ROWS * (q + 1)] for w in wide], axis=1
        ).astype(bf16)
        for g in range(4):
            shared[q, 128:144, 256 * g : 256 * (g + 1)] = part[16 * g : 16 * (g + 1)]


MOST = 3 * ROWS
NEAR_RE, NEAR_IM, COUNT = 0, 2 * ROWS, 4 * ROWS
SPECTRA = COUNT + MOST // 2
BUNDLE = SPECTRA + MOST // 8


def prepare(own_mask, own_spec, one, two, bundle):
    us = [own_spec[...]]
    for k, ref in enumerate((one, two)):
        us.append(take_spectra(ref, SPEC))
        at = ROWS * k
        bundle[NEAR_RE + at : NEAR_RE + at + ROWS, :] = ref[REAL : REAL + ROWS, :]
        bundle[NEAR_IM + at : NEAR_IM + at + ROWS, :] = ref[IMAG : IMAG + ROWS, :]
    masks = [own_mask[...].astype(f32), take_mask(one, NEXT), take_mask(two, MASK)]
    counts = jnp.concatenate(masks, axis=0).astype(bf16)
    for h in range(2):
        bundle[COUNT : COUNT + MOST // 2, WIDE * h : WIDE * (h + 1)] = counts[
            MOST // 2 * h : MOST // 2 * (h + 1)
        ]
    spectra = jnp.concatenate(us, axis=0)
    for h in range(8):
        bundle[SPECTRA : SPECTRA + MOST // 8, 128 * h : 128 * (h + 1)] = spectra[
            MOST // 8 * h : MOST // 8 * (h + 1)
        ].astype(bf16)


def absorb(shared, source, green, three, four, bundle, out, far_re, far_im, far_spec, back, wt):
    real, imag = slice(REAL, REAL + ROWS), slice(IMAG, IMAG + ROWS)
    tall = 5 * ROWS
    scale = source[...]
    held = [(green[0], green[1])]
    for k in range(2):
        re, im = NEAR_RE + ROWS * k, NEAR_IM + ROWS * k
        held.append((bundle[re : re + ROWS, :], bundle[im : im + ROWS, :]))
    for ref in (three, four):
        held.append((ref[real, :], ref[imag, :]))
    for k, (re, im) in enumerate(held):
        at = ROWS * k
        wt[at : at + ROWS, :] = (scale * re.astype(f32)).astype(bf16)
        wt[tall + at : tall + at + ROWS, :] = (scale * im.astype(f32)).astype(bf16)
    spec = jnp.concatenate(
        [
            bundle[SPECTRA : SPECTRA + MOST // 8, 128 * h : 128 * (h + 1)].astype(f32)
            for h in range(8)
        ]
        + [take_spectra(three, SPEC), take_spectra(four, SPEC)],
        axis=0,
    )
    u_re, u_im = spec[:, 0:1], spec[:, 1:2]
    weight = jnp.concatenate(
        [
            bundle[COUNT : COUNT + MOST // 2, WIDE * h : WIDE * (h + 1)].astype(f32)
            for h in range(2)
        ]
        + [take_mask(three, MASK)],
        axis=0,
    )
    for q in range(NQ):
        rows = slice(ROWS * q, ROWS * (q + 1))
        ref = shared.at[q]
        far_re[rows, :] = ref[0:64, :]
        far_im[rows, :] = ref[64:128, :]
        for g in range(4):
            back[ROWS * q + 16 * g : ROWS * q + 16 * (g + 1), :] = ref[
                128:144, 256 * g : 256 * (g + 1)
            ]
        far_spec[0:2, rows] = ref[144:152, 0:128].astype(f32)[0:2, 64:128]
    behind = nt(identity(4 * ROWS), back[...])
    counts = jnp.concatenate(
        [
            weight[0:ROWS],
            weight[ROWS : 4 * ROWS] + behind[0 : 3 * ROWS],
            behind[3 * ROWS : 4 * ROWS],
        ],
        axis=0,
    )
    v_re, v_im = far_spec[0:1, :], far_spec[1:2, :]
    g_re, g_im = far_re[...], far_im[...]
    by_re = nt(wt[...], g_re)
    by_im = nt(wt[...], g_im)
    x_re = (u_re * v_re + u_im * v_im) - (by_re[:tall] + by_im[tall:])
    x_im = (u_im * v_re - u_re * v_im) - (by_re[tall:] - by_im[:tall])
    mis = 0.5 * jnp.sum(counts * (x_re * x_re + x_im * x_im), keepdims=True)
    resid = jnp.concatenate(
        [
            (counts * x_re.astype(bf16).astype(f32)).astype(bf16),
            (counts * x_im.astype(bf16).astype(f32)).astype(bf16),
        ],
        axis=0,
    )
    by_re = nn(resid, g_re)
    by_im = nn(resid, g_im)
    total = jnp.zeros((ROWS, CELLS), f32)
    for k, (re, im) in enumerate(held):
        rows = slice(ROWS * k, ROWS * (k + 1))
        more = slice(tall + ROWS * k, tall + ROWS * (k + 1))
        total = total + (
            re.astype(f32) * (by_re[rows] - by_im[more])
            + im.astype(f32) * (by_im[rows] + by_re[more])
        )
    total = -jnp.sum(total, axis=0, keepdims=True)
    out[:, :, 0:CELLS] = jnp.broadcast_to(total[None], (NZ, 1, CELLS))
    out[:, :, CELLS:LONG] = jnp.broadcast_to(mis[None], (NZ, 1, 128))


def gather_z(parts, out):
    out[...] = jnp.broadcast_to(
        jnp.sum(parts[...], axis=0, keepdims=True), out.shape
    )


def finish(parts, source, new_source, misfit):
    mine = lax.axis_index("xh") * 2 + lax.axis_index("core")
    squares = jnp.zeros((1, CELLS), f32)
    own = jnp.zeros((1, LONG), f32)
    for f in range(NF):
        here = parts[f]
        for q in range(1, NQ):
            here = here + parts[q * NF + f]
        squares = squares + here[:, 0:CELLS] * here[:, 0:CELLS]
        own = jnp.where(mine == f, here, own)
    rms = jnp.sqrt(jnp.sum(squares, keepdims=True) / (NF * CELLS) + 1e-06)
    new_source[...] = source[...] * jnp.exp(-0.5 * own[:, 0:CELLS] / rms)
    stations = NZ * NQ * ROWS
    misfit[0] = jnp.max(own[:, CELLS:LONG]) / (stations * stations)


def shape(dtype, *dims):
    return jax.ShapeDtypeStruct(dims, dtype)


def from_z(array, u):
    return lax.ppermute(array, "z", [(z, (z - u) % NZ) for z in range(NZ)])


def local(spectra, green, source, pair_mask):
    g = green[0]
    vmem = pl.BlockSpec(memory_space=pltpu.VMEM)
    near, far, shared, own_mask, own_spec = pl.pallas_call(
        pack,
        out_shape=[
            shape(bf16, FULL, CELLS),
            shape(bf16, NEXT, CELLS),
            shape(bf16, NQ, SHARED, CELLS),
            shape(bf16, ROWS, WIDE),
            shape(f32, ROWS, 128),
        ],
        in_specs=[vmem] * 3,
        out_specs=[vmem] * 5,
        name="pack",
    )(g, pair_mask, spectra[0])
    three = from_z(from_z(far, -1), -2)
    one = from_z(near, 1)
    shared = lax.all_to_all(shared, PLANE, 0, 0, tiled=True)
    two = from_z(one[:NEXT], 1)
    four = from_z(two[:MASK], 2)
    ready = pl.pallas_call(
        prepare,
        out_shape=shape(bf16, BUNDLE, CELLS),
        in_specs=[vmem] * 4,
        out_specs=vmem,
        cost_estimate=pl.CostEstimate(
            flops=PREPARE, transcendentals=0, bytes_accessed=0
        ),
        name="prepare",
    )(own_mask, own_spec, one, two)
    part = pl.pallas_call(
        absorb,
        out_shape=shape(f32, NZ, 1, LONG),
        in_specs=[vmem] * 6,
        out_specs=vmem,
        scratch_shapes=[
            pltpu.VMEM((WIDE, CELLS), bf16),
            pltpu.VMEM((WIDE, CELLS), bf16),
            pltpu.VMEM((8, WIDE), f32),
            pltpu.VMEM((WIDE, 4 * ROWS), bf16),
            pltpu.VMEM((10 * ROWS, CELLS), bf16),
        ],
        name="absorb",
        compiler_params=pltpu.CompilerParams(vmem_limit_bytes=40 << 20),
    )(shared, source, g, three, four, ready)
    part = lax.all_to_all(part, "z", 0, 0, tiled=True)
    part = pl.pallas_call(
        gather_z,
        out_shape=shape(f32, NQ * NF, 1, LONG),
        in_specs=[vmem],
        out_specs=vmem,
        name="gather_z",
        compiler_params=pltpu.CompilerParams(vmem_limit_bytes=8 << 20),
    )(part)
    part = lax.all_to_all(part, PLANE + FREQ, 0, 0, tiled=True)
    return pl.pallas_call(
        finish,
        out_shape=(shape(f32, 1, CELLS), shape(f32, 1)),
        in_specs=[vmem, vmem],
        out_specs=(vmem, pl.BlockSpec(memory_space=pltpu.SMEM)),
        name="finish",
        compiler_params=pltpu.CompilerParams(vmem_limit_bytes=8 << 20),
    )(part, source)


def solution(mesh):
    fine = Mesh(mesh.devices.reshape(NZ, NX, NY, 2, 2), STA + FREQ)
    placed = (P(FREQ, None, STA), P(FREQ, None, STA, None), P(FREQ, None), P(STA, None))
    return jax.shard_map(
        local, mesh=fine, in_specs=placed, out_specs=(P(FREQ, None), P(FREQ)), check_vma=False
    )
```

```python
import jax
import jax.numpy as jnp
from jax import lax
from jax.experimental import pallas as pl
from jax.experimental.pallas import tpu as pltpu
from jax.sharding import Mesh, PartitionSpec as P

NZ, NX, NY = 8, 2, 4
NQ = NX * NY
NF = 4
ROWS = 64
CELLS = 1024
WIDE = NQ * ROWS
PLANE = ("xl", "y")
FREQ = ("xh", "core")
STA = ("z",) + PLANE
OFFSETS = (1, 2, -3, 4)
SHARED = 152
LONG = CELLS + 128
f32, bf16 = jnp.float32, jnp.bfloat16


def nt(a, b):
    return lax.dot_general(
        a, b, (((1,), (1,)), ((), ())), preferred_element_type=f32
    )


def nn(a, b):
    return lax.dot_general(
        a, b, (((1,), (0,)), ((), ())), preferred_element_type=f32
    )


def identity(n):
    down = lax.broadcasted_iota(jnp.int32, (n, n), 0)
    across = lax.broadcasted_iota(jnp.int32, (n, n), 1)
    return (down == across).astype(f32).astype(bf16)


SPEC, IMAG, REAL, MASK, NEXT, FULL = 0, 8, 72, 136, 168, 200
PREPARE = 17_500_000_000


def window(mask, at):
    start = pl.multiple_of(lax.rem(at + NZ, NZ) * WIDE, WIDE)
    return mask[:, pl.ds(start, WIDE)].astype(f32)


def put_mask(ref, part):
    ref[:, 0:512] = part[0:32]
    ref[:, 512:1024] = part[32:64]


def take_mask(ref, at):
    return jnp.concatenate(
        [ref[at : at + 32, 0:512], ref[at : at + 32, 512:1024]], axis=0
    ).astype(f32)


def take_spectra(ref, at):
    return jnp.concatenate(
        [ref[at : at + 8, 128 * g : 128 * (g + 1)].astype(f32) for g in range(8)],
        axis=0,
    )


def put_spectra(ref, spectra):
    for g in range(8):
        ref[:, 128 * g : 128 * (g + 1)] = spectra[8 * g : 8 * (g + 1)]


def pack(green, mask, spec_row, near, far, shared, own_mask, own_spec):
    z = lax.axis_index("z")
    row = spec_row[...]
    col = nt(identity(ROWS), row)
    lane = lax.broadcasted_iota(jnp.int32, (ROWS, 128), 1)
    own_spec[...] = jnp.where(
        lane == 0, col[:, 0:1], jnp.where(lane == 1, col[:, 1:2], 0.0)
    )
    own_spec[0:2, 64:128] = row.astype(f32)
    spectra = own_spec[...].astype(bf16)
    for ref in (near, far):
        ref[IMAG : IMAG + ROWS, :] = green[1]
        ref[REAL : REAL + ROWS, :] = green[0]
        put_spectra(ref.at[SPEC : SPEC + 8], spectra)
    for u, ref, at in ((1, near, NEXT), (2, near, MASK), (-3, far, MASK)):
        put_mask(ref.at[at : at + 32], window(mask, z - u).astype(bf16))
    own_mask[...] = window(mask, z).astype(bf16)
    wide = [window(mask, z + u) for u in OFFSETS]
    for q in range(NQ):
        shared[q, 0:64, :] = green[0]
        shared[q, 64:128, :] = green[1]
        put_spectra(shared.at[q, 144:152], spectra)
        part = jnp.concatenate(
            [w[:, ROWS * q : ROWS * (q + 1)] for w in wide], axis=1
        ).astype(bf16)
        for g in range(4):
            shared[q, 128:144, 256 * g : 256 * (g + 1)] = part[16 * g : 16 * (g + 1)]


MOST = 3 * ROWS
NEAR_RE, NEAR_IM, COUNT = 0, 2 * ROWS, 4 * ROWS
SPECTRA = COUNT + MOST // 2
BUNDLE = SPECTRA + MOST // 8


def prepare(own_mask, own_spec, one, two, bundle):
    us = [own_spec[...]]
    for k, ref in enumerate((one, two)):
        us.append(take_spectra(ref, SPEC))
        at = ROWS * k
        bundle[NEAR_RE + at : NEAR_RE + at + ROWS, :] = ref[REAL : REAL + ROWS, :]
        bundle[NEAR_IM + at : NEAR_IM + at + ROWS, :] = ref[IMAG : IMAG + ROWS, :]
    masks = [own_mask[...].astype(f32), take_mask(one, NEXT), take_mask(two, MASK)]
    counts = jnp.concatenate(masks, axis=0).astype(bf16)
    for h in range(2):
        bundle[COUNT : COUNT + MOST // 2, WIDE * h : WIDE * (h + 1)] = counts[
            MOST // 2 * h : MOST // 2 * (h + 1)
        ]
    spectra = jnp.concatenate(us, axis=0)
    for h in range(8):
        bundle[SPECTRA : SPECTRA + MOST // 8, 128 * h : 128 * (h + 1)] = spectra[
            MOST // 8 * h : MOST // 8 * (h + 1)
        ].astype(bf16)


def absorb(shared, source, green, three, four, bundle, out, far_re, far_im, far_spec, back, wt):
    real, imag = slice(REAL, REAL + ROWS), slice(IMAG, IMAG + ROWS)
    tall = 5 * ROWS
    scale = source[...]
    held = [(green[0], green[1])]
    for k in range(2):
        re, im = NEAR_RE + ROWS * k, NEAR_IM + ROWS * k
        held.append((bundle[re : re + ROWS, :], bundle[im : im + ROWS, :]))
    for ref in (three, four):
        held.append((ref[real, :], ref[imag, :]))
    for k, (re, im) in enumerate(held):
        at = ROWS * k
        wt[at : at + ROWS, :] = (scale * re.astype(f32)).astype(bf16)
        wt[tall + at : tall + at + ROWS, :] = (scale * im.astype(f32)).astype(bf16)
    spec = jnp.concatenate(
        [
            bundle[SPECTRA : SPECTRA + MOST // 8, 128 * h : 128 * (h + 1)].astype(f32)
            for h in range(8)
        ]
        + [take_spectra(three, SPEC), take_spectra(four, SPEC)],
        axis=0,
    )
    u_re, u_im = spec[:, 0:1], spec[:, 1:2]
    weight = jnp.concatenate(
        [
            bundle[COUNT : COUNT + MOST // 2, WIDE * h : WIDE * (h + 1)].astype(f32)
            for h in range(2)
        ]
        + [take_mask(three, MASK)],
        axis=0,
    )
    for q in range(NQ):
        rows = slice(ROWS * q, ROWS * (q + 1))
        ref = shared.at[q]
        far_re[rows, :] = ref[0:64, :]
        far_im[rows, :] = ref[64:128, :]
        for g in range(4):
            back[ROWS * q + 16 * g : ROWS * q + 16 * (g + 1), :] = ref[
                128:144, 256 * g : 256 * (g + 1)
            ]
        far_spec[0:2, rows] = ref[144:152, 0:128].astype(f32)[0:2, 64:128]
    behind = nt(identity(4 * ROWS), back[...])
    counts = jnp.concatenate(
        [
            weight[0:ROWS],
            weight[ROWS : 4 * ROWS] + behind[0 : 3 * ROWS],
            behind[3 * ROWS : 4 * ROWS],
        ],
        axis=0,
    )
    v_re, v_im = far_spec[0:1, :], far_spec[1:2, :]
    g_re, g_im = far_re[...], far_im[...]
    by_re = nt(wt[...], g_re)
    by_im = nt(wt[...], g_im)
    x_re = (u_re * v_re + u_im * v_im) - (by_re[:tall] + by_im[tall:])
    x_im = (u_im * v_re - u_re * v_im) - (by_re[tall:] - by_im[:tall])
    mis = 0.5 * jnp.sum(counts * (x_re * x_re + x_im * x_im), keepdims=True)
    resid = jnp.concatenate(
        [
            (counts * x_re.astype(bf16).astype(f32)).astype(bf16),
            (counts * x_im.astype(bf16).astype(f32)).astype(bf16),
        ],
        axis=0,
    )
    by_re = nn(resid, g_re)
    by_im = nn(resid, g_im)
    total = jnp.zeros((ROWS, CELLS), f32)
    for k, (re, im) in enumerate(held):
        rows = slice(ROWS * k, ROWS * (k + 1))
        more = slice(tall + ROWS * k, tall + ROWS * (k + 1))
        total = total + (
            re.astype(f32) * (by_re[rows] - by_im[more])
            + im.astype(f32) * (by_im[rows] + by_re[more])
        )
    total = -jnp.sum(total, axis=0, keepdims=True)
    out[:, :, 0:CELLS] = jnp.broadcast_to(total[None], (NZ * NY, 1, CELLS))
    out[:, :, CELLS:LONG] = jnp.broadcast_to(mis[None], (NZ * NY, 1, 128))


def gather_zy(parts, out):
    out[...] = jnp.broadcast_to(
        jnp.sum(parts[...], axis=0, keepdims=True), out.shape
    )


def finish(parts, source, new_source, misfit):
    mine = lax.axis_index("xh") * 2 + lax.axis_index("core")
    squares = jnp.zeros((1, CELLS), f32)
    own = jnp.zeros((1, LONG), f32)
    for f in range(NF):
        here = parts[f]
        for x in range(1, NX):
            here = here + parts[x * NF + f]
        squares = squares + here[:, 0:CELLS] * here[:, 0:CELLS]
        own = jnp.where(mine == f, here, own)
    rms = jnp.sqrt(jnp.sum(squares, keepdims=True) / (NF * CELLS) + 1e-06)
    new_source[...] = source[...] * jnp.exp(-0.5 * own[:, 0:CELLS] / rms)
    stations = NZ * NQ * ROWS
    misfit[0] = jnp.max(own[:, CELLS:LONG]) / (stations * stations)


def shape(dtype, *dims):
    return jax.ShapeDtypeStruct(dims, dtype)


def from_z(array, u):
    return lax.ppermute(array, "z", [(z, (z - u) % NZ) for z in range(NZ)])


def local(spectra, green, source, pair_mask):
    g = green[0]
    vmem = pl.BlockSpec(memory_space=pltpu.VMEM)
    near, far, shared, own_mask, own_spec = pl.pallas_call(
        pack,
        out_shape=[
            shape(bf16, FULL, CELLS),
            shape(bf16, NEXT, CELLS),
            shape(bf16, NQ, SHARED, CELLS),
            shape(bf16, ROWS, WIDE),
            shape(f32, ROWS, 128),
        ],
        in_specs=[vmem] * 3,
        out_specs=[vmem] * 5,
        name="pack",
    )(g, pair_mask, spectra[0])
    three = from_z(from_z(far, -1), -2)
    one = from_z(near, 1)
    shared = lax.all_to_all(shared, PLANE, 0, 0, tiled=True)
    two = from_z(one[:NEXT], 1)
    four = from_z(two[:MASK], 2)
    ready = pl.pallas_call(
        prepare,
        out_shape=shape(bf16, BUNDLE, CELLS),
        in_specs=[vmem] * 4,
        out_specs=vmem,
        cost_estimate=pl.CostEstimate(
            flops=PREPARE, transcendentals=0, bytes_accessed=0
        ),
        name="prepare",
    )(own_mask, own_spec, one, two)
    part = pl.pallas_call(
        absorb,
        out_shape=shape(f32, NZ * NY, 1, LONG),
        in_specs=[vmem] * 6,
        out_specs=vmem,
        scratch_shapes=[
            pltpu.VMEM((WIDE, CELLS), bf16),
            pltpu.VMEM((WIDE, CELLS), bf16),
            pltpu.VMEM((8, WIDE), f32),
            pltpu.VMEM((WIDE, 4 * ROWS), bf16),
            pltpu.VMEM((10 * ROWS, CELLS), bf16),
        ],
        name="absorb",
        compiler_params=pltpu.CompilerParams(vmem_limit_bytes=40 << 20),
    )(shared, source, g, three, four, ready)
    part = lax.all_to_all(part, ("z", "y"), 0, 0, tiled=True)
    part = pl.pallas_call(
        gather_zy,
        out_shape=shape(f32, NX * NF, 1, LONG),
        in_specs=[vmem],
        out_specs=vmem,
        name="gather_zy",
        compiler_params=pltpu.CompilerParams(vmem_limit_bytes=8 << 20),
    )(part)
    part = lax.all_to_all(part, ("xl",) + FREQ, 0, 0, tiled=True)
    return pl.pallas_call(
        finish,
        out_shape=(shape(f32, 1, CELLS), shape(f32, 1)),
        in_specs=[vmem, vmem],
        out_specs=(vmem, pl.BlockSpec(memory_space=pltpu.SMEM)),
        name="finish",
        compiler_params=pltpu.CompilerParams(vmem_limit_bytes=8 << 20),
    )(part, source)


def solution(mesh):
    fine = Mesh(mesh.devices.reshape(NZ, NX, NY, 2, 2), STA + FREQ)
    placed = (P(FREQ, None, STA), P(FREQ, None, STA, None), P(FREQ, None), P(STA, None))
    return jax.shard_map(
        local, mesh=fine, in_specs=placed, out_specs=(P(FREQ, None), P(FREQ)), check_vma=False
    )
```

```python
import jax
import jax.numpy as jnp
from jax import lax
from jax.experimental import pallas as pl
from jax.experimental.pallas import tpu as pltpu
from jax.sharding import Mesh, PartitionSpec as P

NZ, NX, NY = 8, 2, 4
NQ = NX * NY
NF = 4
ROWS = 64
CELLS = 1024
WIDE = NQ * ROWS
PLANE = ("xl", "y")
FREQ = ("xh", "core")
STA = ("z",) + PLANE
OFFSETS = (1, 2, -3)
SHARED = 144
LONG = CELLS + 128
f32, bf16 = jnp.float32, jnp.bfloat16


def nt(a, b):
    return lax.dot_general(
        a, b, (((1,), (1,)), ((), ())), preferred_element_type=f32
    )


def nn(a, b):
    return lax.dot_general(
        a, b, (((1,), (0,)), ((), ())), preferred_element_type=f32
    )


def identity(n):
    down = lax.broadcasted_iota(jnp.int32, (n, n), 0)
    across = lax.broadcasted_iota(jnp.int32, (n, n), 1)
    return (down == across).astype(f32).astype(bf16)


SPEC, IMAG, REAL, MASK, NEXT, FULL = 0, 8, 72, 136, 168, 200
PREPARE = 17_500_000_000


def window(mask, at):
    start = pl.multiple_of(lax.rem(at + NZ, NZ) * WIDE, WIDE)
    return mask[:, pl.ds(start, WIDE)].astype(f32)


def put_mask(ref, part):
    ref[:, 0:512] = part[0:32]
    ref[:, 512:1024] = part[32:64]


def take_mask(ref, at):
    return jnp.concatenate(
        [ref[at : at + 32, 0:512], ref[at : at + 32, 512:1024]], axis=0
    ).astype(f32)


def take_spectra(ref, at):
    return jnp.concatenate(
        [ref[at : at + 8, 128 * g : 128 * (g + 1)].astype(f32) for g in range(8)],
        axis=0,
    )


def put_spectra(ref, spectra):
    for g in range(8):
        ref[:, 128 * g : 128 * (g + 1)] = spectra[8 * g : 8 * (g + 1)]


def pack(green, mask, spec_row, near, far, last, shared, own_mask, own_spec):
    z = lax.axis_index("z")
    row = spec_row[...]
    col = nt(identity(ROWS), row)
    lane = lax.broadcasted_iota(jnp.int32, (ROWS, 128), 1)
    own_spec[...] = jnp.where(
        lane == 0, col[:, 0:1], jnp.where(lane == 1, col[:, 1:2], 0.0)
    )
    own_spec[0:2, 64:128] = row.astype(f32)
    spectra = own_spec[...].astype(bf16)
    for ref in (near, far):
        ref[IMAG : IMAG + ROWS, :] = green[1]
        ref[REAL : REAL + ROWS, :] = green[0]
        put_spectra(ref.at[SPEC : SPEC + 8], spectra)
    for u, ref, at in ((1, near, NEXT), (2, near, MASK), (-3, far, MASK)):
        put_mask(ref.at[at : at + 32], window(mask, z - u).astype(bf16))
    put_mask(last, window(mask, z - 4).astype(bf16))
    own_mask[...] = window(mask, z).astype(bf16)
    wide = [window(mask, z + u) for u in OFFSETS]
    rows = own_spec[:, 64:128]
    for q in range(NQ):
        shared[q, 0:64, :] = green[0]
        shared[q, 64:128, :] = green[1]
        part = jnp.concatenate(
            [w[:, ROWS * q : ROWS * (q + 1)] for w in wide] + [rows], axis=1
        ).astype(bf16)
        for g in range(4):
            shared[q, 128:144, 256 * g : 256 * (g + 1)] = part[16 * g : 16 * (g + 1)]


MOST = 3 * ROWS
NEAR_RE, NEAR_IM, COUNT = 0, 2 * ROWS, 4 * ROWS
SPECTRA = COUNT + MOST // 2
BUNDLE = SPECTRA + MOST // 8


def prepare(own_mask, own_spec, one, two, bundle):
    us = [own_spec[...]]
    for k, ref in enumerate((one, two)):
        us.append(take_spectra(ref, SPEC))
        at = ROWS * k
        bundle[NEAR_RE + at : NEAR_RE + at + ROWS, :] = ref[REAL : REAL + ROWS, :]
        bundle[NEAR_IM + at : NEAR_IM + at + ROWS, :] = ref[IMAG : IMAG + ROWS, :]
    masks = [own_mask[...].astype(f32), take_mask(one, NEXT), take_mask(two, MASK)]
    counts = jnp.concatenate(masks, axis=0).astype(bf16)
    for h in range(2):
        bundle[COUNT : COUNT + MOST // 2, WIDE * h : WIDE * (h + 1)] = counts[
            MOST // 2 * h : MOST // 2 * (h + 1)
        ]
    spectra = jnp.concatenate(us, axis=0)
    for h in range(8):
        bundle[SPECTRA : SPECTRA + MOST // 8, 128 * h : 128 * (h + 1)] = spectra[
            MOST // 8 * h : MOST // 8 * (h + 1)
        ].astype(bf16)


def absorb(shared, source, green, three, four, last, bundle, out, far_re, far_im, far_spec, back, wt):
    real, imag = slice(REAL, REAL + ROWS), slice(IMAG, IMAG + ROWS)
    tall = 5 * ROWS
    scale = source[...]
    held = [(green[0], green[1])]
    for k in range(2):
        re, im = NEAR_RE + ROWS * k, NEAR_IM + ROWS * k
        held.append((bundle[re : re + ROWS, :], bundle[im : im + ROWS, :]))
    for ref in (three, four):
        held.append((ref[real, :], ref[imag, :]))
    for k, (re, im) in enumerate(held):
        at = ROWS * k
        wt[at : at + ROWS, :] = (scale * re.astype(f32)).astype(bf16)
        wt[tall + at : tall + at + ROWS, :] = (scale * im.astype(f32)).astype(bf16)
    spec = jnp.concatenate(
        [
            bundle[SPECTRA : SPECTRA + MOST // 8, 128 * h : 128 * (h + 1)].astype(f32)
            for h in range(8)
        ]
        + [take_spectra(three, SPEC), take_spectra(four, SPEC)],
        axis=0,
    )
    u_re, u_im = spec[:, 0:1], spec[:, 1:2]
    weight = jnp.concatenate(
        [
            bundle[COUNT : COUNT + MOST // 2, WIDE * h : WIDE * (h + 1)].astype(f32)
            for h in range(2)
        ]
        + [take_mask(three, MASK)],
        axis=0,
    )
    for q in range(NQ):
        rows = slice(ROWS * q, ROWS * (q + 1))
        ref = shared.at[q]
        far_re[rows, :] = ref[0:64, :]
        far_im[rows, :] = ref[64:128, :]
        for g in range(4):
            back[ROWS * q + 16 * g : ROWS * q + 16 * (g + 1), :] = ref[
                128:144, 256 * g : 256 * (g + 1)
            ]
        far_spec[0:2, rows] = ref[128:144, 128:256].astype(f32)[0:2, 64:128]
    behind = nt(identity(4 * ROWS), back[...])
    counts = jnp.concatenate(
        [
            weight[0:ROWS],
            weight[ROWS : 4 * ROWS] + behind[0 : 3 * ROWS],
            take_mask(last, 0),
        ],
        axis=0,
    )
    v_re, v_im = far_spec[0:1, :], far_spec[1:2, :]
    g_re, g_im = far_re[...], far_im[...]
    by_re = nt(wt[...], g_re)
    by_im = nt(wt[...], g_im)
    x_re = (u_re * v_re + u_im * v_im) - (by_re[:tall] + by_im[tall:])
    x_im = (u_im * v_re - u_re * v_im) - (by_re[tall:] - by_im[:tall])
    mis = 0.5 * jnp.sum(counts * (x_re * x_re + x_im * x_im), keepdims=True)
    resid = jnp.concatenate(
        [
            (counts * x_re.astype(bf16).astype(f32)).astype(bf16),
            (counts * x_im.astype(bf16).astype(f32)).astype(bf16),
        ],
        axis=0,
    )
    by_re = nn(resid, g_re)
    by_im = nn(resid, g_im)
    total = jnp.zeros((ROWS, CELLS), f32)
    for k, (re, im) in enumerate(held):
        rows = slice(ROWS * k, ROWS * (k + 1))
        more = slice(tall + ROWS * k, tall + ROWS * (k + 1))
        total = total + (
            re.astype(f32) * (by_re[rows] - by_im[more])
            + im.astype(f32) * (by_im[rows] + by_re[more])
        )
    total = -jnp.sum(total, axis=0, keepdims=True)
    out[:, :, 0:CELLS] = jnp.broadcast_to(total[None], (NZ, 1, CELLS))
    out[:, :, CELLS:LONG] = jnp.broadcast_to(mis[None], (NZ, 1, 128))


def gather_z(parts, out):
    out[...] = jnp.broadcast_to(
        jnp.sum(parts[...], axis=0, keepdims=True), out.shape
    )


def finish(parts, source, new_source, misfit):
    mine = lax.axis_index("xh") * 2 + lax.axis_index("core")
    squares = jnp.zeros((1, CELLS), f32)
    own = jnp.zeros((1, LONG), f32)
    for f in range(NF):
        here = parts[f]
        for q in range(1, NQ):
            here = here + parts[q * NF + f]
        squares = squares + here[:, 0:CELLS] * here[:, 0:CELLS]
        own = jnp.where(mine == f, here, own)
    rms = jnp.sqrt(jnp.sum(squares, keepdims=True) / (NF * CELLS) + 1e-06)
    new_source[...] = source[...] * jnp.exp(-0.5 * own[:, 0:CELLS] / rms)
    stations = NZ * NQ * ROWS
    misfit[0] = jnp.max(own[:, CELLS:LONG]) / (stations * stations)


def shape(dtype, *dims):
    return jax.ShapeDtypeStruct(dims, dtype)


def from_z(array, u):
    return lax.ppermute(array, "z", [(z, (z - u) % NZ) for z in range(NZ)])


def local(spectra, green, source, pair_mask):
    g = green[0]
    vmem = pl.BlockSpec(memory_space=pltpu.VMEM)
    near, far, last, shared, own_mask, own_spec = pl.pallas_call(
        pack,
        out_shape=[
            shape(bf16, FULL, CELLS),
            shape(bf16, NEXT, CELLS),
            shape(bf16, 32, CELLS),
            shape(bf16, NQ, SHARED, CELLS),
            shape(bf16, ROWS, WIDE),
            shape(f32, ROWS, 128),
        ],
        in_specs=[vmem] * 3,
        out_specs=[vmem] * 6,
        name="pack",
    )(g, pair_mask, spectra[0])
    three = from_z(from_z(far, -1), -2)
    one = from_z(near, 1)
    shared = lax.all_to_all(shared, PLANE, 0, 0, tiled=True)
    two = from_z(one[:NEXT], 1)
    four = from_z(two[:MASK], 2)
    last = from_z(last, 4)
    ready = pl.pallas_call(
        prepare,
        out_shape=shape(bf16, BUNDLE, CELLS),
        in_specs=[vmem] * 4,
        out_specs=vmem,
        cost_estimate=pl.CostEstimate(
            flops=PREPARE, transcendentals=0, bytes_accessed=0
        ),
        name="prepare",
    )(own_mask, own_spec, one, two)
    part = pl.pallas_call(
        absorb,
        out_shape=shape(f32, NZ, 1, LONG),
        in_specs=[vmem] * 7,
        out_specs=vmem,
        scratch_shapes=[
            pltpu.VMEM((WIDE, CELLS), bf16),
            pltpu.VMEM((WIDE, CELLS), bf16),
            pltpu.VMEM((8, WIDE), f32),
            pltpu.VMEM((WIDE, 4 * ROWS), bf16),
            pltpu.VMEM((10 * ROWS, CELLS), bf16),
        ],
        name="absorb",
        compiler_params=pltpu.CompilerParams(vmem_limit_bytes=40 << 20),
    )(shared, source, g, three, four, last, ready)
    part = lax.all_to_all(part, "z", 0, 0, tiled=True)
    part = pl.pallas_call(
        gather_z,
        out_shape=shape(f32, NQ * NF, 1, LONG),
        in_specs=[vmem],
        out_specs=vmem,
        name="gather_z",
        compiler_params=pltpu.CompilerParams(vmem_limit_bytes=8 << 20),
    )(part)
    part = lax.all_to_all(part, PLANE + FREQ, 0, 0, tiled=True)
    return pl.pallas_call(
        finish,
        out_shape=(shape(f32, 1, CELLS), shape(f32, 1)),
        in_specs=[vmem, vmem],
        out_specs=(vmem, pl.BlockSpec(memory_space=pltpu.SMEM)),
        name="finish",
        compiler_params=pltpu.CompilerParams(vmem_limit_bytes=8 << 20),
    )(part, source)


def solution(mesh):
    fine = Mesh(mesh.devices.reshape(NZ, NX, NY, 2, 2), STA + FREQ)
    placed = (P(FREQ, None, STA), P(FREQ, None, STA, None), P(FREQ, None), P(STA, None))
    return jax.shard_map(
        local, mesh=fine, in_specs=placed, out_specs=(P(FREQ, None), P(FREQ)), check_vma=False
    )
```

```python
import jax
import jax.numpy as jnp
from jax import lax
from jax.experimental import pallas as pl
from jax.experimental.pallas import tpu as pltpu
from jax.sharding import Mesh, PartitionSpec as P

NZ, NX, NY = 8, 2, 4
NQ = NX * NY
NF = 4
ROWS = 64
CELLS = 1024
WIDE = NQ * ROWS
PLANE = ("xl", "y")
FREQ = ("xh", "core")
STA = ("z",) + PLANE
OFFSETS = (1, 2, -3, 4)
SHARED = 152
LONG = CELLS + 128
f32, bf16 = jnp.float32, jnp.bfloat16


def nt(a, b):
    return lax.dot_general(
        a, b, (((1,), (1,)), ((), ())), preferred_element_type=f32
    )


def nn(a, b):
    return lax.dot_general(
        a, b, (((1,), (0,)), ((), ())), preferred_element_type=f32
    )


def identity(n):
    down = lax.broadcasted_iota(jnp.int32, (n, n), 0)
    across = lax.broadcasted_iota(jnp.int32, (n, n), 1)
    return (down == across).astype(f32).astype(bf16)


SPEC, IMAG, REAL, MASK, NEXT, FULL = 0, 8, 72, 136, 168, 200
PREPARE = 17_500_000_000


def window(mask, at):
    start = pl.multiple_of(lax.rem(at + NZ, NZ) * WIDE, WIDE)
    return mask[:, pl.ds(start, WIDE)].astype(f32)


def put_mask(ref, part):
    ref[:, 0:512] = part[0:32]
    ref[:, 512:1024] = part[32:64]


def take_mask(ref, at):
    return jnp.concatenate(
        [ref[at : at + 32, 0:512], ref[at : at + 32, 512:1024]], axis=0
    ).astype(f32)


def take_spectra(ref, at):
    return jnp.concatenate(
        [ref[at : at + 8, 128 * g : 128 * (g + 1)].astype(f32) for g in range(8)],
        axis=0,
    )


def put_spectra(ref, spectra):
    for g in range(8):
        ref[:, 128 * g : 128 * (g + 1)] = spectra[8 * g : 8 * (g + 1)]


def pack(green, mask, spec_row, near, far, shared, own_mask, own_spec):
    z = lax.axis_index("z")
    row = spec_row[...]
    col = nt(identity(ROWS), row)
    lane = lax.broadcasted_iota(jnp.int32, (ROWS, 128), 1)
    own_spec[...] = jnp.where(
        lane == 0, col[:, 0:1], jnp.where(lane == 1, col[:, 1:2], 0.0)
    )
    own_spec[0:2, 64:128] = row.astype(f32)
    spectra = own_spec[...].astype(bf16)
    for ref in (near, far):
        ref[IMAG : IMAG + ROWS, :] = green[1]
        ref[REAL : REAL + ROWS, :] = green[0]
        put_spectra(ref.at[SPEC : SPEC + 8], spectra)
    for u, ref, at in ((1, near, NEXT), (2, near, MASK), (-3, far, MASK)):
        put_mask(ref.at[at : at + 32], window(mask, z - u).astype(bf16))
    own_mask[...] = window(mask, z).astype(bf16)
    wide = [window(mask, z + u) for u in OFFSETS]
    for q in range(NQ):
        shared[q, 0:64, :] = green[0]
        shared[q, 64:128, :] = green[1]
        put_spectra(shared.at[q, 144:152], spectra)
        part = jnp.concatenate(
            [w[:, ROWS * q : ROWS * (q + 1)] for w in wide], axis=1
        ).astype(bf16)
        for g in range(4):
            shared[q, 128:144, 256 * g : 256 * (g + 1)] = part[16 * g : 16 * (g + 1)]


MOST = 3 * ROWS
NEAR_RE, NEAR_IM, COUNT = 0, 2 * ROWS, 4 * ROWS
SPECTRA = COUNT + MOST // 2
BUNDLE = SPECTRA + MOST // 8


def prepare(own_mask, own_spec, one, two, bundle):
    us = [own_spec[...]]
    for k, ref in enumerate((one, two)):
        us.append(take_spectra(ref, SPEC))
        at = ROWS * k
        bundle[NEAR_RE + at : NEAR_RE + at + ROWS, :] = ref[REAL : REAL + ROWS, :]
        bundle[NEAR_IM + at : NEAR_IM + at + ROWS, :] = ref[IMAG : IMAG + ROWS, :]
    masks = [own_mask[...].astype(f32), take_mask(one, NEXT), take_mask(two, MASK)]
    counts = jnp.concatenate(masks, axis=0).astype(bf16)
    for h in range(2):
        bundle[COUNT : COUNT + MOST // 2, WIDE * h : WIDE * (h + 1)] = counts[
            MOST // 2 * h : MOST // 2 * (h + 1)
        ]
    spectra = jnp.concatenate(us, axis=0)
    for h in range(8):
        bundle[SPECTRA : SPECTRA + MOST // 8, 128 * h : 128 * (h + 1)] = spectra[
            MOST // 8 * h : MOST // 8 * (h + 1)
        ].astype(bf16)


def absorb(shared, source, green, three, four, bundle, out, far_re, far_im, far_spec, back, wt):
    real, imag = slice(REAL, REAL + ROWS), slice(IMAG, IMAG + ROWS)
    tall = 5 * ROWS
    scale = source[...]
    held = [(green[0], green[1])]
    for k in range(2):
        re, im = NEAR_RE + ROWS * k, NEAR_IM + ROWS * k
        held.append((bundle[re : re + ROWS, :], bundle[im : im + ROWS, :]))
    for ref in (three, four):
        held.append((ref[real, :], ref[imag, :]))
    for k, (re, im) in enumerate(held):
        at = ROWS * k
        wt[at : at + ROWS, :] = (scale * re.astype(f32)).astype(bf16)
        wt[tall + at : tall + at + ROWS, :] = (scale * im.astype(f32)).astype(bf16)
    spec = jnp.concatenate(
        [
            bundle[SPECTRA : SPECTRA + MOST // 8, 128 * h : 128 * (h + 1)].astype(f32)
            for h in range(8)
        ]
        + [take_spectra(three, SPEC), take_spectra(four, SPEC)],
        axis=0,
    )
    u_re, u_im = spec[:, 0:1], spec[:, 1:2]
    weight = jnp.concatenate(
        [
            bundle[COUNT : COUNT + MOST // 2, WIDE * h : WIDE * (h + 1)].astype(f32)
            for h in range(2)
        ]
        + [take_mask(three, MASK)],
        axis=0,
    )
    for q in range(NQ):
        rows = slice(ROWS * q, ROWS * (q + 1))
        ref = shared.at[q]
        far_re[rows, :] = ref[0:64, :]
        far_im[rows, :] = ref[64:128, :]
        for g in range(4):
            back[ROWS * q + 16 * g : ROWS * q + 16 * (g + 1), :] = ref[
                128:144, 256 * g : 256 * (g + 1)
            ]
        far_spec[0:2, rows] = ref[144:152, 0:128].astype(f32)[0:2, 64:128]
    behind = nt(identity(4 * ROWS), back[...])
    counts = jnp.concatenate(
        [
            weight[0:ROWS],
            weight[ROWS : 4 * ROWS] + behind[0 : 3 * ROWS],
            behind[3 * ROWS : 4 * ROWS],
        ],
        axis=0,
    )
    v_re, v_im = far_spec[0:1, :], far_spec[1:2, :]
    g_re, g_im = far_re[...], far_im[...]
    by_re = nt(wt[...], g_re)
    by_im = nt(wt[...], g_im)
    x_re = (u_re * v_re + u_im * v_im) - (by_re[:tall] + by_im[tall:])
    x_im = (u_im * v_re - u_re * v_im) - (by_re[tall:] - by_im[:tall])
    mis = 0.5 * jnp.sum(counts * (x_re * x_re + x_im * x_im), keepdims=True)
    resid = jnp.concatenate(
        [
            (counts * x_re.astype(bf16).astype(f32)).astype(bf16),
            (counts * x_im.astype(bf16).astype(f32)).astype(bf16),
        ],
        axis=0,
    )
    by_re = nn(resid, g_re)
    by_im = nn(resid, g_im)
    total = jnp.zeros((ROWS, CELLS), f32)
    for k, (re, im) in enumerate(held):
        rows = slice(ROWS * k, ROWS * (k + 1))
        more = slice(tall + ROWS * k, tall + ROWS * (k + 1))
        total = total + (
            re.astype(f32) * (by_re[rows] - by_im[more])
            + im.astype(f32) * (by_im[rows] + by_re[more])
        )
    total = -jnp.sum(total, axis=0, keepdims=True)
    out[:, :, 0:CELLS] = jnp.broadcast_to(total[None], (NZ * NX, 1, CELLS))
    out[:, :, CELLS:LONG] = jnp.broadcast_to(mis[None], (NZ * NX, 1, 128))


def gather_zx(parts, out):
    out[...] = jnp.broadcast_to(
        jnp.sum(parts[...], axis=0, keepdims=True), out.shape
    )


def finish(parts, source, new_source, misfit):
    mine = lax.axis_index("xh") * 2 + lax.axis_index("core")
    squares = jnp.zeros((1, CELLS), f32)
    own = jnp.zeros((1, LONG), f32)
    for f in range(NF):
        here = parts[f]
        for y in range(1, NY):
            here = here + parts[y * NF + f]
        squares = squares + here[:, 0:CELLS] * here[:, 0:CELLS]
        own = jnp.where(mine == f, here, own)
    rms = jnp.sqrt(jnp.sum(squares, keepdims=True) / (NF * CELLS) + 1e-06)
    new_source[...] = source[...] * jnp.exp(-0.5 * own[:, 0:CELLS] / rms)
    stations = NZ * NQ * ROWS
    misfit[0] = jnp.max(own[:, CELLS:LONG]) / (stations * stations)


def shape(dtype, *dims):
    return jax.ShapeDtypeStruct(dims, dtype)


def from_z(array, u):
    return lax.ppermute(array, "z", [(z, (z - u) % NZ) for z in range(NZ)])


def local(spectra, green, source, pair_mask):
    g = green[0]
    vmem = pl.BlockSpec(memory_space=pltpu.VMEM)
    near, far, shared, own_mask, own_spec = pl.pallas_call(
        pack,
        out_shape=[
            shape(bf16, FULL, CELLS),
            shape(bf16, NEXT, CELLS),
            shape(bf16, NQ, SHARED, CELLS),
            shape(bf16, ROWS, WIDE),
            shape(f32, ROWS, 128),
        ],
        in_specs=[vmem] * 3,
        out_specs=[vmem] * 5,
        name="pack",
    )(g, pair_mask, spectra[0])
    three = from_z(from_z(far, -1), -2)
    one = from_z(near, 1)
    shared = lax.all_to_all(shared, PLANE, 0, 0, tiled=True)
    two = from_z(one[:NEXT], 1)
    four = from_z(two[:MASK], 2)
    ready = pl.pallas_call(
        prepare,
        out_shape=shape(bf16, BUNDLE, CELLS),
        in_specs=[vmem] * 4,
        out_specs=vmem,
        cost_estimate=pl.CostEstimate(
            flops=PREPARE, transcendentals=0, bytes_accessed=0
        ),
        name="prepare",
    )(own_mask, own_spec, one, two)
    part = pl.pallas_call(
        absorb,
        out_shape=shape(f32, NZ * NX, 1, LONG),
        in_specs=[vmem] * 6,
        out_specs=vmem,
        scratch_shapes=[
            pltpu.VMEM((WIDE, CELLS), bf16),
            pltpu.VMEM((WIDE, CELLS), bf16),
            pltpu.VMEM((8, WIDE), f32),
            pltpu.VMEM((WIDE, 4 * ROWS), bf16),
            pltpu.VMEM((10 * ROWS, CELLS), bf16),
        ],
        name="absorb",
        compiler_params=pltpu.CompilerParams(vmem_limit_bytes=40 << 20),
    )(shared, source, g, three, four, ready)
    part = lax.all_to_all(part, ("z", "xl"), 0, 0, tiled=True)
    part = pl.pallas_call(
        gather_zx,
        out_shape=shape(f32, NY * NF, 1, LONG),
        in_specs=[vmem],
        out_specs=vmem,
        name="gather_zx",
        compiler_params=pltpu.CompilerParams(vmem_limit_bytes=8 << 20),
    )(part)
    part = lax.all_to_all(part, ("y",) + FREQ, 0, 0, tiled=True)
    return pl.pallas_call(
        finish,
        out_shape=(shape(f32, 1, CELLS), shape(f32, 1)),
        in_specs=[vmem, vmem],
        out_specs=(vmem, pl.BlockSpec(memory_space=pltpu.SMEM)),
        name="finish",
        compiler_params=pltpu.CompilerParams(vmem_limit_bytes=8 << 20),
    )(part, source)


def solution(mesh):
    fine = Mesh(mesh.devices.reshape(NZ, NX, NY, 2, 2), STA + FREQ)
    placed = (P(FREQ, None, STA), P(FREQ, None, STA, None), P(FREQ, None), P(STA, None))
    return jax.shard_map(
        local, mesh=fine, in_specs=placed, out_specs=(P(FREQ, None), P(FREQ)), check_vma=False
    )
```

```python
import jax
import jax.numpy as jnp
from jax import lax
from jax.experimental import pallas as pl
from jax.experimental.pallas import tpu as pltpu
from jax.sharding import Mesh, PartitionSpec as P

NZ, NX, NY = 8, 2, 4
NQ = NX * NY
NF = 4
ROWS = 64
CELLS = 1024
WIDE = NQ * ROWS
PLANE = ("xl", "y")
FREQ = ("xh", "core")
STA = ("z",) + PLANE
OFFSETS = (1, 2, -3, 4)
SHARED = 152
LONG = CELLS + 128
f32, bf16 = jnp.float32, jnp.bfloat16


def nt(a, b):
    return lax.dot_general(
        a, b, (((1,), (1,)), ((), ())), preferred_element_type=f32
    )


def nn(a, b):
    return lax.dot_general(
        a, b, (((1,), (0,)), ((), ())), preferred_element_type=f32
    )


def identity(n):
    down = lax.broadcasted_iota(jnp.int32, (n, n), 0)
    across = lax.broadcasted_iota(jnp.int32, (n, n), 1)
    return (down == across).astype(f32).astype(bf16)


SPEC, IMAG, REAL, MASK, NEXT, FULL = 0, 8, 72, 136, 168, 200
PREPARE = 10_000_000_000


def window(mask, at):
    start = pl.multiple_of(lax.rem(at + NZ, NZ) * WIDE, WIDE)
    return mask[:, pl.ds(start, WIDE)].astype(f32)


def put_mask(ref, part):
    ref[:, 0:512] = part[0:32]
    ref[:, 512:1024] = part[32:64]


def take_mask(ref, at):
    return jnp.concatenate(
        [ref[at : at + 32, 0:512], ref[at : at + 32, 512:1024]], axis=0
    ).astype(f32)


def take_spectra(ref, at):
    return jnp.concatenate(
        [ref[at : at + 8, 128 * g : 128 * (g + 1)].astype(f32) for g in range(8)],
        axis=0,
    )


def put_spectra(ref, spectra):
    for g in range(8):
        ref[:, 128 * g : 128 * (g + 1)] = spectra[8 * g : 8 * (g + 1)]


def pack(green, mask, spec_row, near, far, shared, own_mask, own_spec):
    z = lax.axis_index("z")
    row = spec_row[...]
    col = nt(identity(ROWS), row)
    lane = lax.broadcasted_iota(jnp.int32, (ROWS, 128), 1)
    own_spec[...] = jnp.where(
        lane == 0, col[:, 0:1], jnp.where(lane == 1, col[:, 1:2], 0.0)
    )
    own_spec[0:2, 64:128] = row.astype(f32)
    spectra = own_spec[...].astype(bf16)
    for ref in (near, far):
        ref[IMAG : IMAG + ROWS, :] = green[1]
        ref[REAL : REAL + ROWS, :] = green[0]
        put_spectra(ref.at[SPEC : SPEC + 8], spectra)
    for u, ref, at in ((1, near, NEXT), (2, near, MASK), (-3, far, MASK)):
        put_mask(ref.at[at : at + 32], window(mask, z - u).astype(bf16))
    own_mask[...] = window(mask, z).astype(bf16)
    wide = [window(mask, z + u) for u in OFFSETS]
    for q in range(NQ):
        shared[q, 0:64, :] = green[0]
        shared[q, 64:128, :] = green[1]
        put_spectra(shared.at[q, 144:152], spectra)
        part = jnp.concatenate(
            [w[:, ROWS * q : ROWS * (q + 1)] for w in wide], axis=1
        ).astype(bf16)
        for g in range(4):
            shared[q, 128:144, 256 * g : 256 * (g + 1)] = part[16 * g : 16 * (g + 1)]


MOST = 3 * ROWS
NEAR_RE, NEAR_IM, COUNT = 0, 2 * ROWS, 4 * ROWS
SPECTRA = COUNT + MOST // 2
BUNDLE = SPECTRA + MOST // 8


def prepare(own_mask, own_spec, one, two, bundle):
    us = [own_spec[...]]
    for k, ref in enumerate((one, two)):
        us.append(take_spectra(ref, SPEC))
        at = ROWS * k
        bundle[NEAR_RE + at : NEAR_RE + at + ROWS, :] = ref[REAL : REAL + ROWS, :]
        bundle[NEAR_IM + at : NEAR_IM + at + ROWS, :] = ref[IMAG : IMAG + ROWS, :]
    masks = [own_mask[...].astype(f32), take_mask(one, NEXT), take_mask(two, MASK)]
    counts = jnp.concatenate(masks, axis=0).astype(bf16)
    for h in range(2):
        bundle[COUNT : COUNT + MOST // 2, WIDE * h : WIDE * (h + 1)] = counts[
            MOST // 2 * h : MOST // 2 * (h + 1)
        ]
    spectra = jnp.concatenate(us, axis=0)
    for h in range(8):
        bundle[SPECTRA : SPECTRA + MOST // 8, 128 * h : 128 * (h + 1)] = spectra[
            MOST // 8 * h : MOST // 8 * (h + 1)
        ].astype(bf16)


def absorb(shared, source, green, three, four, bundle, out, far_re, far_im, far_spec, back, wt):
    real, imag = slice(REAL, REAL + ROWS), slice(IMAG, IMAG + ROWS)
    tall = 5 * ROWS
    scale = source[...]
    held = [(green[0], green[1])]
    for k in range(2):
        re, im = NEAR_RE + ROWS * k, NEAR_IM + ROWS * k
        held.append((bundle[re : re + ROWS, :], bundle[im : im + ROWS, :]))
    for ref in (three, four):
        held.append((ref[real, :], ref[imag, :]))
    for k, (re, im) in enumerate(held):
        at = ROWS * k
        wt[at : at + ROWS, :] = (scale * re.astype(f32)).astype(bf16)
        wt[tall + at : tall + at + ROWS, :] = (scale * im.astype(f32)).astype(bf16)
    spec = jnp.concatenate(
        [
            bundle[SPECTRA : SPECTRA + MOST // 8, 128 * h : 128 * (h + 1)].astype(f32)
            for h in range(8)
        ]
        + [take_spectra(three, SPEC), take_spectra(four, SPEC)],
        axis=0,
    )
    u_re, u_im = spec[:, 0:1], spec[:, 1:2]
    weight = jnp.concatenate(
        [
            bundle[COUNT : COUNT + MOST // 2, WIDE * h : WIDE * (h + 1)].astype(f32)
            for h in range(2)
        ]
        + [take_mask(three, MASK)],
        axis=0,
    )
    for q in range(NQ):
        rows = slice(ROWS * q, ROWS * (q + 1))
        ref = shared.at[q]
        far_re[rows, :] = ref[0:64, :]
        far_im[rows, :] = ref[64:128, :]
        for g in range(4):
            back[ROWS * q + 16 * g : ROWS * q + 16 * (g + 1), :] = ref[
                128:144, 256 * g : 256 * (g + 1)
            ]
        far_spec[0:2, rows] = ref[144:152, 0:128].astype(f32)[0:2, 64:128]
    behind = nt(identity(4 * ROWS), back[...])
    counts = jnp.concatenate(
        [
            weight[0:ROWS],
            weight[ROWS : 4 * ROWS] + behind[0 : 3 * ROWS],
            behind[3 * ROWS : 4 * ROWS],
        ],
        axis=0,
    )
    v_re, v_im = far_spec[0:1, :], far_spec[1:2, :]
    g_re, g_im = far_re[...], far_im[...]
    by_re = nt(wt[...], g_re)
    by_im = nt(wt[...], g_im)
    x_re = (u_re * v_re + u_im * v_im) - (by_re[:tall] + by_im[tall:])
    x_im = (u_im * v_re - u_re * v_im) - (by_re[tall:] - by_im[:tall])
    mis = 0.5 * jnp.sum(counts * (x_re * x_re + x_im * x_im), keepdims=True)
    resid = jnp.concatenate(
        [
            (counts * x_re.astype(bf16).astype(f32)).astype(bf16),
            (counts * x_im.astype(bf16).astype(f32)).astype(bf16),
        ],
        axis=0,
    )
    by_re = nn(resid, g_re)
    by_im = nn(resid, g_im)
    total = jnp.zeros((ROWS, CELLS), f32)
    for k, (re, im) in enumerate(held):
        rows = slice(ROWS * k, ROWS * (k + 1))
        more = slice(tall + ROWS * k, tall + ROWS * (k + 1))
        total = total + (
            re.astype(f32) * (by_re[rows] - by_im[more])
            + im.astype(f32) * (by_im[rows] + by_re[more])
        )
    total = -jnp.sum(total, axis=0, keepdims=True)
    out[:, :, 0:CELLS] = jnp.broadcast_to(total[None], (NZ, 1, CELLS))
    out[:, :, CELLS:LONG] = jnp.broadcast_to(mis[None], (NZ, 1, 128))


def gather_z(parts, out):
    out[...] = jnp.broadcast_to(
        jnp.sum(parts[...], axis=0, keepdims=True), out.shape
    )


def finish(parts, source, new_source, misfit):
    mine = lax.axis_index("xh") * 2 + lax.axis_index("core")
    squares = jnp.zeros((1, CELLS), f32)
    own = jnp.zeros((1, LONG), f32)
    for f in range(NF):
        here = parts[f]
        for q in range(1, NQ):
            here = here + parts[q * NF + f]
        squares = squares + here[:, 0:CELLS] * here[:, 0:CELLS]
        own = jnp.where(mine == f, here, own)
    rms = jnp.sqrt(jnp.sum(squares, keepdims=True) / (NF * CELLS) + 1e-06)
    new_source[...] = source[...] * jnp.exp(-0.5 * own[:, 0:CELLS] / rms)
    stations = NZ * NQ * ROWS
    misfit[0] = jnp.max(own[:, CELLS:LONG]) / (stations * stations)


def shape(dtype, *dims):
    return jax.ShapeDtypeStruct(dims, dtype)


def from_z(array, u):
    return lax.ppermute(array, "z", [(z, (z - u) % NZ) for z in range(NZ)])


def local(spectra, green, source, pair_mask):
    g = green[0]
    vmem = pl.BlockSpec(memory_space=pltpu.VMEM)
    near, far, shared, own_mask, own_spec = pl.pallas_call(
        pack,
        out_shape=[
            shape(bf16, FULL, CELLS),
            shape(bf16, NEXT, CELLS),
            shape(bf16, NQ, SHARED, CELLS),
            shape(bf16, ROWS, WIDE),
            shape(f32, ROWS, 128),
        ],
        in_specs=[vmem] * 3,
        out_specs=[vmem] * 5,
        name="pack",
    )(g, pair_mask, spectra[0])
    three = from_z(from_z(far, -1), -2)
    one = from_z(near, 1)
    shared = lax.all_to_all(shared, PLANE, 0, 0, tiled=True)
    two = from_z(one[:NEXT], 1)
    four = from_z(two[:MASK], 2)
    ready = pl.pallas_call(
        prepare,
        out_shape=shape(bf16, BUNDLE, CELLS),
        in_specs=[vmem] * 4,
        out_specs=vmem,
        cost_estimate=pl.CostEstimate(
            flops=PREPARE, transcendentals=0, bytes_accessed=0
        ),
        name="prepare",
    )(own_mask, own_spec, one, two)
    part = pl.pallas_call(
        absorb,
        out_shape=shape(f32, NZ, 1, LONG),
        in_specs=[vmem] * 6,
        out_specs=vmem,
        scratch_shapes=[
            pltpu.VMEM((WIDE, CELLS), bf16),
            pltpu.VMEM((WIDE, CELLS), bf16),
            pltpu.VMEM((8, WIDE), f32),
            pltpu.VMEM((WIDE, 4 * ROWS), bf16),
            pltpu.VMEM((10 * ROWS, CELLS), bf16),
        ],
        name="absorb",
        compiler_params=pltpu.CompilerParams(vmem_limit_bytes=40 << 20),
    )(shared, source, g, three, four, ready)
    part = lax.all_to_all(part, "z", 0, 0, tiled=True)
    part = pl.pallas_call(
        gather_z,
        out_shape=shape(f32, NQ * NF, 1, LONG),
        in_specs=[vmem],
        out_specs=vmem,
        name="gather_z",
        compiler_params=pltpu.CompilerParams(vmem_limit_bytes=8 << 20),
    )(part)
    part = lax.all_to_all(part, PLANE + FREQ, 0, 0, tiled=True)
    return pl.pallas_call(
        finish,
        out_shape=(shape(f32, 1, CELLS), shape(f32, 1)),
        in_specs=[vmem, vmem],
        out_specs=(vmem, pl.BlockSpec(memory_space=pltpu.SMEM)),
        name="finish",
        compiler_params=pltpu.CompilerParams(vmem_limit_bytes=8 << 20),
    )(part, source)


def solution(mesh):
    fine = Mesh(mesh.devices.reshape(NZ, NX, NY, 2, 2), STA + FREQ)
    placed = (P(FREQ, None, STA), P(FREQ, None, STA, None), P(FREQ, None), P(STA, None))
    return jax.shard_map(
        local, mesh=fine, in_specs=placed, out_specs=(P(FREQ, None), P(FREQ)), check_vma=False
    )
```
